128 devices in a mesh: slab: 16 (over z, y), energy: 8 (over x, core).
Axes of the slice: x: 4, y: 4, z: 4, core: 2. Of those that a mesh axis runs over, the one named last changes fastest.
Arguments:
- source: float32 [32, 2, 16, 192, 128], P('slab', None, 'energy'), may hold values from -1.2 to 1.2
- onsite_block: float32 [192, 192], replicated, may hold values from -1.3 to 1.3, as said below
- hopping_block: float32 [192, 192], replicated, may hold values from -0.5 to 1.5
- potential_table: float32 [16, 192], replicated, may hold values from -0.5 to 0.5
- slab_profile: int32 [32], P('slab'), may hold values from 0 to 15
- occupation: float32 [32, 16, 192], P('slab', 'energy'), may hold values from 0.1 to 1
- coupling: float32 [4], replicated, may hold values from 0.02 to 0.08
- phonon_shift: int32 [4], replicated, may hold values from 1 to 2, as said below
Outputs:
- amplitude: float32 [32, 2, 16, 192, 128], P('slab', None, 'energy')
- density: float32 [32, 16, 192], P('slab', 'energy')
The draws below stay inside these ranges and needn't reach their ends.
Inputs may be any that keep to these rules, and one draw needn't show every extreme that they name: `phonon_shift`: some mode shifts by exactly 2 points and some by exactly 1. `onsite_block`: symmetric.
All inputs are finite; a program needn't handle non-finite values.
Results may differ from the reference program's by a relative error of at most 0.0003.
Values sent between devices are 32-bit elements; how exact they have to be, the bound alone decides.
No kernel may reach another device: no remote copies, remote signals or barrier semaphores. Data moves between devices by JAX's collectives and lax.ppermute only.
A program may use at most 128 MiB of HBM per device.

```python
import math
import jax
import jax.numpy as jnp
from jax import lax

ORBITALS = 192
COLUMNS = 128
ENERGY_DEV = 2
LEVELS = 16
PHONON_MODES = 4
SLABS = 32
ENERGIES = 16


def draw_onsite_block(key, part):
    key = jax.random.fold_in(key, 101)
    key_diag, key_off = jax.random.split(key)
    spread = 0.3 / jnp.sqrt(ORBITALS * 1.0)
    diagonal = jax.random.uniform(key_diag, (ORBITALS,), jnp.float32, -0.8, 0.8)
    rough = jnp.clip(jax.random.normal(key_off, (ORBITALS, ORBITALS), jnp.float32), -4.0, 4.0)
    return 0.5 * spread * (rough + rough.T) + jnp.diag(diagonal)


def draw_hopping_block(key, part):
    key = jax.random.fold_in(key, 202)
    key_diag, key_off = jax.random.split(key)
    spread = 0.3 / jnp.sqrt(ORBITALS * 1.0)
    diagonal = jax.random.uniform(key_diag, (ORBITALS,), jnp.float32, 0.8, 1.2)
    rough = jnp.clip(jax.random.normal(key_off, (ORBITALS, ORBITALS), jnp.float32), -4.0, 4.0)
    return spread * rough + jnp.diag(diagonal)


def draw_phonon_shift(key, part):
    key = jax.random.fold_in(key, 303)
    key_values, key_order = jax.random.split(key)
    values = jax.random.randint(key_values, (PHONON_MODES,), 1, ENERGY_DEV + 1, dtype=jnp.int32)
    order = jax.random.permutation(key_order, PHONON_MODES)
    values = values.at[order[0]].set(ENERGY_DEV)
    return values.at[order[1]].set(1)


def place_ends(array, key, least, top_value):
    index_at = [jax.random.randint(jax.random.fold_in(key, axis), (), 0, length) for axis, length in enumerate(array.shape)]
    main_axis = array.shape.index(max(array.shape))
    beside = index_at[:main_axis] + [(index_at[main_axis] + 1) % array.shape[main_axis]] + index_at[main_axis + 1:]
    return array.at[tuple(index_at)].set(least).at[tuple(beside)].set(top_value)


def block_levels(stream_key, shape, shards, least, top_value):
    loudness = 1.0
    for axis_at, shards_of in shards:
        heights = jax.random.uniform(jax.random.fold_in(jax.random.fold_in(stream_key, 6), axis_at), (shards_of,), jnp.float32, least / len(shards), top_value / len(shards))
        loudness = loudness * jnp.repeat(jnp.exp(heights), shape[axis_at] // shards_of).reshape((-1,) + (1,) * (len(shape) - 1 - axis_at))
    return loudness


def scatter_about(own_key, shape, scale, bound, cuts=(), kind=jnp.bfloat16):
    factor_of = block_levels(own_key, shape, cuts, -0.22, 0.18) if cuts else 1.0
    entries = jax.random.normal(own_key, shape, jnp.float32) * scale * factor_of
    return jnp.minimum(jnp.maximum(entries, -bound), bound).astype(kind)


def setup_inputs(seed: int = 0) -> dict:
    seeds = jax.random.split(jax.random.key(seed), 9)
    source = scatter_about(seeds[0], (SLABS, 2, ENERGIES, ORBITALS, COLUMNS), 0.2, 1.2, ((0, 16), (2, 8)), jnp.float32)
    onsite_block = draw_onsite_block(jax.random.fold_in(seeds[8], 71), 0)
    hopping_block = draw_hopping_block(jax.random.fold_in(seeds[8], 71), 0)
    potential_table = jnp.clip(jax.random.uniform(seeds[3], (LEVELS, ORBITALS), jnp.float32, -0.5, 0.5), -0.5, 0.5)
    slab_profile = place_ends(jax.random.randint(seeds[4], (SLABS,), 0, LEVELS), jax.random.fold_in(seeds[4], 1), 0, LEVELS - 1).astype(jnp.int32)
    occupation = jnp.clip(jnp.exp(math.log(1.0) - 2.3025851 * jax.random.uniform(seeds[5], (SLABS, ENERGIES, ORBITALS), jnp.float32) ** block_levels(seeds[5], (SLABS, ENERGIES, ORBITALS), ((0, 16), (1, 8)), -0.2, 0.2)), 0.1, 1.0)
    coupling = jnp.clip(jnp.exp(jax.random.uniform(seeds[6], (PHONON_MODES,), jnp.float32, math.log(0.02), math.log(0.08))), 0.02, 0.08)
    phonon_shift = draw_phonon_shift(jax.random.fold_in(seeds[8], 71), 0)
    return {"source": source, "onsite_block": onsite_block, "hopping_block": hopping_block, "potential_table": potential_table, "slab_profile": slab_profile, "occupation": occupation, "coupling": coupling, "phonon_shift": phonon_shift}


broadening = 0.05
energy_low = -1.2
energy_step = 0.15

def matmul_exact(left, right):
    return jnp.matmul(left, right, precision=lax.Precision.HIGHEST)

def complex_product(left, right):
    real = matmul_exact(left[..., 0, :, :], right[..., 0, :, :]) - matmul_exact(left[..., 1, :, :], right[..., 1, :, :])
    imag = matmul_exact(left[..., 0, :, :], right[..., 1, :, :]) + matmul_exact(left[..., 1, :, :], right[..., 0, :, :])
    return jnp.stack([real, imag], axis=-3)

def invert(block):
    real = block[..., 0, :, :]
    imag = block[..., 1, :, :]
    real = 0.5 * (real + jnp.swapaxes(real, -1, -2))
    imag = 0.5 * (imag + jnp.swapaxes(imag, -1, -2))
    lower_imag = jnp.linalg.cholesky(imag)
    weighed = jax.scipy.linalg.cho_solve((lower_imag, True), real)
    schur = imag + matmul_exact(real, weighed)
    schur = 0.5 * (schur + jnp.swapaxes(schur, -1, -2))
    lower_schur = jnp.linalg.cholesky(schur)
    identity = jnp.broadcast_to(jnp.eye(schur.shape[-1], dtype=schur.dtype), schur.shape)
    schur_inverse = jax.scipy.linalg.cho_solve((lower_schur, True), identity)
    return jnp.stack([matmul_exact(weighed, schur_inverse), -schur_inverse], axis=-3)

def reference(source, onsite_block, hopping_block, potential_table, slab_profile, occupation, coupling, phonon_shift):
    energy_total = occupation.shape[1]
    points = jnp.arange(energy_total, dtype=jnp.int32)
    weights = jnp.zeros((energy_total, energy_total), jnp.float32)
    for mode in range(PHONON_MODES):
        above = (points[None, :] == points[:, None] + phonon_shift[mode]).astype(jnp.float32)
        below = (points[None, :] == points[:, None] - phonon_shift[mode]).astype(jnp.float32)
        weights = weights + coupling[mode] * (above + below)
    damping = jnp.einsum('ek,skb->seb', weights, occupation, precision=lax.Precision.HIGHEST)
    chosen = (slab_profile[:, None] == jnp.arange(LEVELS, dtype=jnp.int32)[None, :]).astype(jnp.float32)
    potential = matmul_exact(chosen, potential_table)
    grid = energy_low + energy_step * points.astype(jnp.float32)
    identity = jnp.eye(ORBITALS, dtype=jnp.float32)
    hop_t = hopping_block.T

    def solve_energy(point):
        real_diag = grid[point] * identity - onsite_block - potential[:, :, None] * identity
        imag_diag = (broadening + damping[:, point])[:, :, None] * identity
        blocks = jnp.stack([real_diag, imag_diag], axis=1)
        right = source[:, :, point]

        def forward(carry, inputs):
            inverse, solved = carry
            block, rhs = inputs
            pivot = block - matmul_exact(hop_t, matmul_exact(inverse, hopping_block))
            rhs = rhs + matmul_exact(hop_t, solved)
            inverse = invert(pivot)
            solved = complex_product(inverse, rhs)
            return ((inverse, solved), (inverse, solved))
        start = (jnp.zeros((2, ORBITALS, ORBITALS), jnp.float32), jnp.zeros((2, ORBITALS, COLUMNS), jnp.float32))
        _, (inverses, solveds) = lax.scan(forward, start, (blocks, right))

        def backward(later, inputs):
            inverse, solved = inputs
            current = solved + complex_product(inverse, matmul_exact(hopping_block, later))
            return (current, current)
        _, result = lax.scan(backward, jnp.zeros((2, ORBITALS, COLUMNS), jnp.float32), (inverses, solveds), reverse=True)
        return result
    stacked = lax.map(solve_energy, points)
    amplitude = jnp.moveaxis(stacked, 0, 2)
    density = jnp.sum(amplitude[:, 0] ** 2 + amplitude[:, 1] ** 2, axis=-1)
    return (amplitude, density)
```

```python
import functools

import jax
import jax.numpy as jnp
from jax import lax
from jax.experimental import pallas as pl
from jax.experimental.pallas import tpu as pltpu
from jax.sharding import PartitionSpec as P

broadening = 0.05
energy_low = -1.2
energy_step = 0.15


N=192
def split(x):
    hi=x.astype(jnp.bfloat16); lo=(x-hi.astype(jnp.float32)).astype(jnp.bfloat16)
    return hi,lo
def tn(a,b):
    return lax.dot_general(a,b,(((0,),(0,)),((),())),preferred_element_type=jnp.float32)
def small_inverse8(mr,mi,b):
    lane=lax.broadcasted_iota(jnp.int32,(b,128),1)
    row8=lax.broadcasted_iota(jnp.int32,(8,128),0)
    seg=(lane//b)*b
    off8=(lane-seg)[0:8]
    bc=lambda v: jnp.broadcast_to(v,(8,128))
    for g in range(b//8):
        o=8*g
        Cr=[jnp.take_along_axis(mr,seg+(o+j),axis=1) for j in range(8)]
        Ci=[jnp.take_along_axis(mi,seg+(o+j),axis=1) for j in range(8)]
        cr=[x[o:o+8] for x in Cr]; ci=[x[o:o+8] for x in Ci]
        for p in range(8):
            dr=bc(cr[p][p:p+1]); di=bc(ci[p][p:p+1])
            inv=1.0/(dr*dr+di*di)
            er=dr*inv; ei=-di*inv
            isrow=row8==p
            pr,pi=cr[p],ci[p]
            for j in range(8):
                if j==p: continue
                fr=bc(cr[j][p:p+1]); fi=bc(ci[j][p:p+1])
                tr=fr*er-fi*ei; ti=fr*ei+fi*er
                cr[j]=jnp.where(isrow,tr,cr[j]-(pr*tr-pi*ti))
                ci[j]=jnp.where(isrow,ti,ci[j]-(pr*ti+pi*tr))
            cr[p]=jnp.where(isrow,er,pi*ei-pr*er)
            ci[p]=jnp.where(isrow,ei,-(pr*ei+pi*er))
        ing=(off8>=o)&(off8<o+8)
        G_r=jnp.where(ing,jnp.where(off8-o==row8,1.0,0.0),mr[o:o+8]); G_i=jnp.where(ing,0.0,mi[o:o+8])
        Rr=None
        for j in range(8):
            gr=bc(G_r[j:j+1]); gi=bc(G_i[j:j+1])
            a=cr[j]*gr-ci[j]*gi; c=cr[j]*gi+ci[j]*gr
            Rr,Ri=(a,c) if Rr is None else (Rr+a,Ri+c)
        out_r=[];out_i=[]
        for h in range(b//8):
            if h==g: out_r.append(Rr);out_i.append(Ri);continue
            xr=jnp.where(ing,0.0,mr[8*h:8*h+8]); xi=jnp.where(ing,0.0,mi[8*h:8*h+8])
            for j in range(8):
                rr=bc(Rr[j:j+1]); ri=bc(Ri[j:j+1])
                ar_=Cr[j][8*h:8*h+8]; ai_=Ci[j][8*h:8*h+8]
                xr=xr-(ar_*rr-ai_*ri); xi=xi-(ar_*ri+ai_*rr)
            out_r.append(xr);out_i.append(xi)
        mr=jnp.concatenate(out_r,0); mi=jnp.concatenate(out_i,0)
    return mr,mi
def inverse_body(B,b,pr,pi,xr,xi,ar,ai):
    W=256
    for e in range(B):
        ar[e,:,0:N]=pr[e]; ai[e,:,0:N]=pi[e]
        ar[e,:,N:]=jnp.zeros((N,W-N),jnp.float32); ai[e,:,N:]=jnp.zeros((N,W-N),jnp.float32)
    lane=lax.broadcasted_iota(jnp.int32,(b,W),1)
    row=lax.broadcasted_iota(jnp.int32,(b,W),0)
    def step(k,_):
        o=pl.multiple_of(k*b,b)
        rows=[(ar[e,pl.ds(o,b),:],ai[e,pl.ds(o,b),:]) for e in range(B)]
        mr=jnp.zeros((b,128),jnp.float32); mi=mr
        l128=lax.broadcasted_iota(jnp.int32,(b,128),1)
        for e in range(B):
            sh=lax.rem(W-o+e*b,W)
            qr=pltpu.roll(rows[e][0],sh,1)[:,0:128]; qi=pltpu.roll(rows[e][1],sh,1)[:,0:128]
            s=(l128>=e*b)&(l128<(e+1)*b)
            mr=jnp.where(s,qr,mr); mi=jnp.where(s,qi,mi)
        if B*b<128:
            l=l128-b*(l128//b)
            r_=lax.broadcasted_iota(jnp.int32,(b,128),0)
            mr=jnp.where((l128>=B*b)&(l==r_),1.0,mr)
        mr,mi=small_inverse8(mr,mi,b)
        for e in range(B):
            rr,ri=rows[e]
            dr=mr[:,e*b:(e+1)*b]; di=mi[:,e*b:(e+1)*b]
            inblk=(lane>=o)&(lane<o+b)
            eye=lane-o==row
            r2=jnp.where(inblk,jnp.where(eye,-1.0,0.0),rr); i2=jnp.where(inblk,0.0,ri)
            drh,drl=split(dr); dih,dil=split(di)
            r2h,r2l=split(r2); i2h,i2l=split(i2)
            lhs=jnp.concatenate([drh,dih,drl,dil,drh,dih],0)
            Rr=tn(lhs,jnp.concatenate([r2h,-i2h,r2h,-i2h,r2l,-i2l],0))
            Ri=tn(lhs,jnp.concatenate([i2h,r2h,i2h,r2h,i2l,r2l],0))
            Rrh,Rrl=split(Rr); Rih,Ril=split(Ri)
            rh,rl=split(rr); ih,il=split(ri)
            lhs=jnp.concatenate([rh,ih,rl,il,rh,ih],0)[:,0:N]
            Ur=tn(lhs,jnp.concatenate([Rrh,-Rih,Rrh,-Rih,Rrl,-Ril],0))
            Ui=tn(lhs,jnp.concatenate([Rih,Rrh,Rih,Rrh,Ril,Rrl],0))
            lN=lax.broadcasted_iota(jnp.int32,(N,W),1)
            m=(lN>=o)&(lN<o+b)
            ar[e]=jnp.where(m,0.0,ar[e])-Ur
            ai[e]=jnp.where(m,0.0,ai[e])-Ui
            ar[e,pl.ds(o,b),:]=Rr; ai[e,pl.ds(o,b),:]=Ri
        return 0
    lax.fori_loop(0,N//b,step,0)
    for e in range(B):
        xr[e]=-ar[e,:,0:N]; xi[e]=-ai[e,:,0:N]
def inverse(pr,pi,b=64):
    B=pr.shape[0]
    f=jax.ShapeDtypeStruct((B,N,N),jnp.float32)
    return pl.pallas_call(functools.partial(inverse_body,B,b),out_shape=(f,f),
      in_specs=[pl.BlockSpec(memory_space=pltpu.VMEM)]*2,out_specs=[pl.BlockSpec(memory_space=pltpu.VMEM)]*2,
      scratch_shapes=[pltpu.VMEM((B,N,256),jnp.float32)]*2,name="block_inverse")(pr,pi)


def padded(block, sides, width):
    for axis, dim in sides:
        count = lax.axis_size(axis)
        forward = [(i, i + 1) for i in range(count - 1)]
        backward = [(target, source) for source, target in forward]
        low = lax.ppermute(
            lax.slice_in_dim(block, block.shape[dim] - width, None, axis=dim), axis, forward
        )
        high = lax.ppermute(lax.slice_in_dim(block, 0, width, axis=dim), axis, backward)
        block = jnp.concatenate([low, block, high], axis=dim)
    return block


def shifted(array, axis, by):
    count = lax.axis_size(axis)
    pairs = [(i, i + by) for i in range(count) if 0 <= i + by < count]
    return lax.ppermute(array, axis, pairs)


def matmul_exact(left, right):
    return jnp.matmul(left, right, precision=lax.Precision.HIGHEST)


def complex_product(left, right):
    real = matmul_exact(left[..., 0, :, :, :], right[..., 0, :, :, :]) - matmul_exact(
        left[..., 1, :, :, :], right[..., 1, :, :, :]
    )
    imag = matmul_exact(left[..., 0, :, :, :], right[..., 1, :, :, :]) + matmul_exact(
        left[..., 1, :, :, :], right[..., 0, :, :, :]
    )
    return jnp.stack([real, imag], axis=-4)


def invert(block):
    real = block[..., 0, :, :, :]
    imag = block[..., 1, :, :, :]
    real = 0.5 * (real + jnp.swapaxes(real, -1, -2))
    imag = 0.5 * (imag + jnp.swapaxes(imag, -1, -2))
    return jnp.stack(inverse(real, imag), axis=-4)


def per_device(
    source,
    onsite_block,
    hopping_block,
    potential_table,
    slab_profile,
    occupation,
    coupling,
    phonon_shift,
):
    slab_count = occupation.shape[0]
    energy_count = occupation.shape[1]
    orbitals = onsite_block.shape[0]
    hop_t = hopping_block.T
    widened = padded(occupation, (("energy", 1),), energy_count)
    own_points = jnp.arange(energy_count, dtype=jnp.int32)[:, None]
    all_points = jnp.arange(3 * energy_count, dtype=jnp.int32)[None, :]
    weights = jnp.zeros((energy_count, 3 * energy_count), jnp.float32)
    for mode in range(phonon_shift.shape[0]):
        above = (all_points == own_points + energy_count + phonon_shift[mode]).astype(jnp.float32)
        below = (all_points == own_points + energy_count - phonon_shift[mode]).astype(jnp.float32)
        weights = weights + coupling[mode] * (above + below)
    damping = jnp.einsum("ek,skb->seb", weights, widened, precision=lax.Precision.HIGHEST)
    chosen = (
        slab_profile[:, None] == jnp.arange(potential_table.shape[0], dtype=jnp.int32)[None, :]
    ).astype(jnp.float32)
    potential = matmul_exact(chosen, potential_table)
    first_point = lax.axis_index("energy") * energy_count
    energies = energy_low + energy_step * (
        first_point + jnp.arange(energy_count, dtype=jnp.int32)
    ).astype(jnp.float32)
    identity = jnp.eye(orbitals, dtype=jnp.float32)
    real_diag = (
        energies[None, :, None, None] * identity
        - onsite_block
        - potential[:, None, :, None] * identity
    )
    imag_diag = (broadening + damping)[..., None] * identity
    blocks = jnp.stack([real_diag, imag_diag], axis=1)
    inner = slab_count - 1
    position = jnp.arange(inner, dtype=jnp.int32)
    zeros_block = jnp.zeros((inner, energy_count, orbitals, orbitals), jnp.float32)
    first_real = (position == 0).astype(jnp.float32)[:, None, None, None] * identity + zeros_block
    last_real = (position == inner - 1).astype(jnp.float32)[
        :, None, None, None
    ] * identity + zeros_block
    first_part = jnp.stack([first_real, zeros_block], axis=1)
    last_part = jnp.stack([last_real, zeros_block], axis=1)
    right = jnp.concatenate([first_part, last_part, source[:inner]], axis=-1)

    def forward(carry, inputs):
        inverse, solved = carry
        block, rhs = inputs
        pivot = block - matmul_exact(hop_t, matmul_exact(inverse, hopping_block))
        rhs = rhs + matmul_exact(hop_t, solved)
        inverse = invert(pivot)
        solved = complex_product(inverse, rhs)
        return ((inverse, solved), (inverse, solved))

    start = (
        jnp.zeros((2, energy_count, orbitals, orbitals), jnp.float32),
        jnp.zeros(right.shape[1:], jnp.float32),
    )
    _, (inverses, solveds) = lax.scan(forward, start, (blocks[:inner], right))

    def backward(later, inputs):
        inverse, solved = inputs
        current = solved + complex_product(inverse, matmul_exact(hopping_block, later))
        return (current, current)

    _, eliminated = lax.scan(
        backward, jnp.zeros(right.shape[1:], jnp.float32), (inverses, solveds), reverse=True
    )
    from_first = eliminated[..., :orbitals]
    from_last = eliminated[..., orbitals : 2 * orbitals]
    interior = eliminated[..., 2 * orbitals :]
    own_block = blocks[inner] - matmul_exact(
        hop_t, matmul_exact(from_last[inner - 1], hopping_block)
    )
    lower = -matmul_exact(hop_t, matmul_exact(from_first[inner - 1], hop_t))
    own_right = source[inner] + matmul_exact(hop_t, interior[inner - 1])
    outgoing = jnp.concatenate(
        [
            -matmul_exact(hopping_block, matmul_exact(from_first[0], hop_t)),
            lower,
            matmul_exact(hopping_block, interior[0]),
        ],
        axis=-1,
    )
    incoming = shifted(outgoing, "slab", -1)
    pivot = own_block + incoming[..., :orbitals]
    upper = jnp.swapaxes(incoming[..., orbitals : 2 * orbitals], -1, -2)
    right_side = own_right + incoming[..., 2 * orbitals :]
    lower_now, upper_now, right_now, pivot_now = (lower, upper, right_side, pivot)
    for level in range((lax.axis_size("slab") - 1).bit_length()):
        distance = 1 << level
        scaled = complex_product(
            invert(pivot_now), jnp.concatenate([lower_now, upper_now, right_now], axis=-1)
        )
        from_below = shifted(scaled, "slab", distance)
        from_above = shifted(scaled, "slab", -distance)
        product_low = complex_product(lower_now, from_below)
        product_up = complex_product(upper_now, from_above)
        pivot_now = (
            pivot_now - product_low[..., orbitals : 2 * orbitals] - product_up[..., :orbitals]
        )
        right_now = right_now - product_low[..., 2 * orbitals :] - product_up[..., 2 * orbitals :]
        lower_now = -product_low[..., :orbitals]
        upper_now = -product_up[..., orbitals : 2 * orbitals]
    separator = complex_product(invert(pivot_now), right_now)
    previous = shifted(separator, "slab", 1)
    inner_solution = (
        interior
        + complex_product(from_first, matmul_exact(hop_t, previous))
        + complex_product(from_last, matmul_exact(hopping_block, separator))
    )
    amplitude = jnp.concatenate([inner_solution, separator[None]], axis=0)
    density = jnp.sum(amplitude[:, 0] ** 2 + amplitude[:, 1] ** 2, axis=-1)
    return (amplitude, density)


def solution(mesh):
    placed = (
        P("slab", None, "energy", None, None),
        P(),
        P(),
        P(),
        P("slab"),
        P("slab", "energy", None),
        P(),
        P(),
    )
    return jax.shard_map(
        per_device,
        mesh=mesh,
        in_specs=placed,
        out_specs=(P("slab", None, "energy", None, None), P("slab", "energy", None)),
        check_vma=False,
    )
```

```python
import functools

import jax
import jax.numpy as jnp
from jax import lax
from jax.experimental import pallas as pl
from jax.experimental.pallas import tpu as pltpu
from jax.sharding import PartitionSpec as P

broadening = 0.05
energy_low = -1.2
energy_step = 0.15
N = 192
COLS = 128
WIDE = 256
BLOCK = 64


def split(x):
    hi=x.astype(jnp.bfloat16); lo=(x-hi.astype(jnp.float32)).astype(jnp.bfloat16)
    return hi,lo
def tn(a,b):
    return lax.dot_general(a,b,(((0,),(0,)),((),())),preferred_element_type=jnp.float32)
def small_inverse8(mr,mi,b):
    lane=lax.broadcasted_iota(jnp.int32,(b,128),1)
    row8=lax.broadcasted_iota(jnp.int32,(8,128),0)
    seg=(lane//b)*b
    off8=(lane-seg)[0:8]
    bc=lambda v: jnp.broadcast_to(v,(8,128))
    for g in range(b//8):
        o=8*g
        Cr=[jnp.take_along_axis(mr,seg+(o+j),axis=1) for j in range(8)]
        Ci=[jnp.take_along_axis(mi,seg+(o+j),axis=1) for j in range(8)]
        cr=[x[o:o+8] for x in Cr]; ci=[x[o:o+8] for x in Ci]
        for p in range(8):
            dr=bc(cr[p][p:p+1]); di=bc(ci[p][p:p+1])
            inv=1.0/(dr*dr+di*di)
            er=dr*inv; ei=-di*inv
            isrow=row8==p
            pr,pi=cr[p],ci[p]
            for j in range(8):
                if j==p: continue
                fr=bc(cr[j][p:p+1]); fi=bc(ci[j][p:p+1])
                tr=fr*er-fi*ei; ti=fr*ei+fi*er
                cr[j]=jnp.where(isrow,tr,cr[j]-(pr*tr-pi*ti))
                ci[j]=jnp.where(isrow,ti,ci[j]-(pr*ti+pi*tr))
            cr[p]=jnp.where(isrow,er,pi*ei-pr*er)
            ci[p]=jnp.where(isrow,ei,-(pr*ei+pi*er))
        ing=(off8>=o)&(off8<o+8)
        G_r=jnp.where(ing,jnp.where(off8-o==row8,1.0,0.0),mr[o:o+8]); G_i=jnp.where(ing,0.0,mi[o:o+8])
        Rr=None
        for j in range(8):
            gr=bc(G_r[j:j+1]); gi=bc(G_i[j:j+1])
            a=cr[j]*gr-ci[j]*gi; c=cr[j]*gi+ci[j]*gr
            Rr,Ri=(a,c) if Rr is None else (Rr+a,Ri+c)
        out_r=[];out_i=[]
        for h in range(b//8):
            if h==g: out_r.append(Rr);out_i.append(Ri);continue
            xr=jnp.where(ing,0.0,mr[8*h:8*h+8]); xi=jnp.where(ing,0.0,mi[8*h:8*h+8])
            for j in range(8):
                rr=bc(Rr[j:j+1]); ri=bc(Ri[j:j+1])
                ar_=Cr[j][8*h:8*h+8]; ai_=Ci[j][8*h:8*h+8]
                xr=xr-(ar_*rr-ai_*ri); xi=xi-(ar_*ri+ai_*rr)
            out_r.append(xr);out_i.append(xi)
        mr=jnp.concatenate(out_r,0); mi=jnp.concatenate(out_i,0)
    return mr,mi

def sweep(B, ar, ai):
    b = BLOCK
    for e in range(B):
        ar[e, :, N:] = jnp.zeros((N, WIDE - N), jnp.float32)
        ai[e, :, N:] = jnp.zeros((N, WIDE - N), jnp.float32)
    lane = lax.broadcasted_iota(jnp.int32, (b, WIDE), 1)
    row = lax.broadcasted_iota(jnp.int32, (b, WIDE), 0)
    l128 = lax.broadcasted_iota(jnp.int32, (b, 128), 1)
    r128 = lax.broadcasted_iota(jnp.int32, (b, 128), 0)

    def step(k, _):
        o = pl.multiple_of(k * b, b)
        rows = [(ar[e, pl.ds(o, b), :], ai[e, pl.ds(o, b), :]) for e in range(B)]
        mr = jnp.where(l128 - b * (l128 // b) == r128, 1.0, 0.0)
        mi = jnp.zeros((b, 128), jnp.float32)
        for e in range(B):
            turn = lax.rem(WIDE - o + e * b, WIDE)
            qr = pltpu.roll(rows[e][0], turn, 1)[:, 0:128]
            qi = pltpu.roll(rows[e][1], turn, 1)[:, 0:128]
            s = (l128 >= e * b) & (l128 < (e + 1) * b)
            mr = jnp.where(s, qr, mr)
            mi = jnp.where(s, qi, mi)
        mr, mi = small_inverse8(mr, mi, b)
        for e in range(B):
            rr, ri = rows[e]
            dr = mr[:, e * b : (e + 1) * b]
            di = mi[:, e * b : (e + 1) * b]
            inside = (lane >= o) & (lane < o + b)
            eye = lane - o == row
            r2 = jnp.where(inside, jnp.where(eye, -1.0, 0.0), rr)
            i2 = jnp.where(inside, 0.0, ri)
            drh, drl = split(dr)
            dih, dil = split(di)
            r2h, r2l = split(r2)
            i2h, i2l = split(i2)
            lhs = jnp.concatenate([drh, dih, drl, dil, drh, dih], 0)
            Rr = tn(lhs, jnp.concatenate([r2h, -i2h, r2h, -i2h, r2l, -i2l], 0))
            Ri = tn(lhs, jnp.concatenate([i2h, r2h, i2h, r2h, i2l, r2l], 0))
            Rrh, Rrl = split(Rr)
            Rih, Ril = split(Ri)
            rh, rl = split(rr)
            ih, il = split(ri)
            lhs = jnp.concatenate([rh, ih, rl, il, rh, ih], 0)[:, 0:N]
            Ur = tn(lhs, jnp.concatenate([Rrh, -Rih, Rrh, -Rih, Rrl, -Ril], 0))
            Ui = tn(lhs, jnp.concatenate([Rih, Rrh, Rih, Rrh, Ril, Rrl], 0))
            wide = lax.broadcasted_iota(jnp.int32, (N, WIDE), 1)
            m = (wide >= o) & (wide < o + b)
            ar[e] = jnp.where(m, 0.0, ar[e]) - Ur
            ai[e] = jnp.where(m, 0.0, ai[e]) - Ui
            ar[e, pl.ds(o, b), :] = Rr
            ai[e, pl.ds(o, b), :] = Ri
        return 0

    lax.fori_loop(0, N // b, step, 0)


def nn(a, b):
    return jnp.dot(a, b, preferred_element_type=jnp.float32)


def nt(a, b):
    return lax.dot_general(a, b, (((1,), (1,)), ((), ())), preferred_element_type=jnp.float32)


def three(dot, a, b):
    return dot(a[0], b[0]) + (dot(a[0], b[1]) + dot(a[1], b[0]))


def csplit(x):
    return split(x[0]), split(x[1])


def cdot(dot, a, b):
    re = three(dot, a[0], b[0]) - three(dot, a[1], b[1])
    im = three(dot, a[0], b[1]) + three(dot, a[1], b[0])
    return re, im


def real_left(dot, a, b):
    return three(dot, a, b[0]), three(dot, a, b[1])


def real_right(dot, a, b):
    return three(dot, a[0], b), three(dot, a[1], b)


def put(ref, x):
    ref[0] = x[0]
    ref[1] = x[1]


def get(ref):
    return ref[0], ref[1]


def neg(x):
    return -x[0], -x[1]


def add(x, y):
    return x[0] + y[0], x[1] + y[1]


def sub(x, y):
    return x[0] - y[0], x[1] - y[1]


def pack(ref, x):
    ref[0] = x[0][:, 0:128]
    ref[1] = x[1][:, 0:128]
    ref[2] = jnp.concatenate([x[0][:, 128:N], x[1][:, 128:N]], axis=1)


def unpack(ref):
    rest = ref[2]
    return (
        jnp.concatenate([ref[0], rest[:, 0:64]], axis=1),
        jnp.concatenate([ref[1], rest[:, 64:128]], axis=1),
    )


def call(body, name, outs, args, scratch=()):
    return pl.pallas_call(
        body,
        out_shape=tuple(jax.ShapeDtypeStruct(s, jnp.float32) for s in outs),
        in_specs=[pl.BlockSpec(memory_space=pltpu.VMEM)] * len(args),
        out_specs=tuple(pl.BlockSpec(memory_space=pltpu.VMEM) for _ in outs),
        scratch_shapes=list(scratch),
        name=name,
    )(*args)


MATRIX = (2, N, N)
PACKED = (3, N, 128)
VECTOR = (2, N, COLS)
MESSAGE = (5, N, 128)


def work(B):
    return [pltpu.VMEM((B, N, WIDE), jnp.float32)] * 2


def first_body(onsite, hop, dre, dim, x0, x2, p1, p3, q0, tl1, tu1, ar, ai):
    row = lax.broadcasted_iota(jnp.int32, (N, N), 0)
    col = lax.broadcasted_iota(jnp.int32, (N, N), 1)
    eye = row == col

    def block(i):
        return (
            jnp.where(eye, dre[i : i + 1, :], 0.0) - onsite[...],
            jnp.where(eye, dim[i : i + 1, :], 0.0),
        )

    for e in range(2):
        re, im = block(2 * e)
        ar[e, :, 0:N] = re
        ai[e, :, 0:N] = im
    sweep(2, ar, ai)
    h = split(hop[...])
    ht = split(hop[...].T)
    got = []
    for e in range(2):
        x = (-ar[e, :, 0:N], -ai[e, :, 0:N])
        put((x0, x2)[e], x)
        xs = csplit(x)
        up = csplit(real_left(nn, h, xs))
        down = csplit(real_left(nn, ht, xs))
        got.append((up, down))
    (up0, down0), (up2, down2) = got
    one = sub(sub(block(1), real_right(nn, down0, h)), real_right(nn, up2, ht))
    put(p1, one)
    put(p3, sub(block(3), real_right(nn, down2, h)))
    put(q0, real_right(nn, up0, ht))
    put(tl1, neg(real_right(nn, up0, h)))
    put(tu1, neg(real_right(nn, down2, ht)))


def first_rhs_body(x0, x2, hop, r, i0, i2, r1, r3, s0):
    h = split(hop[...])
    ht = split(hop[...].T)
    a = cdot(nn, csplit(get(x0)), csplit((r[0, 0], r[0, 1])))
    c = cdot(nn, csplit(get(x2)), csplit((r[2, 0], r[2, 1])))
    put(i0, a)
    put(i2, c)
    a = csplit(a)
    c = csplit(c)
    put(r1, add((r[1, 0], r[1, 1]), add(real_left(nn, ht, a), real_left(nn, h, c))))
    put(r3, add((r[3, 0], r[3, 1]), real_left(nn, ht, c)))
    put(s0, real_left(nn, h, a))


def second_body(p1, p3, q0, tl1, tu1, x1, z, p3n, pm, om, tl3, ar, ai):
    ar[0, :, 0:N] = p1[0]
    ai[0, :, 0:N] = p1[1]
    sweep(1, ar, ai)
    x = (-ar[0, :, 0:N], -ai[0, :, 0:N])
    put(x1, x)
    xs = csplit(x)
    tl = csplit(get(tl1))
    tu = csplit(get(tu1))
    zl = cdot(nn, tl, xs)
    zu = cdot(nn, tu, xs)
    put(z.at[0], zl)
    put(z.at[1], zu)
    zl = csplit(zl)
    zu = csplit(zu)
    put(p3n, sub(get(p3), cdot(nt, zu, tu)))
    pack(pm, add(get(q0), cdot(nt, zl, tl)))
    pack(tl3, neg(cdot(nt, zl, tu)))
    pack(om, neg(cdot(nt, zu, tl)))


def second_rhs_body(x1, z, tl1, tu1, r1, r3, s0, i1, yl, yu, r3n, rm):
    xs = csplit(get(x1))
    r = csplit(get(r1))
    put(i1, cdot(nn, xs, r))
    put(r3n, sub(get(r3), cdot(nn, csplit(get(z.at[1])), r)))
    put(rm, sub(cdot(nn, csplit(get(z.at[0])), r), get(s0)))
    put(yl, cdot(nt, xs, csplit(get(tl1))))
    put(yu, cdot(nt, xs, csplit(get(tu1))))


def invert_body(count, *refs):
    p, got = refs[0], refs[1 : 1 + count]
    pn, x, ar, ai = refs[1 + count :]
    now = get(p)
    for m in got:
        now = sub(now, unpack(m))
    put(pn, now)
    ar[0, :, 0:N] = now[0]
    ai[0, :, 0:N] = now[1]
    sweep(1, ar, ai)
    put(x, (-ar[0, :, 0:N], -ai[0, :, 0:N]))


def pivot_body(x, tl, tu, z, below, above):
    xs = csplit(get(x))
    tls = csplit(unpack(tl))
    tus = csplit(unpack(tu))
    zl = cdot(nn, tls, xs)
    zu = cdot(nn, tus, xs)
    put(z.at[0], zl)
    put(z.at[1], zu)
    pack(below, cdot(nt, csplit(zu), tus))
    pack(above, cdot(nt, csplit(zl), tls))


def rest_body(count, z, tl, tu, r, *refs):
    got, (rn, below, above) = refs[:count], refs[count:]
    now = get(r)
    for m in got:
        now = sub(now, (m[3], m[4]))
    put(rn, now)
    zl = csplit(get(z.at[0]))
    zu = csplit(get(z.at[1]))
    pack(below, neg(cdot(nt, zl, csplit(unpack(tu)))))
    pack(above, neg(cdot(nt, zu, csplit(unpack(tl)))))
    now = csplit(now)
    put(below.at[pl.ds(3, 2)], cdot(nn, zu, now))
    put(above.at[pl.ds(3, 2)], cdot(nn, zl, now))


def final_body(x, r, below, above, out):
    now = sub(sub(get(r), (below[3], below[4])), (above[3], above[4]))
    put(out, cdot(nn, csplit(get(x)), csplit(now)))


def back_body(x0, x2, i0, i2, i1, yl, yu, hop, prev, x3, out):
    h = split(hop[...])
    ht = split(hop[...].T)
    p = csplit(get(prev))
    last = get(x3)
    q = csplit(last)
    one = sub(sub(get(i1), cdot(nn, csplit(get(yl)), p)), cdot(nn, csplit(get(yu)), q))
    o = csplit(one)
    zero = add(real_left(nn, ht, p), real_left(nn, h, o))
    two = add(real_left(nn, ht, o), real_left(nn, h, q))
    put(out.at[0], add(get(i0), cdot(nn, csplit(get(x0)), csplit(zero))))
    put(out.at[1], one)
    put(out.at[2], add(get(i2), cdot(nn, csplit(get(x2)), csplit(two))))
    put(out.at[3], last)


def per_device(
    source,
    onsite_block,
    hopping_block,
    potential_table,
    slab_profile,
    occupation,
    coupling,
    phonon_shift,
):
    slabs = lax.axis_size("slab")
    width = lax.axis_size("energy")
    energy_count = occupation.shape[1]
    place = lax.axis_index("slab")
    side = lax.rem(place, 2)
    odd = side == 1

    def pair(array, by=0):
        pairs = [
            (s * width + e, (s ^ 1) * width + e + by)
            for s in range(slabs)
            for e in range(width)
            if 0 <= e + by < width
        ]
        return lax.ppermute(array, ("slab", "energy"), pairs)

    def along(array, by):
        pairs = [(e, e + by) for e in range(width) if 0 <= e + by < width]
        return lax.ppermute(array, "energy", pairs)

    def shifted(array, groups):
        by = 2 * groups
        pairs = [(s, s + by) for s in range(slabs) if 0 <= s + by < slabs]
        return lax.ppermute(array, "slab", pairs)

    def in_order(own, other):
        return jnp.where(
            odd, jnp.concatenate([other, own], axis=0), jnp.concatenate([own, other], axis=0)
        )

    chosen = (
        slab_profile[:, None] == jnp.arange(potential_table.shape[0], dtype=jnp.int32)[None, :]
    ).astype(jnp.float32)
    potential = jnp.matmul(chosen, potential_table, precision=lax.Precision.HIGHEST)
    own = jnp.concatenate([along(occupation, 1), occupation, along(occupation, -1)], axis=1)
    middle = pair(jnp.concatenate([occupation, potential[:, None, :]], axis=1))
    other = jnp.concatenate(
        [pair(occupation, 1), middle[:, :energy_count], pair(occupation, -1)], axis=1
    )
    occupied = in_order(own, other)
    potential = in_order(potential, middle[:, energy_count])
    points = jnp.arange(3 * energy_count, dtype=jnp.int32)
    weights = jnp.zeros((3 * energy_count,), jnp.float32)
    for mode in range(phonon_shift.shape[0]):
        above = (points == side + energy_count + phonon_shift[mode]).astype(jnp.float32)
        below = (points == side + energy_count - phonon_shift[mode]).astype(jnp.float32)
        weights = weights + coupling[mode] * (above + below)
    damping = jnp.sum(weights[None, :, None] * occupied, axis=1)
    point = lax.axis_index("energy") * energy_count + side
    dre = energy_low + energy_step * point.astype(jnp.float32) - potential
    dim = broadening + damping

    kept = jnp.where(odd, source[:, :, 1], source[:, :, 0])
    given = jnp.where(odd, source[:, :, 0], source[:, :, 1])
    right = in_order(kept, pair(given))

    x0, x2, p1, p3, q0, tl1, tu1 = call(
        first_body, "first", [MATRIX] * 7, (onsite_block, hopping_block, dre, dim), work(2)
    )
    i0, i2, r1, r3, s0 = call(
        first_rhs_body, "first_rhs", [VECTOR] * 5, (x0, x2, hopping_block, right)
    )
    x1, z1, p, pm, om, tl = call(
        second_body,
        "second",
        [MATRIX, (2,) + MATRIX, MATRIX, PACKED, PACKED, PACKED],
        (p1, p3, q0, tl1, tu1),
        work(1),
    )
    got_p = [shifted(pm, -1)]
    i1, yl, yu, r, rm = call(
        second_rhs_body,
        "second_rhs",
        [VECTOR, MATRIX, MATRIX, VECTOR, VECTOR],
        (x1, z1, tl1, tu1, r1, r3, s0),
    )
    message = shifted(jnp.concatenate([om, rm], axis=0), -1)
    got_m = [message]
    tu = message
    groups = slabs // 2
    for level in range((groups - 1).bit_length()):
        distance = 1 << level
        p, x = call(
            functools.partial(invert_body, len(got_p)),
            "invert",
            [MATRIX, MATRIX],
            (p, *got_p),
            work(1),
        )
        z, below, above = call(
            pivot_body, "pivot", [(2,) + MATRIX, PACKED, PACKED], (x, tl, tu)
        )
        got_p = [shifted(below, distance), shifted(above, -distance)]
        r, below, above = call(
            functools.partial(rest_body, len(got_m)),
            "rest",
            [VECTOR, MESSAGE, MESSAGE],
            (z, tl, tu, r, *got_m),
        )
        tl = shifted(below, distance)
        tu = shifted(above, -distance)
        got_m = [tl, tu]
    p, x = call(
        functools.partial(invert_body, len(got_p)), "invert", [MATRIX, MATRIX], (p, *got_p), work(1)
    )
    (x3,) = call(final_body, "final", [VECTOR], (x, r, *got_m))
    prev = shifted(x3, 1)
    (solved,) = call(
        back_body,
        "back",
        [(4,) + VECTOR],
        (x0, x2, i0, i2, i1, yl, yu, hopping_block, prev, x3),
    )
    mine = jnp.where(odd, solved[2:], solved[:2])
    back = pair(jnp.where(odd, solved[:2], solved[2:]))
    amplitude = jnp.where(
        odd, jnp.stack([back, mine], axis=2), jnp.stack([mine, back], axis=2)
    )
    density = jnp.sum(amplitude[:, 0] ** 2 + amplitude[:, 1] ** 2, axis=-1)
    return (amplitude, density)


def solution(mesh):
    placed = (
        P("slab", None, "energy", None, None),
        P(),
        P(),
        P(),
        P("slab"),
        P("slab", "energy", None),
        P(),
        P(),
    )
    return jax.shard_map(
        per_device,
        mesh=mesh,
        in_specs=placed,
        out_specs=(P("slab", None, "energy", None, None), P("slab", "energy", None)),
        check_vma=False,
    )
```

```python
import functools

import jax
import jax.numpy as jnp
from jax import lax
from jax.experimental import pallas as pl
from jax.experimental.pallas import tpu as pltpu
from jax.sharding import PartitionSpec as P

broadening = 0.05
energy_low = -1.2
energy_step = 0.15
N = 192
COLS = 128
WIDE = 256
BLOCK = 32


def split(x):
    hi = x.astype(jnp.bfloat16)
    lo = (x - hi.astype(jnp.float32)).astype(jnp.bfloat16)
    return hi, lo


def tn(a, b):
    return lax.dot_general(a, b, (((0,), (0,)), ((), ())), preferred_element_type=jnp.float32)


def spread(row):
    return jnp.broadcast_to(row, (8, 128))


def invert_eight(cr, ci):
    row = lax.broadcasted_iota(jnp.int32, (8, 128), 0)
    for p in range(8):
        dr, di = spread(cr[p][p : p + 1]), spread(ci[p][p : p + 1])
        inv = 1.0 / (dr * dr + di * di)
        er, ei = dr * inv, -di * inv
        here = row == p
        wr = jnp.where(here, 1.0 - er, cr[p] * er - ci[p] * ei)
        wi = jnp.where(here, -ei, cr[p] * ei + ci[p] * er)
        for j in range(8):
            if j != p:
                fr, fi = spread(cr[j][p : p + 1]), spread(ci[j][p : p + 1])
                cr[j], ci[j] = cr[j] - (wr * fr - wi * fi), ci[j] - (wr * fi + wi * fr)
        cr[p] = jnp.where(here, er, -wr)
        ci[p] = jnp.where(here, ei, -wi)
    return cr, ci


def small_inverse(m):
    lane = lax.broadcasted_iota(jnp.int32, (8, 128), 1)
    row = lax.broadcasted_iota(jnp.int32, (8, 128), 0)
    start = (lane // 64) * 64
    real = lane - start < 32
    off = lane - (lane // 32) * 32

    def turned(x):
        return jnp.where(real, -pltpu.roll(x, 96, 1), pltpu.roll(x, 32, 1))

    def group(g, _):
        o = pl.multiple_of(8 * g, 8)
        own = m[pl.ds(o, 8), :]
        parts = [m[8 * h : 8 * h + 8, :] for h in range(4)]
        take = lambda x, j: jnp.take_along_axis(x, start + (o + j), axis=1)
        cr = [take(own, j) for j in range(8)]
        ci = [take(own, j + 32) for j in range(8)]
        wide_r = [[take(x, j) for j in range(8)] for x in parts]
        wide_i = [[take(x, j + 32) for j in range(8)] for x in parts]
        inside = (off >= o) & (off < o + 8)
        eye = jnp.where(real & (off - o == row), 1.0, 0.0)
        now = jnp.where(inside, eye, own)
        side = turned(now)
        rows = [(spread(now[j : j + 1]), spread(side[j : j + 1])) for j in range(8)]
        cr, ci = invert_eight(cr, ci)
        out = sum(cr[j] * rows[j][0] + ci[j] * rows[j][1] for j in range(8))
        turn = sum(cr[j] * rows[j][1] - ci[j] * rows[j][0] for j in range(8))
        for h in range(4):
            x = jnp.where(inside, 0.0, parts[h])
            for j in range(8):
                x = x - (
                    wide_r[h][j] * spread(out[j : j + 1]) + wide_i[h][j] * spread(turn[j : j + 1])
                )
            m[8 * h : 8 * h + 8, :] = x
        m[pl.ds(o, 8), :] = out
        return 0

    lax.fori_loop(0, 4, group, 0)


def sweep(B, ar, ai, m):
    b = BLOCK
    for e in range(B):
        ar[e, :, N:] = jnp.zeros((N, WIDE - N), jnp.float32)
        ai[e, :, N:] = jnp.zeros((N, WIDE - N), jnp.float32)
    lane = lax.broadcasted_iota(jnp.int32, (b, WIDE), 1)
    row = lax.broadcasted_iota(jnp.int32, (b, WIDE), 0)
    l128 = lax.broadcasted_iota(jnp.int32, (b, 128), 1)
    r128 = lax.broadcasted_iota(jnp.int32, (b, 128), 0)
    quarter = l128 // 32

    def step(k, _):
        o = pl.multiple_of(k * b, b)
        rows = [(ar[e, pl.ds(o, b), :], ai[e, pl.ds(o, b), :]) for e in range(B)]
        q = jnp.where((lax.rem(quarter, 2) == 0) & (l128 - 32 * quarter == r128), 1.0, 0.0)
        for e in range(B):
            for part in range(2):
                turn = lax.rem(WIDE - o + 64 * e + 32 * part, WIDE)
                q = jnp.where(
                    quarter == 2 * e + part, pltpu.roll(rows[e][part], turn, 1)[:, 0:128], q
                )
        m[...] = q
        small_inverse(m)
        q = m[...]
        for e in range(B):
            rr, ri = rows[e]
            dr = q[:, 64 * e : 64 * e + 32]
            di = q[:, 64 * e + 32 : 64 * e + 64]
            inside = (lane >= o) & (lane < o + b)
            eye = lane - o == row
            r2 = jnp.where(inside, jnp.where(eye, -1.0, 0.0), rr)
            i2 = jnp.where(inside, 0.0, ri)
            drh, drl = split(dr)
            dih, dil = split(di)
            r2h, r2l = split(r2)
            i2h, i2l = split(i2)
            lhs = jnp.concatenate([drh, dih, drl, dil, drh, dih], 0)
            Rr = tn(lhs, jnp.concatenate([r2h, -i2h, r2h, -i2h, r2l, -i2l], 0))
            Ri = tn(lhs, jnp.concatenate([i2h, r2h, i2h, r2h, i2l, r2l], 0))
            Rrh, Rrl = split(Rr)
            Rih, Ril = split(Ri)
            rh, rl = split(rr)
            ih, il = split(ri)
            lhs = jnp.concatenate([rh, ih, rl, il, rh, ih], 0)[:, 0:N]
            Ur = tn(lhs, jnp.concatenate([Rrh, -Rih, Rrh, -Rih, Rrl, -Ril], 0))
            Ui = tn(lhs, jnp.concatenate([Rih, Rrh, Rih, Rrh, Ril, Rrl], 0))
            wide = lax.broadcasted_iota(jnp.int32, (N, WIDE), 1)
            strip = (wide >= o) & (wide < o + b)
            ar[e] = jnp.where(strip, 0.0, ar[e]) - Ur
            ai[e] = jnp.where(strip, 0.0, ai[e]) - Ui
            ar[e, pl.ds(o, b), :] = Rr
            ai[e, pl.ds(o, b), :] = Ri
        return 0

    lax.fori_loop(0, N // b, step, 0)


def nn(a, b):
    return jnp.dot(a, b, preferred_element_type=jnp.float32)


def nt(a, b):
    return lax.dot_general(a, b, (((1,), (1,)), ((), ())), preferred_element_type=jnp.float32)


def three(dot, a, b):
    return dot(a[0], b[0]) + (dot(a[0], b[1]) + dot(a[1], b[0]))


def csplit(x):
    return split(x[0]), split(x[1])


def cdot(dot, a, b):
    re = three(dot, a[0], b[0]) - three(dot, a[1], b[1])
    im = three(dot, a[0], b[1]) + three(dot, a[1], b[0])
    return re, im


def real_left(dot, a, b):
    return three(dot, a, b[0]), three(dot, a, b[1])


def real_right(dot, a, b):
    return three(dot, a[0], b), three(dot, a[1], b)


def put(ref, x):
    ref[0] = x[0]
    ref[1] = x[1]


def get(ref):
    return ref[0], ref[1]


def neg(x):
    return -x[0], -x[1]


def add(x, y):
    return x[0] + y[0], x[1] + y[1]


def sub(x, y):
    return x[0] - y[0], x[1] - y[1]


def pack(ref, x):
    ref[0] = x[0][:, 0:128]
    ref[1] = x[1][:, 0:128]
    ref[2] = jnp.concatenate([x[0][:, 128:N], x[1][:, 128:N]], axis=1)


def unpack(ref):
    rest = ref[2]
    return (
        jnp.concatenate([ref[0], rest[:, 0:64]], axis=1),
        jnp.concatenate([ref[1], rest[:, 64:128]], axis=1),
    )


def call(body, name, cost, outs, args, scratch=(), scalars=0):
    return pl.pallas_call(
        body,
        out_shape=tuple(jax.ShapeDtypeStruct(s, jnp.float32) for s in outs),
        in_specs=[pl.BlockSpec(memory_space=pltpu.SMEM)] * scalars
        + [pl.BlockSpec(memory_space=pltpu.VMEM)] * (len(args) - scalars),
        out_specs=tuple(pl.BlockSpec(memory_space=pltpu.VMEM) for _ in outs),
        scratch_shapes=list(scratch),
        name=name,
        cost_estimate=pl.CostEstimate(
            flops=int(cost * 1.1e9), bytes_accessed=1 << 20, transcendentals=0
        ),
    )(*args)


MATRIX = (2, N, N)
PACKED = (3, N, 128)
VECTOR = (2, N, COLS)
MESSAGE = (5, N, 128)


def work(B):
    return [pltpu.VMEM((B, N, WIDE), jnp.float32)] * 2 + [pltpu.VMEM((BLOCK, 128), jnp.float32)]


def first_body(onsite, hop, dre, dim, xa, p1, p3, q0, tl1, tu1, ar, ai, m):
    row = lax.broadcasted_iota(jnp.int32, (N, N), 0)
    col = lax.broadcasted_iota(jnp.int32, (N, N), 1)
    eye = row == col

    def block(i):
        return (
            jnp.where(eye, dre[i : i + 1, :], 0.0) - onsite[...],
            jnp.where(eye, dim[i : i + 1, :], 0.0),
        )

    for e in range(2):
        re, im = block(2 * e)
        ar[e, :, 0:N] = re
        ai[e, :, 0:N] = im
    sweep(2, ar, ai, m)
    h = split(hop[...])
    ht = split(hop[...].T)
    got = []
    for e in range(2):
        x = (-ar[e, :, 0:N], -ai[e, :, 0:N])
        put(xa.at[e], x)
        xs = csplit(x)
        up = csplit(real_left(nn, h, xs))
        down = csplit(real_left(nn, ht, xs))
        got.append((up, down))
    (up0, down0), (up2, down2) = got
    one = sub(sub(block(1), real_right(nn, down0, h)), real_right(nn, up2, ht))
    put(p1, one)
    put(p3, sub(block(3), real_right(nn, down2, h)))
    put(q0, real_right(nn, up0, ht))
    put(tl1, neg(real_right(nn, up0, h)))
    put(tu1, neg(real_right(nn, down2, ht)))


def first_rhs_body(xa, hop, r, ia, r1, r3, s0):
    h = split(hop[...])
    ht = split(hop[...].T)
    a = cdot(nn, csplit(get(xa.at[0])), csplit((r[0, 0], r[0, 1])))
    c = cdot(nn, csplit(get(xa.at[1])), csplit((r[2, 0], r[2, 1])))
    put(ia.at[0], a)
    put(ia.at[1], c)
    a = csplit(a)
    c = csplit(c)
    put(r1, add((r[1, 0], r[1, 1]), add(real_left(nn, ht, a), real_left(nn, h, c))))
    put(r3, add((r[3, 0], r[3, 1]), real_left(nn, ht, c)))
    put(s0, real_left(nn, h, a))


def second_body(p1, p3, q0, tl1, tu1, x1, z, p3n, pm, om, tl3, ar, ai, m):
    ar[0, :, 0:N] = p1[0]
    ai[0, :, 0:N] = p1[1]
    sweep(1, ar, ai, m)
    x = (-ar[0, :, 0:N], -ai[0, :, 0:N])
    put(x1, x)
    xs = csplit(x)
    tl = csplit(get(tl1))
    tu = csplit(get(tu1))
    zl = cdot(nn, tl, xs)
    zu = cdot(nn, tu, xs)
    put(z.at[0], zl)
    put(z.at[1], zu)
    zl = csplit(zl)
    zu = csplit(zu)
    put(p3n, sub(get(p3), cdot(nt, zu, tu)))
    pack(pm, add(get(q0), cdot(nt, zl, tl)))
    pack(tl3, neg(cdot(nt, zl, tu)))
    pack(om, neg(cdot(nt, zu, tl)))


def second_rhs_body(x1, z, tl1, tu1, r1, r3, s0, i1, yl, yu, r3n, rm):
    xs = csplit(get(x1))
    r = csplit(get(r1))
    put(i1, cdot(nn, xs, r))
    put(r3n, sub(get(r3), cdot(nn, csplit(get(z.at[1])), r)))
    put(rm, sub(cdot(nn, csplit(get(z.at[0])), r), get(s0)))
    put(yl, cdot(nt, xs, csplit(get(tl1))))
    put(yu, cdot(nt, xs, csplit(get(tu1))))


def invert_body(count, *refs):
    p, got = refs[0], refs[1 : 1 + count]
    pn, x, ar, ai, m = refs[1 + count :]
    now = get(p)
    for one in got:
        now = sub(now, unpack(one))
    put(pn, now)
    ar[0, :, 0:N] = now[0]
    ai[0, :, 0:N] = now[1]
    sweep(1, ar, ai, m)
    put(x, (-ar[0, :, 0:N], -ai[0, :, 0:N]))


def pivot_body(x, tl, tu, z, below, above):
    xs = csplit(get(x))
    tls = csplit(unpack(tl))
    tus = csplit(unpack(tu))
    zl = cdot(nn, tls, xs)
    zu = cdot(nn, tus, xs)
    put(z.at[0], zl)
    put(z.at[1], zu)
    pack(below, cdot(nt, csplit(zu), tus))
    pack(above, cdot(nt, csplit(zl), tls))


def rest_body(count, z, tl, tu, r, *refs):
    got, (rn, below, above) = refs[:count], refs[count:]
    now = get(r)
    for one in got:
        now = sub(now, (one[3], one[4]))
    put(rn, now)
    zl = csplit(get(z.at[0]))
    zu = csplit(get(z.at[1]))
    pack(below, neg(cdot(nt, zl, csplit(unpack(tu)))))
    pack(above, neg(cdot(nt, zu, csplit(unpack(tl)))))
    now = csplit(now)
    put(below.at[pl.ds(3, 2)], cdot(nn, zu, now))
    put(above.at[pl.ds(3, 2)], cdot(nn, zl, now))


def final_body(x, r, below, above, out):
    now = sub(sub(get(r), get(below)), get(above))
    put(out, cdot(nn, csplit(get(x)), csplit(now)))


def last_body(count, z, r, *refs):
    got, (rn, below, above) = refs[:count], refs[count:]
    now = get(r)
    for one in got:
        now = sub(now, (one[3], one[4]))
    put(rn, now)
    now = csplit(now)
    put(below, cdot(nn, csplit(get(z.at[1])), now))
    put(above, cdot(nn, csplit(get(z.at[0])), now))


def solve_pair(low, xa, ia, h, ht, first, second, out):
    t = add(real_left(nn, ht, csplit(first)), real_left(nn, h, csplit(second)))
    at = 1 - low
    x = xa[at, 0], xa[at, 1]
    put(out.at[0], add((ia[at, 0], ia[at, 1]), cdot(nn, csplit(x), csplit(t))))
    put(out.at[1], second)


def chosen_ends(low, prev, middle, last):
    pick = jnp.full((N, COLS), low, jnp.int32) == 1
    first = tuple(jnp.where(pick, a, b) for a, b in zip(prev, middle))
    second = tuple(jnp.where(pick, a, b) for a, b in zip(middle, last))
    return first, second


def back_body(odd, xa, ia, i1, yl, yu, hop, prev, x3, mid, out):
    last = get(x3)
    before = get(prev)
    one = sub(
        sub(get(i1), cdot(nn, csplit(get(yl)), csplit(before))),
        cdot(nn, csplit(get(yu)), csplit(last)),
    )
    put(mid, one)
    low = odd[0]
    first, second = chosen_ends(low, before, one, last)
    solve_pair(low, xa, ia, split(hop[...]), split(hop[...].T), first, second, out)


def own_body(odd, xa, ia, mid, hop, prev, x3, out):
    low = 1 - odd[0]
    first, second = chosen_ends(low, get(prev), get(mid), get(x3))
    solve_pair(low, xa, ia, split(hop[...]), split(hop[...].T), first, second, out)


def finish_body(side, mine, other, amplitude, density):
    for which, part in ((side[0], mine), (1 - side[0], other)):
        for slab in range(2):
            re, im = part[slab, 0], part[slab, 1]
            amplitude[slab, 0, which] = re
            amplitude[slab, 1, which] = im
            total = jnp.sum((re * re + im * im).T, axis=0, keepdims=True)
            density[slab, pl.ds(which, 1), :] = total


def per_device(
    source,
    onsite_block,
    hopping_block,
    potential_table,
    slab_profile,
    occupation,
    coupling,
    phonon_shift,
):
    slabs = lax.axis_size("slab")
    width = lax.axis_size("energy")
    energy_count = occupation.shape[1]
    place = lax.axis_index("slab")
    odd = lax.rem(place, 2)
    side = (lax.rem(place, 4) // 2 + odd + 1) % 2
    def pair(array, by=0):
        pairs = [
            (s * width + e, (s ^ 1) * width + e + by)
            for s in range(slabs)
            for e in range(width)
            if 0 <= e + by < width
        ]
        return lax.ppermute(array, ("slab", "energy"), pairs)

    def along(array, by):
        pairs = [(e, e + by) for e in range(width) if 0 <= e + by < width]
        return lax.ppermute(array, "energy", pairs)

    def shifted(array, groups):
        count = slabs // 2
        spot = lambda g, chain: 2 * g + ((1 - chain) if g % 2 == 0 else chain)
        pairs = [
            (spot(g, chain), spot(g + groups, chain))
            for g in range(count)
            for chain in range(2)
            if 0 <= g + groups < count
        ]
        return lax.ppermute(array, "slab", pairs)

    def in_order(own, other):
        return jnp.where(
            odd == 1, jnp.concatenate([other, own], axis=0), jnp.concatenate([own, other], axis=0)
        )

    chosen = (
        slab_profile[:, None] == jnp.arange(potential_table.shape[0], dtype=jnp.int32)[None, :]
    ).astype(jnp.float32)
    potential = jnp.matmul(chosen, potential_table, precision=lax.Precision.HIGHEST)
    own = jnp.concatenate([along(occupation, 1), occupation, along(occupation, -1)], axis=1)
    middle = pair(jnp.concatenate([occupation, potential[:, None, :]], axis=1))
    other = jnp.concatenate(
        [pair(occupation, 1), middle[:, :energy_count], pair(occupation, -1)], axis=1
    )
    occupied = in_order(own, other)
    potential = in_order(potential, middle[:, energy_count])
    points = jnp.arange(3 * energy_count, dtype=jnp.int32)
    weights = jnp.zeros((3 * energy_count,), jnp.float32)
    for mode in range(phonon_shift.shape[0]):
        above = (points == side + energy_count + phonon_shift[mode]).astype(jnp.float32)
        below = (points == side + energy_count - phonon_shift[mode]).astype(jnp.float32)
        weights = weights + coupling[mode] * (above + below)
    damping = jnp.sum(weights[None, :, None] * occupied, axis=1)
    point = lax.axis_index("energy") * energy_count + side
    dre = energy_low + energy_step * point.astype(jnp.float32) - potential
    dim = broadening + damping

    kept = lax.dynamic_index_in_dim(source, side, 2, keepdims=False)
    given = lax.dynamic_index_in_dim(source, 1 - side, 2, keepdims=False)
    right = in_order(kept, pair(given))

    xa, p1, p3, q0, tl1, tu1 = call(
        first_body,
        "first",
        14,
        [(2,) + MATRIX] + [MATRIX] * 5,
        (onsite_block, hopping_block, dre, dim),
        work(2),
    )
    ia, r1, r3, s0 = call(
        first_rhs_body, "first_rhs", 4, [(2,) + VECTOR] + [VECTOR] * 3, (xa, hopping_block, right)
    )
    x1, z1, p, pm, om, tl = call(
        second_body,
        "second",
        14,
        [MATRIX, (2,) + MATRIX, MATRIX, PACKED, PACKED, PACKED],
        (p1, p3, q0, tl1, tu1),
        work(1),
    )
    got_p = [shifted(pm, -1)]
    i1, yl, yu, r, rm = call(
        second_rhs_body,
        "second_rhs",
        4,
        [VECTOR, MATRIX, MATRIX, VECTOR, VECTOR],
        (x1, z1, tl1, tu1, r1, r3, s0),
    )
    message = shifted(jnp.concatenate([om, rm], axis=0), -1)
    got_m = [message]
    tu = message
    groups = slabs // 2
    levels = (groups - 1).bit_length()
    for level in range(levels):
        distance = 1 << level
        p, x = call(
            functools.partial(invert_body, len(got_p)),
            "invert",
            12,
            [MATRIX, MATRIX],
            (p, *got_p),
            work(1),
        )
        z, below, above = call(
            pivot_body, "pivot", 4, [(2,) + MATRIX, PACKED, PACKED], (x, tl, tu)
        )
        got_p = [shifted(below, distance), shifted(above, -distance)]
        if level < levels - 1:
            r, below, above = call(
                functools.partial(rest_body, len(got_m)),
                "rest",
                4,
                [VECTOR, MESSAGE, MESSAGE],
                (z, tl, tu, r, *got_m),
            )
        else:
            r, below, above = call(
                functools.partial(last_body, len(got_m)), "last", 2, [VECTOR] * 3, (z, r, *got_m)
            )
        tl = shifted(below, distance)
        tu = shifted(above, -distance)
        got_m = [tl, tu]
    p, x = call(
        functools.partial(invert_body, len(got_p)),
        "invert",
        12,
        [MATRIX, MATRIX],
        (p, *got_p),
        work(1),
    )
    (x3,) = call(final_body, "final", 2, [VECTOR], (x, r, *got_m))
    prev = shifted(x3, 1)
    low = jnp.reshape(odd, (1,))
    mid, sent = call(
        back_body,
        "back",
        3,
        [VECTOR, (2,) + VECTOR],
        (low, xa, ia, i1, yl, yu, hopping_block, prev, x3),
        scalars=1,
    )
    back = pair(sent)
    (mine,) = call(
        own_body,
        "own",
        2,
        [(2,) + VECTOR],
        (low, xa, ia, mid, hopping_block, prev, x3),
        scalars=1,
    )
    return call(
        finish_body,
        "finish",
        2,
        [source.shape, occupation.shape],
        (jnp.reshape(side, (1,)), mine, back),
        scalars=1,
    )


def solution(mesh):
    placed = (
        P("slab", None, "energy", None, None),
        P(),
        P(),
        P(),
        P("slab"),
        P("slab", "energy", None),
        P(),
        P(),
    )
    return jax.shard_map(
        per_device,
        mesh=mesh,
        in_specs=placed,
        out_specs=(P("slab", None, "energy", None, None), P("slab", "energy", None)),
        check_vma=False,
    )
```

```python
import functools

import jax
import jax.numpy as jnp
from jax import lax
from jax.experimental import pallas as pl
from jax.experimental.pallas import tpu as pltpu
from jax.sharding import PartitionSpec as P

broadening = 0.05
energy_low = -1.2
energy_step = 0.15
N = 192
COLS = 128
WIDE = 256
BLOCK = 32


def split(x):
    hi = x.astype(jnp.bfloat16)
    lo = (x - hi.astype(jnp.float32)).astype(jnp.bfloat16)
    return hi, lo


def tn(a, b):
    return lax.dot_general(a, b, (((0,), (0,)), ((), ())), preferred_element_type=jnp.float32)


def spread(row):
    return jnp.broadcast_to(row, (8, 128))


def invert_eight(cr, ci):
    row = lax.broadcasted_iota(jnp.int32, (8, 128), 0)
    for p in range(8):
        dr, di = spread(cr[p][p : p + 1]), spread(ci[p][p : p + 1])
        inv = 1.0 / (dr * dr + di * di)
        er, ei = dr * inv, -di * inv
        here = row == p
        wr = jnp.where(here, 1.0 - er, cr[p] * er - ci[p] * ei)
        wi = jnp.where(here, -ei, cr[p] * ei + ci[p] * er)
        for j in range(8):
            if j != p:
                fr, fi = spread(cr[j][p : p + 1]), spread(ci[j][p : p + 1])
                cr[j], ci[j] = cr[j] - (wr * fr - wi * fi), ci[j] - (wr * fi + wi * fr)
        cr[p] = jnp.where(here, er, -wr)
        ci[p] = jnp.where(here, ei, -wi)
    return cr, ci


def small_inverse(m):
    lane = lax.broadcasted_iota(jnp.int32, (8, 128), 1)
    row = lax.broadcasted_iota(jnp.int32, (8, 128), 0)
    start = (lane // 64) * 64
    real = lane - start < 32
    off = lane - (lane // 32) * 32

    def turned(x):
        return jnp.where(real, -pltpu.roll(x, 96, 1), pltpu.roll(x, 32, 1))

    def group(g, _):
        o = pl.multiple_of(8 * g, 8)
        own = m[pl.ds(o, 8), :]
        parts = [m[8 * h : 8 * h + 8, :] for h in range(4)]
        take = lambda x, j: jnp.take_along_axis(x, start + (o + j), axis=1)
        cr = [take(own, j) for j in range(8)]
        ci = [take(own, j + 32) for j in range(8)]
        wide_r = [[take(x, j) for j in range(8)] for x in parts]
        wide_i = [[take(x, j + 32) for j in range(8)] for x in parts]
        inside = (off >= o) & (off < o + 8)
        eye = jnp.where(real & (off - o == row), 1.0, 0.0)
        now = jnp.where(inside, eye, own)
        side = turned(now)
        rows = [(spread(now[j : j + 1]), spread(side[j : j + 1])) for j in range(8)]
        cr, ci = invert_eight(cr, ci)
        out = sum(cr[j] * rows[j][0] + ci[j] * rows[j][1] for j in range(8))
        turn = sum(cr[j] * rows[j][1] - ci[j] * rows[j][0] for j in range(8))
        for h in range(4):
            x = jnp.where(inside, 0.0, parts[h])
            for j in range(8):
                x = x - (
                    wide_r[h][j] * spread(out[j : j + 1]) + wide_i[h][j] * spread(turn[j : j + 1])
                )
            m[8 * h : 8 * h + 8, :] = x
        m[pl.ds(o, 8), :] = out
        return 0

    lax.fori_loop(0, 4, group, 0)


def sweep(B, ar, ai, m):
    b = BLOCK
    for e in range(B):
        ar[e, :, N:] = jnp.zeros((N, WIDE - N), jnp.float32)
        ai[e, :, N:] = jnp.zeros((N, WIDE - N), jnp.float32)
    lane = lax.broadcasted_iota(jnp.int32, (b, WIDE), 1)
    row = lax.broadcasted_iota(jnp.int32, (b, WIDE), 0)
    l128 = lax.broadcasted_iota(jnp.int32, (b, 128), 1)
    r128 = lax.broadcasted_iota(jnp.int32, (b, 128), 0)
    quarter = l128 // 32

    def step(k, _):
        o = pl.multiple_of(k * b, b)
        rows = [(ar[e, pl.ds(o, b), :], ai[e, pl.ds(o, b), :]) for e in range(B)]
        q = jnp.where((lax.rem(quarter, 2) == 0) & (l128 - 32 * quarter == r128), 1.0, 0.0)
        for e in range(B):
            for part in range(2):
                turn = lax.rem(WIDE - o + 64 * e + 32 * part, WIDE)
                q = jnp.where(
                    quarter == 2 * e + part, pltpu.roll(rows[e][part], turn, 1)[:, 0:128], q
                )
        m[...] = q
        small_inverse(m)
        q = m[...]
        for e in range(B):
            rr, ri = rows[e]
            dr = q[:, 64 * e : 64 * e + 32]
            di = q[:, 64 * e + 32 : 64 * e + 64]
            inside = (lane >= o) & (lane < o + b)
            eye = lane - o == row
            r2 = jnp.where(inside, jnp.where(eye, -1.0, 0.0), rr)
            i2 = jnp.where(inside, 0.0, ri)
            drh, drl = split(dr)
            dih, dil = split(di)
            r2h, r2l = split(r2)
            i2h, i2l = split(i2)
            lhs = jnp.concatenate([drh, dih, drl, dil, drh, dih], 0)
            Rr = tn(lhs, jnp.concatenate([r2h, -i2h, r2h, -i2h, r2l, -i2l], 0))
            Ri = tn(lhs, jnp.concatenate([i2h, r2h, i2h, r2h, i2l, r2l], 0))
            Rrh, Rrl = split(Rr)
            Rih, Ril = split(Ri)
            rh, rl = split(rr)
            ih, il = split(ri)
            lhs = jnp.concatenate([rh, ih, rl, il, rh, ih], 0)[:, 0:N]
            Ur = tn(lhs, jnp.concatenate([Rrh, -Rih, Rrh, -Rih, Rrl, -Ril], 0))
            Ui = tn(lhs, jnp.concatenate([Rih, Rrh, Rih, Rrh, Ril, Rrl], 0))
            wide = lax.broadcasted_iota(jnp.int32, (N, WIDE), 1)
            strip = (wide >= o) & (wide < o + b)
            ar[e] = jnp.where(strip, 0.0, ar[e]) - Ur
            ai[e] = jnp.where(strip, 0.0, ai[e]) - Ui
            ar[e, pl.ds(o, b), :] = Rr
            ai[e, pl.ds(o, b), :] = Ri
        return 0

    lax.fori_loop(0, N // b, step, 0)


def nn(a, b):
    return jnp.dot(a, b, preferred_element_type=jnp.float32)


def nt(a, b):
    return lax.dot_general(a, b, (((1,), (1,)), ((), ())), preferred_element_type=jnp.float32)


def three(dot, a, b):
    return dot(a[0], b[0]) + (dot(a[0], b[1]) + dot(a[1], b[0]))


def csplit(x):
    return split(x[0]), split(x[1])


def cdot(dot, a, b):
    re = three(dot, a[0], b[0]) - three(dot, a[1], b[1])
    im = three(dot, a[0], b[1]) + three(dot, a[1], b[0])
    return re, im


def real_left(dot, a, b):
    return three(dot, a, b[0]), three(dot, a, b[1])


def real_right(dot, a, b):
    return three(dot, a[0], b), three(dot, a[1], b)


def put(ref, x):
    ref[0] = x[0]
    ref[1] = x[1]


def get(ref):
    return ref[0], ref[1]


def neg(x):
    return -x[0], -x[1]


def add(x, y):
    return x[0] + y[0], x[1] + y[1]


def sub(x, y):
    return x[0] - y[0], x[1] - y[1]


def pack(ref, x):
    ref[0] = x[0][:, 0:128]
    ref[1] = x[1][:, 0:128]
    ref[2] = jnp.concatenate([x[0][:, 128:N], x[1][:, 128:N]], axis=1)


def unpack(ref):
    rest = ref[2]
    return (
        jnp.concatenate([ref[0], rest[:, 0:64]], axis=1),
        jnp.concatenate([ref[1], rest[:, 64:128]], axis=1),
    )


def call(body, name, cost, outs, args, scratch=(), scalars=0):
    return pl.pallas_call(
        body,
        out_shape=tuple(jax.ShapeDtypeStruct(s, jnp.float32) for s in outs),
        in_specs=[pl.BlockSpec(memory_space=pltpu.SMEM)] * scalars
        + [pl.BlockSpec(memory_space=pltpu.VMEM)] * (len(args) - scalars),
        out_specs=tuple(pl.BlockSpec(memory_space=pltpu.VMEM) for _ in outs),
        scratch_shapes=list(scratch),
        name=name,
        cost_estimate=pl.CostEstimate(
            flops=int(cost * 1.1e9), bytes_accessed=1 << 20, transcendentals=0
        ),
    )(*args)


MATRIX = (2, N, N)
PACKED = (3, N, 128)
VECTOR = (2, N, COLS)
ENDS = (6, N, 128)
RHS = (4, N, COLS)


def work(B):
    return [pltpu.VMEM((B, N, WIDE), jnp.float32)] * 2 + [pltpu.VMEM((BLOCK, 128), jnp.float32)]


def choose(flag, yes, no):
    pick = jnp.full(yes[0].shape, flag, jnp.int32) == 1
    return tuple(jnp.where(pick, y, n) for y, n in zip(yes, no))


def first_body(onsite, hop, dre, dim, xa, p, left, right, ar, ai, m):
    row = lax.broadcasted_iota(jnp.int32, (N, N), 0)
    col = lax.broadcasted_iota(jnp.int32, (N, N), 1)
    eye = row == col

    def block(i):
        return (
            jnp.where(eye, dre[i : i + 1, :], 0.0) - onsite[...],
            jnp.where(eye, dim[i : i + 1, :], 0.0),
        )

    for e in range(2):
        re, im = block(2 * e)
        ar[e, :, 0:N] = re
        ai[e, :, 0:N] = im
    sweep(2, ar, ai, m)
    h = split(hop[...])
    ht = split(hop[...].T)
    got = []
    for e in range(2):
        x = (-ar[e, :, 0:N], -ai[e, :, 0:N])
        put(xa.at[e], x)
        xs = csplit(x)
        up = csplit(real_left(nn, h, xs))
        down = csplit(real_left(nn, ht, xs))
        got.append((up, down))
    (up0, down0), (up2, down2) = got
    pack(p, sub(sub(block(1), real_right(nn, down0, h)), real_right(nn, up2, ht)))
    pack(left.at[pl.ds(0, 3)], neg(real_right(nn, up0, h)))
    pack(left.at[pl.ds(3, 3)], neg(real_right(nn, up0, ht)))
    pack(right.at[pl.ds(0, 3)], neg(real_right(nn, down2, ht)))
    pack(right.at[pl.ds(3, 3)], sub(block(3), real_right(nn, down2, h)))


def first_rhs_body(xa, hop, r, ia, left, right):
    h = split(hop[...])
    ht = split(hop[...].T)
    a = cdot(nn, csplit(get(xa.at[0])), csplit((r[0, 0], r[0, 1])))
    c = cdot(nn, csplit(get(xa.at[1])), csplit((r[2, 0], r[2, 1])))
    put(ia.at[0], a)
    put(ia.at[1], c)
    a = csplit(a)
    c = csplit(c)
    put(
        left.at[pl.ds(0, 2)],
        add((r[1, 0], r[1, 1]), add(real_left(nn, ht, a), real_left(nn, h, c))),
    )
    put(left.at[pl.ds(2, 2)], real_left(nn, h, a))
    right[0] = jnp.zeros((N, COLS), jnp.float32)
    right[1] = jnp.zeros((N, COLS), jnp.float32)
    put(right.at[pl.ds(2, 2)], add((r[3, 0], r[3, 1]), real_left(nn, ht, c)))


def invert_body(count, *refs):
    got = refs[:count]
    x, ar, ai, m = refs[count:]
    now = unpack(got[0])
    for one in got[1:]:
        now = add(now, unpack(one))
    ar[0, :, 0:N] = now[0]
    ai[0, :, 0:N] = now[1]
    sweep(1, ar, ai, m)
    put(x, (-ar[0, :, 0:N], -ai[0, :, 0:N]))


def coupling(ref):
    return unpack(ref.at[pl.ds(0, 3)])


def end_block(ref):
    return unpack(ref.at[pl.ds(3, 3)])


def near_body(flag, x, own, other, zn, near):
    t = csplit(choose(flag[0], coupling(other), coupling(own)))
    z = cdot(nn, t, csplit(get(x)))
    put(zn, z)
    f = choose(flag[0], end_block(other), end_block(own))
    pack(near, sub(f, cdot(nt, csplit(z), t)))


def far_body(flag, x, own, other, zf, out):
    tn_ = csplit(choose(flag[0], coupling(other), coupling(own)))
    tf = csplit(choose(flag[0], coupling(own), coupling(other)))
    z = cdot(nn, tf, csplit(get(x)))
    put(zf, z)
    z = csplit(z)
    pack(out.at[pl.ds(0, 3)], neg(cdot(nt, z, tn_)))
    f = choose(flag[0], end_block(own), end_block(other))
    pack(out.at[pl.ds(3, 3)], sub(f, cdot(nt, z, tf)))


def rhs_ends(ref):
    return (ref[0], ref[1]), (ref[2], ref[3])


def rhs_body(flag, x, zn, zf, own, other, w, out):
    mine, mine_far = rhs_ends(own)
    theirs, theirs_far = rhs_ends(other)
    r = csplit(add(mine, theirs))
    put(w, cdot(nn, csplit(get(x)), r))
    near = choose(flag[0], theirs_far, mine_far)
    far = choose(flag[0], mine_far, theirs_far)
    put(out.at[pl.ds(0, 2)], sub(near, cdot(nn, csplit(get(zn)), r)))
    put(out.at[pl.ds(2, 2)], sub(far, cdot(nn, csplit(get(zf)), r)))


def last_rhs_body(flag, x, zn, own, other, w, out):
    mine, mine_far = rhs_ends(own)
    theirs, theirs_far = rhs_ends(other)
    r = csplit(add(mine, theirs))
    put(w, cdot(nn, csplit(get(x)), r))
    near = choose(flag[0], theirs_far, mine_far)
    put(out, sub(near, cdot(nn, csplit(get(zn)), r)))


def solve_pair(low, xa, ia, h, ht, first, second, out):
    t = add(real_left(nn, ht, csplit(first)), real_left(nn, h, csplit(second)))
    at = 1 - low
    x = xa[at, 0], xa[at, 1]
    put(out.at[0], add((ia[at, 0], ia[at, 1]), cdot(nn, csplit(x), csplit(t))))
    put(out.at[1], second)


def chosen_ends(low, prev, middle, last):
    return choose(low, prev, middle), choose(low, middle, last)


def back_body(count, odd, flags, x, r, *refs):
    levels = [refs[3 * i : 3 * i + 3] for i in range(count)]
    top, xa, ia, hop, prev_out, mid, last_out, out = (
        refs[3 * count : 3 * count + 2],
        *refs[3 * count + 2 :],
    )
    end = cdot(nn, csplit(get(x)), csplit(get(r)))
    zero = (jnp.zeros((N, COLS), jnp.float32),) * 2
    w, zn = top
    one = sub(get(w), cdot(tn, csplit(get(zn)), csplit(end)))
    flag = flags[count]
    near, far = one, choose(flag, zero, end)
    for i in range(count - 1, -1, -1):
        w, zn, zf = levels[i]
        one = sub(
            sub(get(w), cdot(tn, csplit(get(zn)), csplit(near))),
            cdot(tn, csplit(get(zf)), csplit(far)),
        )
        flag = flags[i]
        if i:
            near, far = one, choose(flag, far, near)
    prev = choose(flag, far, near)
    last = choose(flag, near, far)
    put(prev_out, prev)
    put(mid, one)
    put(last_out, last)
    low = odd[0]
    first, second = chosen_ends(low, prev, one, last)
    solve_pair(low, xa, ia, split(hop[...]), split(hop[...].T), first, second, out)


def own_body(odd, xa, ia, mid, hop, prev, x3, out):
    low = 1 - odd[0]
    first, second = chosen_ends(low, get(prev), get(mid), get(x3))
    solve_pair(low, xa, ia, split(hop[...]), split(hop[...].T), first, second, out)


def finish_body(side, mine, other, amplitude, density):
    for which, part in ((side[0], mine), (1 - side[0], other)):
        for slab in range(2):
            re, im = part[slab, 0], part[slab, 1]
            amplitude[slab, 0, which] = re
            amplitude[slab, 1, which] = im
            total = jnp.sum((re * re + im * im).T, axis=0, keepdims=True)
            density[slab, pl.ds(which, 1), :] = total


def per_device(
    source,
    onsite_block,
    hopping_block,
    potential_table,
    slab_profile,
    occupation,
    coupling,
    phonon_shift,
):
    slabs = lax.axis_size("slab")
    energy_count = occupation.shape[1]
    place = lax.axis_index("slab")
    odd = lax.rem(place, 2)
    side = (lax.rem(place, 4) // 2 + odd + 1) % 2
    def pair(array):
        return lax.ppermute(array, "slab", [(s, s ^ 1) for s in range(slabs)])

    def along(array, by):
        width = lax.axis_size("energy")
        pairs = [(e, e + by) for e in range(width) if 0 <= e + by < width]
        return lax.ppermute(array, "energy", pairs)

    def swapped(array, distance):
        spot = lambda g, chain: 2 * g + ((1 - chain) if g % 2 == 0 else chain)
        pairs = [
            (spot(g, chain), spot(g ^ distance, chain))
            for g in range(slabs // 2)
            for chain in range(2)
        ]
        return lax.ppermute(array, "slab", pairs)

    def in_order(own, other):
        return jnp.where(
            odd == 1, jnp.concatenate([other, own], axis=0), jnp.concatenate([own, other], axis=0)
        )

    chosen = (
        slab_profile[:, None] == jnp.arange(potential_table.shape[0], dtype=jnp.int32)[None, :]
    ).astype(jnp.float32)
    potential = jnp.matmul(chosen, potential_table, precision=lax.Precision.HIGHEST)
    widened = jnp.concatenate([along(occupation, 1), occupation, along(occupation, -1)], axis=1)
    own_points = jnp.arange(energy_count, dtype=jnp.int32)[:, None]
    points = jnp.arange(3 * energy_count, dtype=jnp.int32)[None, :]
    weights = jnp.zeros((energy_count, 3 * energy_count), jnp.float32)
    for mode in range(phonon_shift.shape[0]):
        above = (points == own_points + energy_count + phonon_shift[mode]).astype(jnp.float32)
        below = (points == own_points + energy_count - phonon_shift[mode]).astype(jnp.float32)
        weights = weights + coupling[mode] * (above + below)
    damping = jnp.sum(weights[None, :, :, None] * widened[:, None, :, :], axis=2)
    first_side = side == 0
    mine = jnp.where(first_side, damping[:, 0], damping[:, 1])
    yours = jnp.where(first_side, damping[:, 1], damping[:, 0])
    both = in_order(
        jnp.stack([mine, potential], axis=1), pair(jnp.stack([yours, potential], axis=1))
    )
    point = lax.axis_index("energy") * energy_count + side
    dre = energy_low + energy_step * point.astype(jnp.float32) - both[:, 1]
    dim = broadening + both[:, 0]

    kept = lax.dynamic_index_in_dim(source, side, 2, keepdims=False)
    given = lax.dynamic_index_in_dim(source, 1 - side, 2, keepdims=False)
    right = in_order(kept, pair(given))

    xa, near, own, other = call(
        first_body,
        "first",
        14,
        [(2,) + MATRIX, PACKED, ENDS, ENDS],
        (onsite_block, hopping_block, dre, dim),
        work(2),
    )
    ia, own_r, other_r = call(
        first_rhs_body, "first_rhs", 4, [(2,) + VECTOR, RHS, RHS], (xa, hopping_block, right)
    )
    blocks = (near,)
    group = place // 2
    count = (slabs // 2 - 1).bit_length()
    bit = lambda k: (group >> k) & 1
    flags = []
    kept_levels = []
    for level in range(count + 1):
        before = bit(level - 1) if level else 0
        after = bit(level) if level < count else 0
        flag = jnp.reshape((before == after).astype(jnp.int32), (1,))
        flags.append(flag)
        (x,) = call(
            functools.partial(invert_body, len(blocks)), "invert", 12, [MATRIX], blocks, work(1)
        )
        zn, near = call(
            near_body, "near", 3, [MATRIX, PACKED], (flag, x, own, other), scalars=1
        )
        if level == count:
            w, rest = call(
                last_rhs_body,
                "last_rhs",
                2,
                [VECTOR, VECTOR],
                (flag, x, zn, own_r, other_r),
                scalars=1,
            )
            break
        distance = 1 << level
        blocks = (near, swapped(near, distance))
        zf, ends = call(far_body, "far", 3, [MATRIX, ENDS], (flag, x, own, other), scalars=1)
        own, other = ends, swapped(ends, distance)
        w, rest = call(
            rhs_body, "rhs", 2, [VECTOR, RHS], (flag, x, zn, zf, own_r, other_r), scalars=1
        )
        own_r, other_r = rest, swapped(rest, distance)
        kept_levels += [w, zn, zf]
    (x,) = call(functools.partial(invert_body, 1), "invert", 12, [MATRIX], (near,), work(1))
    low = jnp.reshape(odd, (1,))
    prev, mid, x3, sent = call(
        functools.partial(back_body, count),
        "back",
        8,
        [VECTOR, VECTOR, VECTOR, (2,) + VECTOR],
        (low, jnp.concatenate(flags), x, rest, *kept_levels, w, zn, xa, ia, hopping_block),
        scalars=2,
    )
    back = pair(sent)
    (mine,) = call(
        own_body,
        "own",
        2,
        [(2,) + VECTOR],
        (low, xa, ia, mid, hopping_block, prev, x3),
        scalars=1,
    )
    return call(
        finish_body,
        "finish",
        2,
        [source.shape, occupation.shape],
        (jnp.reshape(side, (1,)), mine, back),
        scalars=1,
    )


def solution(mesh):
    placed = (
        P("slab", None, "energy", None, None),
        P(),
        P(),
        P(),
        P("slab"),
        P("slab", "energy", None),
        P(),
        P(),
    )
    return jax.shard_map(
        per_device,
        mesh=mesh,
        in_specs=placed,
        out_specs=(P("slab", None, "energy", None, None), P("slab", "energy", None)),
        check_vma=False,
    )
```

```python
import functools

import jax
import jax.numpy as jnp
from jax import lax
from jax.experimental import pallas as pl
from jax.experimental.pallas import tpu as pltpu
from jax.sharding import PartitionSpec as P

broadening = 0.05
energy_low = -1.2
energy_step = 0.15
N = 192
COLS = 128
WIDE = 256
BLOCK = 32


def split(x):
    hi = x.astype(jnp.bfloat16)
    lo = (x - hi.astype(jnp.float32)).astype(jnp.bfloat16)
    return hi, lo


def tn(a, b):
    return lax.dot_general(a, b, (((0,), (0,)), ((), ())), preferred_element_type=jnp.float32)


def spread(row):
    return jnp.broadcast_to(row, (8, 128))


def invert_eight(cr, ci):
    row = lax.broadcasted_iota(jnp.int32, (8, 128), 0)
    for p in range(8):
        dr, di = spread(cr[p][p : p + 1]), spread(ci[p][p : p + 1])
        inv = 1.0 / (dr * dr + di * di)
        er, ei = dr * inv, -di * inv
        here = row == p
        wr = jnp.where(here, 1.0 - er, cr[p] * er - ci[p] * ei)
        wi = jnp.where(here, -ei, cr[p] * ei + ci[p] * er)
        for j in range(8):
            if j != p:
                fr, fi = spread(cr[j][p : p + 1]), spread(ci[j][p : p + 1])
                cr[j], ci[j] = cr[j] - (wr * fr - wi * fi), ci[j] - (wr * fi + wi * fr)
        cr[p] = jnp.where(here, er, -wr)
        ci[p] = jnp.where(here, ei, -wi)
    return cr, ci


def small_inverse(m):
    lane = lax.broadcasted_iota(jnp.int32, (8, 128), 1)
    row = lax.broadcasted_iota(jnp.int32, (8, 128), 0)
    start = (lane // 64) * 64
    real = lane - start < 32
    off = lane - (lane // 32) * 32

    def turned(x):
        return jnp.where(real, -pltpu.roll(x, 96, 1), pltpu.roll(x, 32, 1))

    def group(g, _):
        o = pl.multiple_of(8 * g, 8)
        own = m[pl.ds(o, 8), :]
        parts = [m[8 * h : 8 * h + 8, :] for h in range(4)]
        take = lambda x, j: jnp.take_along_axis(x, start + (o + j), axis=1)
        cr = [take(own, j) for j in range(8)]
        ci = [take(own, j + 32) for j in range(8)]
        wide_r = [[take(x, j) for j in range(8)] for x in parts]
        wide_i = [[take(x, j + 32) for j in range(8)] for x in parts]
        inside = (off >= o) & (off < o + 8)
        eye = jnp.where(real & (off - o == row), 1.0, 0.0)
        now = jnp.where(inside, eye, own)
        side = turned(now)
        rows = [(spread(now[j : j + 1]), spread(side[j : j + 1])) for j in range(8)]
        cr, ci = invert_eight(cr, ci)
        out = sum(cr[j] * rows[j][0] + ci[j] * rows[j][1] for j in range(8))
        turn = sum(cr[j] * rows[j][1] - ci[j] * rows[j][0] for j in range(8))
        for h in range(4):
            x = jnp.where(inside, 0.0, parts[h])
            for j in range(8):
                x = x - (
                    wide_r[h][j] * spread(out[j : j + 1]) + wide_i[h][j] * spread(turn[j : j + 1])
                )
            m[8 * h : 8 * h + 8, :] = x
        m[pl.ds(o, 8), :] = out
        return 0

    lax.fori_loop(0, 4, group, 0)


def sweep(B, ar, ai, m):
    b = BLOCK
    for e in range(B):
        ar[e, :, N:] = jnp.zeros((N, WIDE - N), jnp.float32)
        ai[e, :, N:] = jnp.zeros((N, WIDE - N), jnp.float32)
    lane = lax.broadcasted_iota(jnp.int32, (b, WIDE), 1)
    row = lax.broadcasted_iota(jnp.int32, (b, WIDE), 0)
    l128 = lax.broadcasted_iota(jnp.int32, (b, 128), 1)
    r128 = lax.broadcasted_iota(jnp.int32, (b, 128), 0)
    quarter = l128 // 32

    def step(k, _):
        o = pl.multiple_of(k * b, b)
        rows = [(ar[e, pl.ds(o, b), :], ai[e, pl.ds(o, b), :]) for e in range(B)]
        q = jnp.where((lax.rem(quarter, 2) == 0) & (l128 - 32 * quarter == r128), 1.0, 0.0)
        for e in range(B):
            for part in range(2):
                turn = lax.rem(WIDE - o + 64 * e + 32 * part, WIDE)
                q = jnp.where(
                    quarter == 2 * e + part, pltpu.roll(rows[e][part], turn, 1)[:, 0:128], q
                )
        m[...] = q
        small_inverse(m)
        q = m[...]
        for e in range(B):
            rr, ri = rows[e]
            dr = q[:, 64 * e : 64 * e + 32]
            di = q[:, 64 * e + 32 : 64 * e + 64]
            inside = (lane >= o) & (lane < o + b)
            eye = lane - o == row
            r2 = jnp.where(inside, jnp.where(eye, -1.0, 0.0), rr)
            i2 = jnp.where(inside, 0.0, ri)
            drh, drl = split(dr)
            dih, dil = split(di)
            r2h, r2l = split(r2)
            i2h, i2l = split(i2)
            lhs = jnp.concatenate([drh, dih, drl, dil, drh, dih], 0)
            Rr = tn(lhs, jnp.concatenate([r2h, -i2h, r2h, -i2h, r2l, -i2l], 0))
            Ri = tn(lhs, jnp.concatenate([i2h, r2h, i2h, r2h, i2l, r2l], 0))
            Rrh, Rrl = split(Rr)
            Rih, Ril = split(Ri)
            rh, rl = split(rr)
            ih, il = split(ri)
            lhs = jnp.concatenate([rh, ih, rl, il, rh, ih], 0)[:, 0:N]
            Ur = tn(lhs, jnp.concatenate([Rrh, -Rih, Rrh, -Rih, Rrl, -Ril], 0))
            Ui = tn(lhs, jnp.concatenate([Rih, Rrh, Rih, Rrh, Ril, Rrl], 0))
            wide = lax.broadcasted_iota(jnp.int32, (N, WIDE), 1)
            strip = (wide >= o) & (wide < o + b)
            ar[e] = jnp.where(strip, 0.0, ar[e]) - Ur
            ai[e] = jnp.where(strip, 0.0, ai[e]) - Ui
            ar[e, pl.ds(o, b), :] = Rr
            ai[e, pl.ds(o, b), :] = Ri
        return 0

    lax.fori_loop(0, N // b, step, 0)


def nn(a, b):
    return jnp.dot(a, b, preferred_element_type=jnp.float32)


def nt(a, b):
    return lax.dot_general(a, b, (((1,), (1,)), ((), ())), preferred_element_type=jnp.float32)


def three(dot, a, b):
    return dot(a[0], b[0]) + (dot(a[0], b[1]) + dot(a[1], b[0]))


def csplit(x):
    return split(x[0]), split(x[1])


def cdot(dot, a, b):
    re = three(dot, a[0], b[0]) - three(dot, a[1], b[1])
    im = three(dot, a[0], b[1]) + three(dot, a[1], b[0])
    return re, im


def real_left(dot, a, b):
    return three(dot, a, b[0]), three(dot, a, b[1])


def real_right(dot, a, b):
    return three(dot, a[0], b), three(dot, a[1], b)


def put(ref, x):
    ref[0] = x[0]
    ref[1] = x[1]


def get(ref):
    return ref[0], ref[1]


def neg(x):
    return -x[0], -x[1]


def add(x, y):
    return x[0] + y[0], x[1] + y[1]


def sub(x, y):
    return x[0] - y[0], x[1] - y[1]


def pack(ref, x):
    ref[0] = x[0][:, 0:128]
    ref[1] = x[1][:, 0:128]
    ref[2] = jnp.concatenate([x[0][:, 128:N], x[1][:, 128:N]], axis=1)


def unpack(ref):
    rest = ref[2]
    return (
        jnp.concatenate([ref[0], rest[:, 0:64]], axis=1),
        jnp.concatenate([ref[1], rest[:, 64:128]], axis=1),
    )


def call(body, name, cost, outs, args, scratch=(), scalars=0):
    return pl.pallas_call(
        body,
        out_shape=tuple(jax.ShapeDtypeStruct(s, jnp.float32) for s in outs),
        in_specs=[pl.BlockSpec(memory_space=pltpu.SMEM)] * scalars
        + [pl.BlockSpec(memory_space=pltpu.VMEM)] * (len(args) - scalars),
        out_specs=tuple(pl.BlockSpec(memory_space=pltpu.VMEM) for _ in outs),
        scratch_shapes=list(scratch),
        name=name,
        cost_estimate=pl.CostEstimate(
            flops=int(cost * 1.1e9), bytes_accessed=1 << 20, transcendentals=0
        ),
    )(*args)


MATRIX = (2, N, N)
PACKED = (3, N, 128)
VECTOR = (2, N, COLS)
ENDS = (6, N, 128)
RHS = (4, N, COLS)
MESSAGE = (10, N, 128)


def work(B):
    return [pltpu.VMEM((B, N, WIDE), jnp.float32)] * 2 + [pltpu.VMEM((BLOCK, 128), jnp.float32)]


def vdot(dot, a, v):
    high, low = split(jnp.concatenate(v, axis=1))
    turn = lambda s: jnp.concatenate([-s[:, COLS:], s[:, :COLS]], axis=1)
    both = three(dot, a[0], (high, low)) + three(dot, a[1], (turn(high), turn(low)))
    return both[:, :COLS], both[:, COLS:]


def real_vdot(a, v):
    both = three(nn, a, split(jnp.concatenate(v, axis=1)))
    return both[:, :COLS], both[:, COLS:]


def choose(flag, yes, no):
    pick = jnp.full(yes[0].shape, flag, jnp.int32) == 1
    return tuple(jnp.where(pick, y, n) for y, n in zip(yes, no))


def damping_body(info, shift, profile, coupling, low, occ, high, table, mine, yours):
    for out, k in ((mine, info[1]), (yours, 1 - info[1])):
        for slab in range(2):
            total = jnp.full((1, N), broadening, jnp.float32)
            for q in range(6):
                w = jnp.float32(0.0)
                for mode in range(shift.shape[0]):
                    c = coupling[mode]
                    w = w + jnp.where(q == k + 2 + shift[mode], c, 0.0)
                    w = w + jnp.where(q == k + 2 - shift[mode], c, 0.0)
                row = (low, occ, high)[q // 2][slab, q % 2 : q % 2 + 1, :]
                total = total + w * row
            out[slab, 0:1, :] = total
            out[slab, 1:2, :] = table[pl.ds(profile[slab], 1), :]


def first_body(info, onsite, hop, mine, theirs, xa, x, zn, left, right, near, ar, ai, m):
    row = lax.broadcasted_iota(jnp.int32, (N, N), 0)
    col = lax.broadcasted_iota(jnp.int32, (N, N), 1)
    eye = row == col
    energy = energy_low + energy_step * info[2].astype(jnp.float32)

    def block(i):
        flag = info[0] if i // 2 else 1 - info[0]
        at = i % 2
        (both,) = choose(flag, (mine[at],), (theirs[at],))
        return (
            jnp.where(eye, energy - both[1:2], 0.0) - onsite[...],
            jnp.where(eye, both[0:1], 0.0),
        )

    for e in range(2):
        re, im = block(2 * e)
        ar[e, :, 0:N] = re
        ai[e, :, 0:N] = im
    sweep(2, ar, ai, m)
    h = split(hop[...])
    ht = split(hop[...].T)
    got = []
    for e in range(2):
        one = (-ar[e, :, 0:N], -ai[e, :, 0:N])
        put(xa.at[e], one)
        xs = csplit(one)
        up = csplit(real_left(nn, h, xs))
        down = csplit(real_left(nn, ht, xs))
        got.append((up, down))
    (up0, down0), (up2, down2) = got
    middle = sub(sub(block(1), real_right(nn, down0, h)), real_right(nn, up2, ht))
    pack(left.at[pl.ds(0, 3)], neg(real_right(nn, up0, h)))
    pack(left.at[pl.ds(3, 3)], neg(real_right(nn, up0, ht)))
    pack(right.at[pl.ds(0, 3)], neg(real_right(nn, down2, ht)))
    pack(right.at[pl.ds(3, 3)], sub(block(3), real_right(nn, down2, h)))
    ar[0, :, 0:N] = middle[0]
    ai[0, :, 0:N] = middle[1]
    sweep(1, ar, ai, m)
    put(x, (-ar[0, :, 0:N], -ai[0, :, 0:N]))
    near_end(info[3], get(x), left, right, zn, lambda v: pack(near, v))


def first_rhs_body(info, xa, hop, kept, other, ia, left, right):
    h = split(hop[...])
    ht = split(hop[...].T)

    def r(i):
        flag = info[0] if i // 2 else 1 - info[0]
        at = i % 2
        return choose(flag, (kept[at, 0], kept[at, 1]), (other[at, 0], other[at, 1]))

    a = vdot(nn, csplit(get(xa.at[0])), r(0))
    c = vdot(nn, csplit(get(xa.at[1])), r(2))
    put(ia.at[0], a)
    put(ia.at[1], c)
    put(left.at[pl.ds(0, 2)], add(r(1), add(real_vdot(ht, a), real_vdot(h, c))))
    put(left.at[pl.ds(2, 2)], real_vdot(h, a))
    right[0] = jnp.zeros((N, COLS), jnp.float32)
    right[1] = jnp.zeros((N, COLS), jnp.float32)
    put(right.at[pl.ds(2, 2)], add(r(3), real_vdot(ht, c)))


def invert_body(own, other, x, ar, ai, m):
    now = add(unpack(own), unpack(other))
    ar[0, :, 0:N] = now[0]
    ai[0, :, 0:N] = now[1]
    sweep(1, ar, ai, m)
    put(x, (-ar[0, :, 0:N], -ai[0, :, 0:N]))


def coupling_of(ref):
    return unpack(ref.at[pl.ds(0, 3)])


def end_block(ref):
    return unpack(ref.at[pl.ds(3, 3)])


def near_end(flag, x, own, other, zn, store):
    t = csplit(choose(flag, coupling_of(other), coupling_of(own)))
    z = cdot(nn, t, csplit(x))
    put(zn, z)
    f = choose(flag, end_block(other), end_block(own))
    store(sub(f, cdot(nt, csplit(z), t)))


def near_body(level, info, x, own, other, zn, near):
    near_end(info[3 + level], get(x), own, other, zn, lambda v: pack(near, v))


def rhs_ends(ref, base):
    return (ref[base], ref[base + 1]), (ref[base + 2], ref[base + 3])


def rest_body(level, base, info, x, zn, own, other, own_r, other_r, w, zf, out):
    flag = info[3 + level]
    xs = csplit(get(x))
    zns = csplit(get(zn))
    t_near = csplit(choose(flag, coupling_of(other), coupling_of(own)))
    t_far = csplit(choose(flag, coupling_of(own), coupling_of(other)))
    mine, mine_far = rhs_ends(own_r, base)
    theirs, theirs_far = rhs_ends(other_r, base)
    r = add(mine, theirs)
    z = cdot(nn, t_far, xs)
    put(w, vdot(nn, xs, r))
    put(out.at[pl.ds(6, 2)], sub(choose(flag, theirs_far, mine_far), vdot(nn, zns, r)))
    put(zf, z)
    z = csplit(z)
    pack(out.at[pl.ds(0, 3)], neg(cdot(nt, z, t_near)))
    f = choose(flag, end_block(own), end_block(other))
    pack(out.at[pl.ds(3, 3)], sub(f, cdot(nt, z, t_far)))
    put(out.at[pl.ds(8, 2)], sub(choose(flag, mine_far, theirs_far), vdot(nn, z, r)))


def solve_pair(low, xa, ia, hop, prev, middle, last, out):
    first = choose(low, prev, middle)
    second = choose(low, middle, last)
    t = add(real_vdot(split(hop[...].T), first), real_vdot(split(hop[...]), second))
    at = 1 - low
    x = xa[at, 0], xa[at, 1]
    put(out.at[0], add((ia[at, 0], ia[at, 1]), vdot(nn, csplit(x), t)))
    put(out.at[1], second)


def back_body(count, info, x, own, other, *refs):
    levels = [refs[3 * i : 3 * i + 3] for i in range(count)]
    xa, ia, hop, prev_out, mid, last_out, out, zn, ar, ai, m = refs[3 * count :]
    flag = info[3 + count]
    xs = get(x)

    def store(v):
        ar[0, :, 0:N] = v[0]
        ai[0, :, 0:N] = v[1]

    near_end(flag, xs, own, other, zn, store)
    mine, mine_far = rhs_ends(own, 6)
    theirs, theirs_far = rhs_ends(other, 6)
    r = add(mine, theirs)
    w = vdot(nn, csplit(xs), r)
    rest = sub(choose(flag, theirs_far, mine_far), vdot(nn, csplit(get(zn)), r))
    sweep(1, ar, ai, m)
    end = vdot(nn, csplit((-ar[0, :, 0:N], -ai[0, :, 0:N])), rest)
    one = sub(w, vdot(tn, csplit(get(zn)), end))
    near, far = one, choose(flag, (jnp.zeros((N, COLS), jnp.float32),) * 2, end)
    for i in range(count - 1, -1, -1):
        w, z_near, z_far = levels[i]
        one = sub(
            sub(get(w), vdot(tn, csplit(get(z_near)), near)),
            vdot(tn, csplit(get(z_far)), far),
        )
        flag = info[3 + i]
        if i:
            near, far = one, choose(flag, far, near)
    prev = choose(flag, far, near)
    last = choose(flag, near, far)
    put(prev_out, prev)
    put(mid, one)
    put(last_out, last)
    solve_pair(info[0], xa, ia, hop, prev, one, last, out)


def own_body(info, xa, ia, mid, hop, prev, last, out):
    solve_pair(1 - info[0], xa, ia, hop, get(prev), get(mid), get(last), out)


def finish_body(info, mine, other, amplitude, density):
    for which, part in ((info[1], mine), (1 - info[1], other)):
        for slab in range(2):
            re, im = part[slab, 0], part[slab, 1]
            amplitude[slab, 0, which] = re
            amplitude[slab, 1, which] = im
            total = jnp.sum((re * re + im * im).T, axis=0, keepdims=True)
            density[slab, pl.ds(which, 1), :] = total


def per_device(
    source,
    onsite_block,
    hopping_block,
    potential_table,
    slab_profile,
    occupation,
    coupling,
    phonon_shift,
):
    slabs = lax.axis_size("slab")
    energy_count = occupation.shape[1]
    place = lax.axis_index("slab")
    odd = lax.rem(place, 2)
    side = (lax.rem(place, 4) // 2 + odd + 1) % 2
    def pair(array):
        return lax.ppermute(array, "slab", [(s, s ^ 1) for s in range(slabs)])

    def along(array, by):
        width = lax.axis_size("energy")
        pairs = [(e, e + by) for e in range(width) if 0 <= e + by < width]
        return lax.ppermute(array, "energy", pairs)

    def swapped(array, distance):
        spot = lambda g, chain: 2 * g + ((1 - chain) if g % 2 == 0 else chain)
        pairs = [
            (spot(g, chain), spot(g ^ distance, chain))
            for g in range(slabs // 2)
            for chain in range(2)
        ]
        return lax.ppermute(array, "slab", pairs)

    group = place // 2
    count = (slabs // 2 - 1).bit_length()
    bit = lambda k: (group >> k) & 1 if 0 <= k < count else 0
    facing = [(bit(k - 1) == bit(k)) * 1 for k in range(count + 1)]
    point = lax.axis_index("energy") * energy_count + side
    info = jnp.stack([jnp.asarray(v, jnp.int32) for v in (odd, side, point, *facing)])
    mine, yours = call(
        damping_body,
        "damping",
        1,
        [(2, 2, N)] * 2,
        (
            info,
            phonon_shift,
            slab_profile,
            coupling,
            along(occupation, 1),
            occupation,
            along(occupation, -1),
            potential_table,
        ),
        scalars=4,
    )
    theirs = pair(yours)
    kept = lax.dynamic_index_in_dim(source, side, 2, keepdims=False)
    given = pair(lax.dynamic_index_in_dim(source, 1 - side, 2, keepdims=False))

    xa, x, zn, own, other, near = call(
        first_body,
        "first",
        30,
        [(2,) + MATRIX, MATRIX, MATRIX, ENDS, ENDS, PACKED],
        (info, onsite_block, hopping_block, mine, theirs),
        work(2),
        scalars=1,
    )
    ia, own_r, other_r = call(
        first_rhs_body,
        "first_rhs",
        3,
        [(2,) + VECTOR, RHS, RHS],
        (info, xa, hopping_block, kept, given),
        scalars=1,
    )
    held = []
    for level in range(count):
        distance = 1 << level
        facing_block = swapped(near, distance)
        w, zf, rest = call(
            functools.partial(rest_body, level, 6 if level else 0),
            "rest",
            5,
            [VECTOR, MATRIX, MESSAGE],
            (info, x, zn, own, other, own_r, other_r),
            scalars=1,
        )
        held += [w, zn, zf]
        own = own_r = rest
        other = other_r = swapped(rest, distance)
        (x,) = call(invert_body, "invert", 12, [MATRIX], (near, facing_block), work(1))
        if level < count - 1:
            zn, near = call(
                functools.partial(near_body, level + 1),
                "near",
                3,
                [MATRIX, PACKED],
                (info, x, own, other),
                scalars=1,
            )
    prev, mid, last, sent = call(
        functools.partial(back_body, count),
        "back",
        22,
        [VECTOR, VECTOR, VECTOR, (2,) + VECTOR],
        (info, x, own, other, *held, xa, ia, hopping_block),
        [pltpu.VMEM(MATRIX, jnp.float32)] + work(1),
        scalars=1,
    )
    back = pair(sent)
    (mine,) = call(
        own_body,
        "own",
        2,
        [(2,) + VECTOR],
        (info, xa, ia, mid, hopping_block, prev, last),
        scalars=1,
    )
    return call(
        finish_body,
        "finish",
        2,
        [source.shape, occupation.shape],
        (info, mine, back),
        scalars=1,
    )


def solution(mesh):
    placed = (
        P("slab", None, "energy", None, None),
        P(),
        P(),
        P(),
        P("slab"),
        P("slab", "energy", None),
        P(),
        P(),
    )
    return jax.shard_map(
        per_device,
        mesh=mesh,
        in_specs=placed,
        out_specs=(P("slab", None, "energy", None, None), P("slab", "energy", None)),
        check_vma=False,
    )
```

```python
import functools

import jax
import jax.numpy as jnp
from jax import lax
from jax.experimental import pallas as pl
from jax.experimental.pallas import tpu as pltpu
from jax.sharding import PartitionSpec as P

broadening = 0.05
energy_low = -1.2
energy_step = 0.15
N = 192
COLS = 128
WIDE = 256
BLOCK = 32


def split(x):
    hi = x.astype(jnp.bfloat16)
    lo = (x - hi.astype(jnp.float32)).astype(jnp.bfloat16)
    return hi, lo


def tn(a, b):
    return lax.dot_general(a, b, (((0,), (0,)), ((), ())), preferred_element_type=jnp.float32)


def spread(row):
    return jnp.broadcast_to(row, (8, 128))


def invert_eight(cr, ci):
    row = lax.broadcasted_iota(jnp.int32, (8, 128), 0)
    for p in range(8):
        dr, di = spread(cr[p][p : p + 1]), spread(ci[p][p : p + 1])
        inv = 1.0 / (dr * dr + di * di)
        er, ei = dr * inv, -di * inv
        here = row == p
        wr = jnp.where(here, 1.0 - er, cr[p] * er - ci[p] * ei)
        wi = jnp.where(here, -ei, cr[p] * ei + ci[p] * er)
        for j in range(8):
            if j != p:
                fr, fi = spread(cr[j][p : p + 1]), spread(ci[j][p : p + 1])
                cr[j], ci[j] = cr[j] - (wr * fr - wi * fi), ci[j] - (wr * fi + wi * fr)
        cr[p] = jnp.where(here, er, -wr)
        ci[p] = jnp.where(here, ei, -wi)
    return cr, ci


def small_inverse(m):
    lane = lax.broadcasted_iota(jnp.int32, (8, 128), 1)
    row = lax.broadcasted_iota(jnp.int32, (8, 128), 0)
    start = (lane // 64) * 64
    real = lane - start < 32
    off = lane - (lane // 32) * 32

    def turned(x):
        return jnp.where(real, -pltpu.roll(x, 96, 1), pltpu.roll(x, 32, 1))

    def group(g, _):
        o = pl.multiple_of(8 * g, 8)
        own = m[pl.ds(o, 8), :]
        parts = [m[8 * h : 8 * h + 8, :] for h in range(4)]
        take = lambda x, j: jnp.take_along_axis(x, start + (o + j), axis=1)
        cr = [take(own, j) for j in range(8)]
        ci = [take(own, j + 32) for j in range(8)]
        wide_r = [[take(x, j) for j in range(8)] for x in parts]
        wide_i = [[take(x, j + 32) for j in range(8)] for x in parts]
        inside = (off >= o) & (off < o + 8)
        eye = jnp.where(real & (off - o == row), 1.0, 0.0)
        now = jnp.where(inside, eye, own)
        side = turned(now)
        rows = [(spread(now[j : j + 1]), spread(side[j : j + 1])) for j in range(8)]
        cr, ci = invert_eight(cr, ci)
        out = sum(cr[j] * rows[j][0] + ci[j] * rows[j][1] for j in range(8))
        turn = sum(cr[j] * rows[j][1] - ci[j] * rows[j][0] for j in range(8))
        for h in range(4):
            x = jnp.where(inside, 0.0, parts[h])
            for j in range(8):
                x = x - (
                    wide_r[h][j] * spread(out[j : j + 1]) + wide_i[h][j] * spread(turn[j : j + 1])
                )
            m[8 * h : 8 * h + 8, :] = x
        m[pl.ds(o, 8), :] = out
        return 0

    lax.fori_loop(0, 4, group, 0)


def sweep(B, ar, ai, m):
    b = BLOCK
    for e in range(B):
        ar[e, :, N:] = jnp.zeros((N, WIDE - N), jnp.float32)
        ai[e, :, N:] = jnp.zeros((N, WIDE - N), jnp.float32)
    lane = lax.broadcasted_iota(jnp.int32, (b, WIDE), 1)
    row = lax.broadcasted_iota(jnp.int32, (b, WIDE), 0)
    l128 = lax.broadcasted_iota(jnp.int32, (b, 128), 1)
    r128 = lax.broadcasted_iota(jnp.int32, (b, 128), 0)
    quarter = l128 // 32

    def step(k, _):
        o = pl.multiple_of(k * b, b)
        rows = [(ar[e, pl.ds(o, b), :], ai[e, pl.ds(o, b), :]) for e in range(B)]
        q = jnp.where((lax.rem(quarter, 2) == 0) & (l128 - 32 * quarter == r128), 1.0, 0.0)
        for e in range(B):
            for part in range(2):
                turn = lax.rem(WIDE - o + 64 * e + 32 * part, WIDE)
                q = jnp.where(
                    quarter == 2 * e + part, pltpu.roll(rows[e][part], turn, 1)[:, 0:128], q
                )
        m[...] = q
        small_inverse(m)
        q = m[...]
        for e in range(B):
            rr, ri = rows[e]
            dr = q[:, 64 * e : 64 * e + 32]
            di = q[:, 64 * e + 32 : 64 * e + 64]
            inside = (lane >= o) & (lane < o + b)
            eye = lane - o == row
            r2 = jnp.where(inside, jnp.where(eye, -1.0, 0.0), rr)
            i2 = jnp.where(inside, 0.0, ri)
            drh, drl = split(dr)
            dih, dil = split(di)
            r2h, r2l = split(r2)
            i2h, i2l = split(i2)
            lhs = jnp.concatenate([drh, dih, drl, dil, drh, dih], 0)
            Rr = tn(lhs, jnp.concatenate([r2h, -i2h, r2h, -i2h, r2l, -i2l], 0))
            Ri = tn(lhs, jnp.concatenate([i2h, r2h, i2h, r2h, i2l, r2l], 0))
            Rrh, Rrl = split(Rr)
            Rih, Ril = split(Ri)
            rh, rl = split(rr)
            ih, il = split(ri)
            lhs = jnp.concatenate([rh, ih, rl, il, rh, ih], 0)[:, 0:N]
            Ur = tn(lhs, jnp.concatenate([Rrh, -Rih, Rrh, -Rih, Rrl, -Ril], 0))
            Ui = tn(lhs, jnp.concatenate([Rih, Rrh, Rih, Rrh, Ril, Rrl], 0))
            wide = lax.broadcasted_iota(jnp.int32, (N, WIDE), 1)
            strip = (wide >= o) & (wide < o + b)
            ar[e] = jnp.where(strip, 0.0, ar[e]) - Ur
            ai[e] = jnp.where(strip, 0.0, ai[e]) - Ui
            ar[e, pl.ds(o, b), :] = Rr
            ai[e, pl.ds(o, b), :] = Ri
        return 0

    lax.fori_loop(0, N // b, step, 0)


def nn(a, b):
    return jnp.dot(a, b, preferred_element_type=jnp.float32)


def nt(a, b):
    return lax.dot_general(a, b, (((1,), (1,)), ((), ())), preferred_element_type=jnp.float32)


def three(dot, a, b):
    return dot(a[0], b[0]) + (dot(a[0], b[1]) + dot(a[1], b[0]))


def csplit(x):
    return split(x[0]), split(x[1])


def cdot(dot, a, b):
    re = three(dot, a[0], b[0]) - three(dot, a[1], b[1])
    im = three(dot, a[0], b[1]) + three(dot, a[1], b[0])
    return re, im


def real_left(dot, a, b):
    return three(dot, a, b[0]), three(dot, a, b[1])


def real_right(dot, a, b):
    return three(dot, a[0], b), three(dot, a[1], b)


def put(ref, x):
    ref[0] = x[0]
    ref[1] = x[1]


def get(ref):
    return ref[0], ref[1]


def neg(x):
    return -x[0], -x[1]


def add(x, y):
    return x[0] + y[0], x[1] + y[1]


def sub(x, y):
    return x[0] - y[0], x[1] - y[1]


def pack(ref, x):
    ref[0] = x[0][:, 0:128]
    ref[1] = x[1][:, 0:128]
    ref[2] = jnp.concatenate([x[0][:, 128:N], x[1][:, 128:N]], axis=1)


def unpack(ref):
    rest = ref[2]
    return (
        jnp.concatenate([ref[0], rest[:, 0:64]], axis=1),
        jnp.concatenate([ref[1], rest[:, 64:128]], axis=1),
    )


def call(body, name, cost, outs, args, scratch=(), scalars=0):
    return pl.pallas_call(
        body,
        out_shape=tuple(jax.ShapeDtypeStruct(s, jnp.float32) for s in outs),
        in_specs=[pl.BlockSpec(memory_space=pltpu.SMEM)] * scalars
        + [pl.BlockSpec(memory_space=pltpu.VMEM)] * (len(args) - scalars),
        out_specs=tuple(pl.BlockSpec(memory_space=pltpu.VMEM) for _ in outs),
        scratch_shapes=list(scratch),
        name=name,
        cost_estimate=pl.CostEstimate(
            flops=int(cost * 1.1e9), bytes_accessed=1 << 20, transcendentals=0
        ),
    )(*args)


MATRIX = (2, N, N)
PACKED = (3, N, 128)
VECTOR = (2, N, COLS)
ENDS = (6, N, 128)
RHS = (4, N, COLS)


def work(B):
    return [pltpu.VMEM((B, N, WIDE), jnp.float32)] * 2 + [pltpu.VMEM((BLOCK, 128), jnp.float32)]


def vdot(dot, a, v):
    high, low = split(jnp.concatenate(v, axis=1))
    turn = lambda s: jnp.concatenate([-s[:, COLS:], s[:, :COLS]], axis=1)
    both = three(dot, a[0], (high, low)) + three(dot, a[1], (turn(high), turn(low)))
    return both[:, :COLS], both[:, COLS:]


def real_vdot(a, v):
    both = three(nn, a, split(jnp.concatenate(v, axis=1)))
    return both[:, :COLS], both[:, COLS:]


def choose(flag, yes, no):
    pick = jnp.full(yes[0].shape, flag, jnp.int32) == 1
    return tuple(jnp.where(pick, y, n) for y, n in zip(yes, no))


def damping_body(info, shift, profile, coupling, low, occ, high, table, mine, yours):
    for out, k in ((mine, info[1]), (yours, 1 - info[1])):
        for slab in range(2):
            total = jnp.full((1, N), broadening, jnp.float32)
            for q in range(6):
                w = jnp.float32(0.0)
                for mode in range(shift.shape[0]):
                    c = coupling[mode]
                    w = w + jnp.where(q == k + 2 + shift[mode], c, 0.0)
                    w = w + jnp.where(q == k + 2 - shift[mode], c, 0.0)
                row = (low, occ, high)[q // 2][slab, q % 2 : q % 2 + 1, :]
                total = total + w * row
            out[slab, 0:1, :] = total
            out[slab, 1:2, :] = table[pl.ds(profile[slab], 1), :]


def first_body(info, onsite, hop, mine, theirs, xa, x, zn, left, right, near, ar, ai, m):
    row = lax.broadcasted_iota(jnp.int32, (N, N), 0)
    col = lax.broadcasted_iota(jnp.int32, (N, N), 1)
    eye = row == col
    energy = energy_low + energy_step * info[2].astype(jnp.float32)

    def block(i):
        flag = info[0] if i // 2 else 1 - info[0]
        at = i % 2
        (both,) = choose(flag, (mine[at],), (theirs[at],))
        return (
            jnp.where(eye, energy - both[1:2], 0.0) - onsite[...],
            jnp.where(eye, both[0:1], 0.0),
        )

    for e in range(2):
        re, im = block(2 * e)
        ar[e, :, 0:N] = re
        ai[e, :, 0:N] = im
    sweep(2, ar, ai, m)
    h = split(hop[...])
    ht = split(hop[...].T)
    got = []
    for e in range(2):
        one = (-ar[e, :, 0:N], -ai[e, :, 0:N])
        put(xa.at[e], one)
        xs = csplit(one)
        up = csplit(real_left(nn, h, xs))
        down = csplit(real_left(nn, ht, xs))
        got.append((up, down))
    (up0, down0), (up2, down2) = got
    middle = sub(sub(block(1), real_right(nn, down0, h)), real_right(nn, up2, ht))
    pack(left.at[pl.ds(0, 3)], neg(real_right(nn, up0, h)))
    pack(left.at[pl.ds(3, 3)], neg(real_right(nn, up0, ht)))
    pack(right.at[pl.ds(0, 3)], neg(real_right(nn, down2, ht)))
    pack(right.at[pl.ds(3, 3)], sub(block(3), real_right(nn, down2, h)))
    ar[0, :, 0:N] = middle[0]
    ai[0, :, 0:N] = middle[1]
    sweep(1, ar, ai, m)
    put(x, (-ar[0, :, 0:N], -ai[0, :, 0:N]))
    near_end(info[3], get(x), left, right, zn, lambda v: pack(near, v))


def first_rhs_body(info, xa, hop, kept, other, ia, left, right):
    h = split(hop[...])
    ht = split(hop[...].T)

    def r(i):
        flag = info[0] if i // 2 else 1 - info[0]
        at = i % 2
        return choose(flag, (kept[at, 0], kept[at, 1]), (other[at, 0], other[at, 1]))

    a = vdot(nn, csplit(get(xa.at[0])), r(0))
    c = vdot(nn, csplit(get(xa.at[1])), r(2))
    put(ia.at[0], a)
    put(ia.at[1], c)
    put(left.at[pl.ds(0, 2)], add(r(1), add(real_vdot(ht, a), real_vdot(h, c))))
    put(left.at[pl.ds(2, 2)], real_vdot(h, a))
    right[0] = jnp.zeros((N, COLS), jnp.float32)
    right[1] = jnp.zeros((N, COLS), jnp.float32)
    put(right.at[pl.ds(2, 2)], add(r(3), real_vdot(ht, c)))


def invert_body(own, other, x, ar, ai, m):
    now = add(unpack(own), unpack(other))
    ar[0, :, 0:N] = now[0]
    ai[0, :, 0:N] = now[1]
    sweep(1, ar, ai, m)
    put(x, (-ar[0, :, 0:N], -ai[0, :, 0:N]))


def coupling_of(ref):
    return unpack(ref.at[pl.ds(0, 3)])


def end_block(ref):
    return unpack(ref.at[pl.ds(3, 3)])


def near_end(flag, x, own, other, zn, store):
    t = csplit(choose(flag, coupling_of(other), coupling_of(own)))
    z = cdot(nn, t, csplit(x))
    put(zn, z)
    f = choose(flag, end_block(other), end_block(own))
    store(sub(f, cdot(nt, csplit(z), t)))


def near_body(level, info, x, own, other, zn, near):
    near_end(info[3 + level], get(x), own, other, zn, lambda v: pack(near, v))


def rhs_ends(ref):
    return (ref[0], ref[1]), (ref[2], ref[3])


def rest_body(level, info, x, zn, own, other, own_r, other_r, w, zf, out, out_r):
    flag = info[3 + level]
    xs = csplit(get(x))
    zns = csplit(get(zn))
    t_near = csplit(choose(flag, coupling_of(other), coupling_of(own)))
    t_far = csplit(choose(flag, coupling_of(own), coupling_of(other)))
    mine, mine_far = rhs_ends(own_r)
    theirs, theirs_far = rhs_ends(other_r)
    r = add(mine, theirs)
    z = cdot(nn, t_far, xs)
    put(w, vdot(nn, xs, r))
    put(out_r.at[pl.ds(0, 2)], sub(choose(flag, theirs_far, mine_far), vdot(nn, zns, r)))
    put(zf, z)
    z = csplit(z)
    pack(out.at[pl.ds(0, 3)], neg(cdot(nt, z, t_near)))
    f = choose(flag, end_block(own), end_block(other))
    pack(out.at[pl.ds(3, 3)], sub(f, cdot(nt, z, t_far)))
    put(out_r.at[pl.ds(2, 2)], sub(choose(flag, mine_far, theirs_far), vdot(nn, z, r)))


def solve_pair(low, xa, ia, hop, prev, middle, last, out):
    first = choose(low, prev, middle)
    second = choose(low, middle, last)
    t = add(real_vdot(split(hop[...].T), first), real_vdot(split(hop[...]), second))
    at = 1 - low
    x = xa[at, 0], xa[at, 1]
    put(out.at[0], add((ia[at, 0], ia[at, 1]), vdot(nn, csplit(x), t)))
    put(out.at[1], second)


def back_body(count, info, x, own, other, own_r, other_r, *refs):
    levels = [refs[3 * i : 3 * i + 3] for i in range(count)]
    xa, ia, hop, prev_out, mid, last_out, out, zn, ar, ai, m = refs[3 * count :]
    flag = info[3 + count]
    xs = get(x)

    def store(v):
        ar[0, :, 0:N] = v[0]
        ai[0, :, 0:N] = v[1]

    near_end(flag, xs, own, other, zn, store)
    mine, mine_far = rhs_ends(own_r)
    theirs, theirs_far = rhs_ends(other_r)
    r = add(mine, theirs)
    w = vdot(nn, csplit(xs), r)
    rest = sub(choose(flag, theirs_far, mine_far), vdot(nn, csplit(get(zn)), r))
    sweep(1, ar, ai, m)
    end = vdot(nn, csplit((-ar[0, :, 0:N], -ai[0, :, 0:N])), rest)
    one = sub(w, vdot(tn, csplit(get(zn)), end))
    near, far = one, choose(flag, (jnp.zeros((N, COLS), jnp.float32),) * 2, end)
    for i in range(count - 1, -1, -1):
        w, z_near, z_far = levels[i]
        one = sub(
            sub(get(w), vdot(tn, csplit(get(z_near)), near)),
            vdot(tn, csplit(get(z_far)), far),
        )
        flag = info[3 + i]
        if i:
            near, far = one, choose(flag, far, near)
    prev = choose(flag, far, near)
    last = choose(flag, near, far)
    put(prev_out, prev)
    put(mid, one)
    put(last_out, last)
    solve_pair(info[0], xa, ia, hop, prev, one, last, out)


def own_body(info, xa, ia, mid, hop, prev, last, out):
    solve_pair(1 - info[0], xa, ia, hop, get(prev), get(mid), get(last), out)


def finish_body(info, mine, other, amplitude, density):
    for which, part in ((info[1], mine), (1 - info[1], other)):
        for slab in range(2):
            re, im = part[slab, 0], part[slab, 1]
            amplitude[slab, 0, which] = re
            amplitude[slab, 1, which] = im
            total = jnp.sum((re * re + im * im).T, axis=0, keepdims=True)
            density[slab, pl.ds(which, 1), :] = total


def per_device(
    source,
    onsite_block,
    hopping_block,
    potential_table,
    slab_profile,
    occupation,
    coupling,
    phonon_shift,
):
    slabs = lax.axis_size("slab")
    energy_count = occupation.shape[1]
    place = lax.axis_index("slab")
    odd = lax.rem(place, 2)
    side = (lax.rem(place, 4) // 2 + odd + 1) % 2
    def pair(array):
        return lax.ppermute(array, "slab", [(s, s ^ 1) for s in range(slabs)])

    def along(array, by):
        width = lax.axis_size("energy")
        pairs = [(e, e + by) for e in range(width) if 0 <= e + by < width]
        return lax.ppermute(array, "energy", pairs)

    def swapped(array, distance):
        spot = lambda g, chain: 2 * g + ((1 - chain) if g % 2 == 0 else chain)
        pairs = [
            (spot(g, chain), spot(g ^ distance, chain))
            for g in range(slabs // 2)
            for chain in range(2)
        ]
        return lax.ppermute(array, "slab", pairs)

    group = place // 2
    count = (slabs // 2 - 1).bit_length()
    bit = lambda k: (group >> k) & 1 if 0 <= k < count else 0
    facing = [(bit(k - 1) == bit(k)) * 1 for k in range(count + 1)]
    point = lax.axis_index("energy") * energy_count + side
    info = jnp.stack([jnp.asarray(v, jnp.int32) for v in (odd, side, point, *facing)])
    mine, yours = call(
        damping_body,
        "damping",
        1,
        [(2, 2, N)] * 2,
        (
            info,
            phonon_shift,
            slab_profile,
            coupling,
            along(occupation, 1),
            occupation,
            along(occupation, -1),
            potential_table,
        ),
        scalars=4,
    )
    theirs = pair(yours)
    kept = lax.dynamic_index_in_dim(source, side, 2, keepdims=False)
    given = pair(lax.dynamic_index_in_dim(source, 1 - side, 2, keepdims=False))

    xa, x, zn, own, other, near = call(
        first_body,
        "first",
        30,
        [(2,) + MATRIX, MATRIX, MATRIX, ENDS, ENDS, PACKED],
        (info, onsite_block, hopping_block, mine, theirs),
        work(2),
        scalars=1,
    )
    ia, own_r, other_r = call(
        first_rhs_body,
        "first_rhs",
        3,
        [(2,) + VECTOR, RHS, RHS],
        (info, xa, hopping_block, kept, given),
        scalars=1,
    )
    held = []
    for level in range(count):
        distance = 1 << level
        facing_block = swapped(near, distance)
        w, zf, ends, sides = call(
            functools.partial(rest_body, level),
            "rest",
            5,
            [VECTOR, MATRIX, ENDS, RHS],
            (info, x, zn, own, other, own_r, other_r),
            scalars=1,
        )
        held += [w, zn, zf]
        own, other = ends, swapped(ends, distance)
        own_r, other_r = sides, swapped(sides, distance)
        (x,) = call(invert_body, "invert", 12, [MATRIX], (near, facing_block), work(1))
        if level < count - 1:
            zn, near = call(
                functools.partial(near_body, level + 1),
                "near",
                3,
                [MATRIX, PACKED],
                (info, x, own, other),
                scalars=1,
            )
    prev, mid, last, sent = call(
        functools.partial(back_body, count),
        "back",
        22,
        [VECTOR, VECTOR, VECTOR, (2,) + VECTOR],
        (info, x, own, other, own_r, other_r, *held, xa, ia, hopping_block),
        [pltpu.VMEM(MATRIX, jnp.float32)] + work(1),
        scalars=1,
    )
    back = pair(sent)
    (mine,) = call(
        own_body,
        "own",
        2,
        [(2,) + VECTOR],
        (info, xa, ia, mid, hopping_block, prev, last),
        scalars=1,
    )
    return call(
        finish_body,
        "finish",
        2,
        [source.shape, occupation.shape],
        (info, mine, back),
        scalars=1,
    )


def solution(mesh):
    placed = (
        P("slab", None, "energy", None, None),
        P(),
        P(),
        P(),
        P("slab"),
        P("slab", "energy", None),
        P(),
        P(),
    )
    return jax.shard_map(
        per_device,
        mesh=mesh,
        in_specs=placed,
        out_specs=(P("slab", None, "energy", None, None), P("slab", "energy", None)),
        check_vma=False,
    )
```

```python
import functools

import jax
import jax.numpy as jnp
from jax import lax
from jax.experimental import pallas as pl
from jax.experimental.pallas import tpu as pltpu
from jax.sharding import PartitionSpec as P

broadening = 0.05
energy_low = -1.2
energy_step = 0.15
N = 192
COLS = 128
WIDE = 256
BLOCK = 32


def split(x):
    hi = x.astype(jnp.bfloat16)
    lo = (x - hi.astype(jnp.float32)).astype(jnp.bfloat16)
    return hi, lo


def tn(a, b):
    return lax.dot_general(a, b, (((0,), (0,)), ((), ())), preferred_element_type=jnp.float32)


def spread(row):
    return jnp.broadcast_to(row, (8, 128))


def solve_eight(cr, ci, now, side):
    row = lax.broadcasted_iota(jnp.int32, (8, 128), 0)
    for p in range(8):
        dr, di = spread(cr[p][p : p + 1]), spread(ci[p][p : p + 1])
        inv = 1.0 / (dr * dr + di * di)
        er, ei = dr * inv, -di * inv
        here = row == p
        wr = jnp.where(here, 1.0 - er, cr[p] * er - ci[p] * ei)
        wi = jnp.where(here, -ei, cr[p] * ei + ci[p] * er)
        for j in range(p + 1, 8):
            fr, fi = spread(cr[j][p : p + 1]), spread(ci[j][p : p + 1])
            cr[j], ci[j] = cr[j] - (wr * fr - wi * fi), ci[j] - (wr * fi + wi * fr)
        n, t = spread(now[p : p + 1]), spread(side[p : p + 1])
        now, side = now - (wr * n + wi * t), side - (wr * t - wi * n)
    return now, side


def take(x, index):
    return lax.gather(
        x,
        index[:, :, None],
        lax.GatherDimensionNumbers(
            offset_dims=(),
            collapsed_slice_dims=(1,),
            start_index_map=(1,),
            operand_batching_dims=(0,),
            start_indices_batching_dims=(0,),
        ),
        slice_sizes=(1, 1),
        mode=lax.GatherScatterMode.PROMISE_IN_BOUNDS,
    )


def small_inverse(m):
    lane = lax.broadcasted_iota(jnp.int32, (8, 128), 1)
    row = lax.broadcasted_iota(jnp.int32, (8, 128), 0)
    start = (lane // 64) * 64
    real = lane - start < 32
    off = lane - (lane // 32) * 32

    def turned(x):
        return jnp.where(real, -pltpu.roll(x, 96, 1), pltpu.roll(x, 32, 1))

    def group(g, _):
        o = pl.multiple_of(8 * g, 8)
        own = m[pl.ds(o, 8), :]
        parts = [m[8 * h : 8 * h + 8, :] for h in range(4)]
        at = [start + (o + j) for j in range(8)]
        far = [a + 32 for a in at]
        cr = [take(own, a) for a in at]
        ci = [take(own, a) for a in far]
        wide_r = [[take(x, a) for a in at] for x in parts]
        wide_i = [[take(x, a) for a in far] for x in parts]
        inside = (off >= o) & (off < o + 8)
        eye = jnp.where(real & (off - o == row), 1.0, 0.0)
        now = jnp.where(inside, eye, own)
        out, turn = solve_eight(cr, ci, now, turned(now))
        for h in range(4):
            x = jnp.where(inside, 0.0, parts[h])
            for j in range(8):
                x = x - (
                    wide_r[h][j] * spread(out[j : j + 1]) + wide_i[h][j] * spread(turn[j : j + 1])
                )
            m[8 * h : 8 * h + 8, :] = x
        m[pl.ds(o, 8), :] = out
        return 0

    lax.fori_loop(0, 4, group, 0)


def sweep(B, ar, ai, m):
    b = BLOCK
    for e in range(B):
        ar[e, :, N:] = jnp.zeros((N, WIDE - N), jnp.float32)
        ai[e, :, N:] = jnp.zeros((N, WIDE - N), jnp.float32)
    lane = lax.broadcasted_iota(jnp.int32, (b, WIDE), 1)
    row = lax.broadcasted_iota(jnp.int32, (b, WIDE), 0)
    l128 = lax.broadcasted_iota(jnp.int32, (b, 128), 1)
    r128 = lax.broadcasted_iota(jnp.int32, (b, 128), 0)
    quarter = l128 // 32

    def step(k, _):
        o = pl.multiple_of(k * b, b)
        rows = [(ar[e, pl.ds(o, b), :], ai[e, pl.ds(o, b), :]) for e in range(B)]
        q = jnp.where((lax.rem(quarter, 2) == 0) & (l128 - 32 * quarter == r128), 1.0, 0.0)
        for e in range(B):
            for part in range(2):
                turn = lax.rem(WIDE - o + 64 * e + 32 * part, WIDE)
                q = jnp.where(
                    quarter == 2 * e + part, pltpu.roll(rows[e][part], turn, 1)[:, 0:128], q
                )
        m[...] = q
        small_inverse(m)
        q = m[...]
        for e in range(B):
            rr, ri = rows[e]
            dr = q[:, 64 * e : 64 * e + 32]
            di = q[:, 64 * e + 32 : 64 * e + 64]
            inside = (lane >= o) & (lane < o + b)
            eye = lane - o == row
            r2 = jnp.where(inside, jnp.where(eye, -1.0, 0.0), rr)
            i2 = jnp.where(inside, 0.0, ri)
            drh, drl = split(dr)
            dih, dil = split(di)
            r2h, r2l = split(r2)
            i2h, i2l = split(i2)
            lhs = jnp.concatenate([drh, dih, drl, dil, drh, dih], 0)
            Rr = tn(lhs, jnp.concatenate([r2h, -i2h, r2h, -i2h, r2l, -i2l], 0))
            Ri = tn(lhs, jnp.concatenate([i2h, r2h, i2h, r2h, i2l, r2l], 0))
            Rrh, Rrl = split(Rr)
            Rih, Ril = split(Ri)
            rh, rl = split(rr)
            ih, il = split(ri)
            lhs = jnp.concatenate([rh, ih, rl, il, rh, ih], 0)[:, 0:N]
            Ur = tn(lhs, jnp.concatenate([Rrh, -Rih, Rrh, -Rih, Rrl, -Ril], 0))
            Ui = tn(lhs, jnp.concatenate([Rih, Rrh, Rih, Rrh, Ril, Rrl], 0))
            wide = lax.broadcasted_iota(jnp.int32, (N, WIDE), 1)
            strip = (wide >= o) & (wide < o + b)
            ar[e] = jnp.where(strip, 0.0, ar[e]) - Ur
            ai[e] = jnp.where(strip, 0.0, ai[e]) - Ui
            ar[e, pl.ds(o, b), :] = Rr
            ai[e, pl.ds(o, b), :] = Ri
        return 0

    lax.fori_loop(0, N // b, step, 0)


def nn(a, b):
    return jnp.dot(a, b, preferred_element_type=jnp.float32)


def nt(a, b):
    return lax.dot_general(a, b, (((1,), (1,)), ((), ())), preferred_element_type=jnp.float32)


def three(dot, a, b):
    return dot(a[0], b[0]) + (dot(a[0], b[1]) + dot(a[1], b[0]))


def csplit(x):
    return split(x[0]), split(x[1])


def cdot(dot, a, b):
    re = three(dot, a[0], b[0]) - three(dot, a[1], b[1])
    im = three(dot, a[0], b[1]) + three(dot, a[1], b[0])
    return re, im


def real_left(dot, a, b):
    return three(dot, a, b[0]), three(dot, a, b[1])


def real_right(dot, a, b):
    return three(dot, a[0], b), three(dot, a[1], b)


def put(ref, x):
    ref[0] = x[0]
    ref[1] = x[1]


def get(ref):
    return ref[0], ref[1]


def neg(x):
    return -x[0], -x[1]


def add(x, y):
    return x[0] + y[0], x[1] + y[1]


def sub(x, y):
    return x[0] - y[0], x[1] - y[1]


def pack(ref, x):
    ref[0] = x[0][:, 0:128]
    ref[1] = x[1][:, 0:128]
    ref[2] = jnp.concatenate([x[0][:, 128:N], x[1][:, 128:N]], axis=1)


def unpack(ref):
    rest = ref[2]
    return (
        jnp.concatenate([ref[0], rest[:, 0:64]], axis=1),
        jnp.concatenate([ref[1], rest[:, 64:128]], axis=1),
    )


def call(body, cost, outs, args, scratch=(), scalars=0):
    return pl.pallas_call(
        body,
        out_shape=tuple(jax.ShapeDtypeStruct(s, jnp.float32) for s in outs),
        in_specs=[pl.BlockSpec(memory_space=pltpu.SMEM)] * scalars
        + [pl.BlockSpec(memory_space=pltpu.VMEM)] * (len(args) - scalars),
        out_specs=tuple(pl.BlockSpec(memory_space=pltpu.VMEM) for _ in outs),
        scratch_shapes=list(scratch),
        cost_estimate=pl.CostEstimate(
            flops=int(cost * 1.1e9), bytes_accessed=1 << 20, transcendentals=0
        ),
    )(*args)


MATRIX = (2, N, N)
PACKED = (3, N, 128)
VECTOR = (2, N, COLS)
ENDS = (6, N, 128)
RHS = (4, N, COLS)


def work(B):
    return [pltpu.VMEM((B, N, WIDE), jnp.float32)] * 2 + [pltpu.VMEM((BLOCK, 128), jnp.float32)]


def vdot(dot, a, v):
    high, low = split(jnp.concatenate(v, axis=1))
    turn = lambda s: jnp.concatenate([-s[:, COLS:], s[:, :COLS]], axis=1)
    both = three(dot, a[0], (high, low)) + three(dot, a[1], (turn(high), turn(low)))
    return both[:, :COLS], both[:, COLS:]


def real_vdot(a, v):
    both = three(nn, a, split(jnp.concatenate(v, axis=1)))
    return both[:, :COLS], both[:, COLS:]


def choose(flag, yes, no):
    pick = jnp.full(yes[0].shape, flag, jnp.int32) == 1
    return tuple(jnp.where(pick, y, n) for y, n in zip(yes, no))


def damping_body(info, shift, profile, coupling, low, occ, high, table, mine, yours):
    for out, k in ((mine, info[1]), (yours, 1 - info[1])):
        for slab in range(2):
            total = jnp.full((1, N), broadening, jnp.float32)
            for q in range(6):
                w = jnp.float32(0.0)
                for mode in range(shift.shape[0]):
                    c = coupling[mode]
                    w = w + jnp.where(q == k + 2 + shift[mode], c, 0.0)
                    w = w + jnp.where(q == k + 2 - shift[mode], c, 0.0)
                row = (low, occ, high)[q // 2][slab, q % 2 : q % 2 + 1, :]
                total = total + w * row
            out[slab, 0:1, :] = total
            out[slab, 1:2, :] = table[pl.ds(profile[slab], 1), :]


def first_body(info, onsite, hop, mine, theirs, xa, x, zn, left, right, near, ar, ai, m):
    row = lax.broadcasted_iota(jnp.int32, (N, N), 0)
    col = lax.broadcasted_iota(jnp.int32, (N, N), 1)
    eye = row == col
    energy = energy_low + energy_step * info[2].astype(jnp.float32)

    def block(i):
        flag = info[0] if i // 2 else 1 - info[0]
        at = i % 2
        (both,) = choose(flag, (mine[at],), (theirs[at],))
        return (
            jnp.where(eye, energy - both[1:2], 0.0) - onsite[...],
            jnp.where(eye, both[0:1], 0.0),
        )

    for e in range(2):
        re, im = block(2 * e)
        ar[e, :, 0:N] = re
        ai[e, :, 0:N] = im
    sweep(2, ar, ai, m)
    h = split(hop[...])
    ht = split(hop[...].T)
    got = []
    for e in range(2):
        one = (-ar[e, :, 0:N], -ai[e, :, 0:N])
        put(xa.at[e], one)
        xs = csplit(one)
        up = csplit(real_left(nn, h, xs))
        down = csplit(real_left(nn, ht, xs))
        got.append((up, down))
    (up0, down0), (up2, down2) = got
    middle = sub(sub(block(1), real_right(nn, down0, h)), real_right(nn, up2, ht))
    pack(left.at[pl.ds(0, 3)], neg(real_right(nn, up0, h)))
    pack(left.at[pl.ds(3, 3)], neg(real_right(nn, up0, ht)))
    pack(right.at[pl.ds(0, 3)], neg(real_right(nn, down2, ht)))
    pack(right.at[pl.ds(3, 3)], sub(block(3), real_right(nn, down2, h)))
    ar[0, :, 0:N] = middle[0]
    ai[0, :, 0:N] = middle[1]
    sweep(1, ar, ai, m)
    put(x, (-ar[0, :, 0:N], -ai[0, :, 0:N]))
    near_end(info[3], get(x), left, right, zn, lambda v: pack(near, v))


def first_rhs_body(info, xa, hop, kept, other, ia, left, right):
    h = split(hop[...])
    ht = split(hop[...].T)

    def r(i):
        flag = info[0] if i // 2 else 1 - info[0]
        at = i % 2
        return choose(flag, (kept[at, 0], kept[at, 1]), (other[at, 0], other[at, 1]))

    a = vdot(nn, csplit(get(xa.at[0])), r(0))
    c = vdot(nn, csplit(get(xa.at[1])), r(2))
    put(ia.at[0], a)
    put(ia.at[1], c)
    put(left.at[pl.ds(0, 2)], add(r(1), add(real_vdot(ht, a), real_vdot(h, c))))
    put(left.at[pl.ds(2, 2)], real_vdot(h, a))
    right[0] = jnp.zeros((N, COLS), jnp.float32)
    right[1] = jnp.zeros((N, COLS), jnp.float32)
    put(right.at[pl.ds(2, 2)], add(r(3), real_vdot(ht, c)))


def invert_body(own, other, x, ar, ai, m):
    now = add(unpack(own), unpack(other))
    ar[0, :, 0:N] = now[0]
    ai[0, :, 0:N] = now[1]
    sweep(1, ar, ai, m)
    put(x, (-ar[0, :, 0:N], -ai[0, :, 0:N]))


def coupling_of(ref):
    return unpack(ref.at[pl.ds(0, 3)])


def end_block(ref):
    return unpack(ref.at[pl.ds(3, 3)])


def near_end(flag, x, own, other, zn, store):
    t = csplit(choose(flag, coupling_of(other), coupling_of(own)))
    z = cdot(nn, t, csplit(x))
    put(zn, z)
    f = choose(flag, end_block(other), end_block(own))
    store(sub(f, cdot(nt, csplit(z), t)))


def near_body(level, info, x, own, other, zn, near):
    near_end(info[3 + level], get(x), own, other, zn, lambda v: pack(near, v))


def rhs_ends(ref):
    return (ref[0], ref[1]), (ref[2], ref[3])


def rest_body(level, info, x, zn, own, other, own_r, other_r, w, zf, out, out_r):
    flag = info[3 + level]
    xs = csplit(get(x))
    zns = csplit(get(zn))
    t_near = csplit(choose(flag, coupling_of(other), coupling_of(own)))
    t_far = csplit(choose(flag, coupling_of(own), coupling_of(other)))
    mine, mine_far = rhs_ends(own_r)
    theirs, theirs_far = rhs_ends(other_r)
    r = add(mine, theirs)
    z = cdot(nn, t_far, xs)
    put(w, vdot(nn, xs, r))
    put(out_r.at[pl.ds(0, 2)], sub(choose(flag, theirs_far, mine_far), vdot(nn, zns, r)))
    put(zf, z)
    z = csplit(z)
    pack(out.at[pl.ds(0, 3)], neg(cdot(nt, z, t_near)))
    f = choose(flag, end_block(own), end_block(other))
    pack(out.at[pl.ds(3, 3)], sub(f, cdot(nt, z, t_far)))
    put(out_r.at[pl.ds(2, 2)], sub(choose(flag, mine_far, theirs_far), vdot(nn, z, r)))


def solve_pair(low, xa, ia, hop, prev, middle, last, out):
    first = choose(low, prev, middle)
    second = choose(low, middle, last)
    t = add(real_vdot(split(hop[...].T), first), real_vdot(split(hop[...]), second))
    at = 1 - low
    x = xa[at, 0], xa[at, 1]
    put(out.at[0], add((ia[at, 0], ia[at, 1]), vdot(nn, csplit(x), t)))
    put(out.at[1], second)


def back_body(count, info, x, own, other, own_r, other_r, *refs):
    levels = [refs[3 * i : 3 * i + 3] for i in range(count)]
    xa, ia, hop, prev_out, mid, last_out, out, zn, ar, ai, m = refs[3 * count :]
    flag = info[3 + count]
    xs = get(x)

    def store(v):
        ar[0, :, 0:N] = v[0]
        ai[0, :, 0:N] = v[1]

    near_end(flag, xs, own, other, zn, store)
    mine, mine_far = rhs_ends(own_r)
    theirs, theirs_far = rhs_ends(other_r)
    r = add(mine, theirs)
    w = vdot(nn, csplit(xs), r)
    rest = sub(choose(flag, theirs_far, mine_far), vdot(nn, csplit(get(zn)), r))
    sweep(1, ar, ai, m)
    end = vdot(nn, csplit((-ar[0, :, 0:N], -ai[0, :, 0:N])), rest)
    one = sub(w, vdot(tn, csplit(get(zn)), end))
    near, far = one, choose(flag, (jnp.zeros((N, COLS), jnp.float32),) * 2, end)
    for i in range(count - 1, -1, -1):
        w, z_near, z_far = levels[i]
        one = sub(
            sub(get(w), vdot(tn, csplit(get(z_near)), near)),
            vdot(tn, csplit(get(z_far)), far),
        )
        flag = info[3 + i]
        if i:
            near, far = one, choose(flag, far, near)
    prev = choose(flag, far, near)
    last = choose(flag, near, far)
    put(prev_out, prev)
    put(mid, one)
    put(last_out, last)
    solve_pair(info[0], xa, ia, hop, prev, one, last, out)


def own_body(info, xa, ia, mid, hop, prev, last, out):
    solve_pair(1 - info[0], xa, ia, hop, get(prev), get(mid), get(last), out)


def finish_body(info, mine, other, amplitude, density):
    for which, part in ((info[1], mine), (1 - info[1], other)):
        for slab in range(2):
            re, im = part[slab, 0], part[slab, 1]
            amplitude[slab, 0, which] = re
            amplitude[slab, 1, which] = im
            total = jnp.sum((re * re + im * im).T, axis=0, keepdims=True)
            density[slab, pl.ds(which, 1), :] = total


def per_device(
    source,
    onsite_block,
    hopping_block,
    potential_table,
    slab_profile,
    occupation,
    coupling,
    phonon_shift,
):
    slabs = lax.axis_size("slab")
    energy_count = occupation.shape[1]
    place = lax.axis_index("slab")
    odd = lax.rem(place, 2)
    side = (lax.rem(place, 4) // 2 + odd + 1) % 2

    def pair(array):
        return lax.ppermute(array, "slab", [(s, s ^ 1) for s in range(slabs)])

    def along(array, by):
        width = lax.axis_size("energy")
        pairs = [(e, e + by) for e in range(width) if 0 <= e + by < width]
        return lax.ppermute(array, "energy", pairs)

    def swapped(array, distance):
        spot = lambda g, chain: 2 * g + ((1 - chain) if g % 2 == 0 else chain)
        pairs = [
            (spot(g, chain), spot(g ^ distance, chain))
            for g in range(slabs // 2)
            for chain in range(2)
        ]
        return lax.ppermute(array, "slab", pairs)

    group = place // 2
    count = (slabs // 2 - 1).bit_length()
    bit = lambda k: (group >> k) & 1 if 0 <= k < count else 0
    facing = [(bit(k - 1) == bit(k)) * 1 for k in range(count + 1)]
    point = lax.axis_index("energy") * energy_count + side
    info = jnp.stack([jnp.asarray(v, jnp.int32) for v in (odd, side, point, *facing)])
    mine, yours = call(
        damping_body,
        1,
        [(2, 2, N)] * 2,
        (
            info,
            phonon_shift,
            slab_profile,
            coupling,
            along(occupation, 1),
            occupation,
            along(occupation, -1),
            potential_table,
        ),
        scalars=4,
    )
    theirs = pair(yours)
    kept = lax.dynamic_index_in_dim(source, side, 2, keepdims=False)
    given = pair(lax.dynamic_index_in_dim(source, 1 - side, 2, keepdims=False))

    xa, x, zn, own, other, near = call(
        first_body,
        30,
        [(2,) + MATRIX, MATRIX, MATRIX, ENDS, ENDS, PACKED],
        (info, onsite_block, hopping_block, mine, theirs),
        work(2),
        scalars=1,
    )
    ia, own_r, other_r = call(
        first_rhs_body,
        3,
        [(2,) + VECTOR, RHS, RHS],
        (info, xa, hopping_block, kept, given),
        scalars=1,
    )
    held = []
    for level in range(count):
        distance = 1 << level
        facing_block = swapped(near, distance)
        w, zf, ends, sides = call(
            functools.partial(rest_body, level),
            5,
            [VECTOR, MATRIX, ENDS, RHS],
            (info, x, zn, own, other, own_r, other_r),
            scalars=1,
        )
        held += [w, zn, zf]
        other = swapped(ends, distance)
        other_r = swapped(sides, distance)
        own, own_r = ends, sides
        (x,) = call(invert_body, 12, [MATRIX], (near, facing_block), work(1))
        if level < count - 1:
            zn, near = call(
                functools.partial(near_body, level + 1),
                3,
                [MATRIX, PACKED],
                (info, x, own, other),
                scalars=1,
            )
    prev, mid, last, sent = call(
        functools.partial(back_body, count),
        22,
        [VECTOR, VECTOR, VECTOR, (2,) + VECTOR],
        (info, x, own, other, own_r, other_r, *held, xa, ia, hopping_block),
        [pltpu.VMEM(MATRIX, jnp.float32)] + work(1),
        scalars=1,
    )
    back = pair(sent)
    (mine,) = call(
        own_body,
        2,
        [(2,) + VECTOR],
        (info, xa, ia, mid, hopping_block, prev, last),
        scalars=1,
    )
    return call(
        finish_body, 2, [source.shape, occupation.shape], (info, mine, back), scalars=1
    )


def solution(mesh):
    placed = (
        P("slab", None, "energy", None, None),
        P(),
        P(),
        P(),
        P("slab"),
        P("slab", "energy", None),
        P(),
        P(),
    )
    return jax.shard_map(
        per_device,
        mesh=mesh,
        in_specs=placed,
        out_specs=(P("slab", None, "energy", None, None), P("slab", "energy", None)),
        check_vma=False,
    )
```

```python
import functools

import jax
import jax.numpy as jnp
from jax import lax
from jax.experimental import pallas as pl
from jax.experimental.pallas import tpu as pltpu
from jax.sharding import PartitionSpec as P

broadening = 0.05
energy_low = -1.2
energy_step = 0.15
N = 192
COLS = 128
WIDE = 256
BLOCK = 32


def split(x):
    hi = x.astype(jnp.bfloat16)
    lo = (x - hi.astype(jnp.float32)).astype(jnp.bfloat16)
    return hi, lo


def tn(a, b):
    return lax.dot_general(a, b, (((0,), (0,)), ((), ())), preferred_element_type=jnp.float32)


def spread(row):
    return jnp.broadcast_to(row, (8, 128))


def solve_eight(cr, ci, now, side):
    row = lax.broadcasted_iota(jnp.int32, (8, 128), 0)
    for p in range(8):
        dr, di = spread(cr[p][p : p + 1]), spread(ci[p][p : p + 1])
        inv = 1.0 / (dr * dr + di * di)
        er, ei = dr * inv, -di * inv
        here = row == p
        wr = jnp.where(here, 1.0 - er, cr[p] * er - ci[p] * ei)
        wi = jnp.where(here, -ei, cr[p] * ei + ci[p] * er)
        for j in range(p + 1, 8):
            fr, fi = spread(cr[j][p : p + 1]), spread(ci[j][p : p + 1])
            cr[j], ci[j] = cr[j] - (wr * fr - wi * fi), ci[j] - (wr * fi + wi * fr)
        n, t = spread(now[p : p + 1]), spread(side[p : p + 1])
        now, side = now - (wr * n + wi * t), side - (wr * t - wi * n)
    return now, side


def take(x, index):
    return lax.gather(
        x,
        index[:, :, None],
        lax.GatherDimensionNumbers(
            offset_dims=(),
            collapsed_slice_dims=(1,),
            start_index_map=(1,),
            operand_batching_dims=(0,),
            start_indices_batching_dims=(0,),
        ),
        slice_sizes=(1, 1),
        mode=lax.GatherScatterMode.PROMISE_IN_BOUNDS,
    )


def small_inverse(m):
    lane = lax.broadcasted_iota(jnp.int32, (8, 128), 1)
    row = lax.broadcasted_iota(jnp.int32, (8, 128), 0)
    start = (lane // 64) * 64
    real = lane - start < 32
    off = lane - (lane // 32) * 32

    def turned(x):
        return jnp.where(real, -pltpu.roll(x, 96, 1), pltpu.roll(x, 32, 1))

    def group(g, _):
        o = pl.multiple_of(8 * g, 8)
        own = m[pl.ds(o, 8), :]
        parts = [m[8 * h : 8 * h + 8, :] for h in range(4)]
        at = [start + (o + j) for j in range(8)]
        far = [a + 32 for a in at]
        cr = [take(own, a) for a in at]
        ci = [take(own, a) for a in far]
        wide_r = [[take(x, a) for a in at] for x in parts]
        wide_i = [[take(x, a) for a in far] for x in parts]
        inside = (off >= o) & (off < o + 8)
        eye = jnp.where(real & (off - o == row), 1.0, 0.0)
        now = jnp.where(inside, eye, own)
        out, turn = solve_eight(cr, ci, now, turned(now))
        for h in range(4):
            x = jnp.where(inside, 0.0, parts[h])
            for j in range(8):
                x = x - (
                    wide_r[h][j] * spread(out[j : j + 1]) + wide_i[h][j] * spread(turn[j : j + 1])
                )
            m[8 * h : 8 * h + 8, :] = x
        m[pl.ds(o, 8), :] = out
        return 0

    lax.fori_loop(0, 4, group, 0)


def sweep(B, ar, ai, m):
    b = BLOCK
    for e in range(B):
        ar[e, :, N:] = jnp.zeros((N, WIDE - N), jnp.float32)
        ai[e, :, N:] = jnp.zeros((N, WIDE - N), jnp.float32)
    lane = lax.broadcasted_iota(jnp.int32, (b, WIDE), 1)
    row = lax.broadcasted_iota(jnp.int32, (b, WIDE), 0)
    l128 = lax.broadcasted_iota(jnp.int32, (b, 128), 1)
    r128 = lax.broadcasted_iota(jnp.int32, (b, 128), 0)
    quarter = l128 // 32

    def step(k, _):
        o = pl.multiple_of(k * b, b)
        rows = [(ar[e, pl.ds(o, b), :], ai[e, pl.ds(o, b), :]) for e in range(B)]
        q = jnp.where((lax.rem(quarter, 2) == 0) & (l128 - 32 * quarter == r128), 1.0, 0.0)
        for e in range(B):
            for part in range(2):
                turn = lax.rem(WIDE - o + 64 * e + 32 * part, WIDE)
                q = jnp.where(
                    quarter == 2 * e + part, pltpu.roll(rows[e][part], turn, 1)[:, 0:128], q
                )
        m[...] = q
        small_inverse(m)
        q = m[...]
        for e in range(B):
            rr, ri = rows[e]
            dr = q[:, 64 * e : 64 * e + 32]
            di = q[:, 64 * e + 32 : 64 * e + 64]
            inside = (lane >= o) & (lane < o + b)
            eye = lane - o == row
            r2 = jnp.where(inside, jnp.where(eye, -1.0, 0.0), rr)
            i2 = jnp.where(inside, 0.0, ri)
            drh, drl = split(dr)
            dih, dil = split(di)
            r2h, r2l = split(r2)
            i2h, i2l = split(i2)
            lhs = jnp.concatenate([drh, dih, drl, dil, drh, dih], 0)
            Rr = tn(lhs, jnp.concatenate([r2h, -i2h, r2h, -i2h, r2l, -i2l], 0))
            Ri = tn(lhs, jnp.concatenate([i2h, r2h, i2h, r2h, i2l, r2l], 0))
            Rrh, Rrl = split(Rr)
            Rih, Ril = split(Ri)
            rh, rl = split(rr)
            ih, il = split(ri)
            lhs = jnp.concatenate([rh, ih, rl, il, rh, ih], 0)[:, 0:N]
            Ur = tn(lhs, jnp.concatenate([Rrh, -Rih, Rrh, -Rih, Rrl, -Ril], 0))
            Ui = tn(lhs, jnp.concatenate([Rih, Rrh, Rih, Rrh, Ril, Rrl], 0))
            wide = lax.broadcasted_iota(jnp.int32, (N, WIDE), 1)
            strip = (wide >= o) & (wide < o + b)
            ar[e] = jnp.where(strip, 0.0, ar[e]) - Ur
            ai[e] = jnp.where(strip, 0.0, ai[e]) - Ui
            ar[e, pl.ds(o, b), :] = Rr
            ai[e, pl.ds(o, b), :] = Ri
        return 0

    lax.fori_loop(0, N // b, step, 0)


def nn(a, b):
    return jnp.dot(a, b, preferred_element_type=jnp.float32)


def nt(a, b):
    return lax.dot_general(a, b, (((1,), (1,)), ((), ())), preferred_element_type=jnp.float32)


def three(dot, a, b):
    return dot(a[0], b[0]) + (dot(a[0], b[1]) + dot(a[1], b[0]))


def csplit(x):
    return split(x[0]), split(x[1])


def cdot(dot, a, b):
    re = three(dot, a[0], b[0]) - three(dot, a[1], b[1])
    im = three(dot, a[0], b[1]) + three(dot, a[1], b[0])
    return re, im


def real_left(dot, a, b):
    return three(dot, a, b[0]), three(dot, a, b[1])


def real_right(dot, a, b):
    return three(dot, a[0], b), three(dot, a[1], b)


def put(ref, x):
    ref[0] = x[0]
    ref[1] = x[1]


def get(ref):
    return ref[0], ref[1]


def neg(x):
    return -x[0], -x[1]


def add(x, y):
    return x[0] + y[0], x[1] + y[1]


def sub(x, y):
    return x[0] - y[0], x[1] - y[1]


def pack(ref, x):
    ref[0] = x[0][:, 0:128]
    ref[1] = x[1][:, 0:128]
    ref[2] = jnp.concatenate([x[0][:, 128:N], x[1][:, 128:N]], axis=1)


def unpack(ref):
    rest = ref[2]
    return (
        jnp.concatenate([ref[0], rest[:, 0:64]], axis=1),
        jnp.concatenate([ref[1], rest[:, 64:128]], axis=1),
    )


def call(body, cost, outs, args, scratch=(), scalars=0):
    return pl.pallas_call(
        body,
        out_shape=tuple(jax.ShapeDtypeStruct(s, jnp.float32) for s in outs),
        in_specs=[pl.BlockSpec(memory_space=pltpu.SMEM)] * scalars
        + [pl.BlockSpec(memory_space=pltpu.VMEM)] * (len(args) - scalars),
        out_specs=tuple(pl.BlockSpec(memory_space=pltpu.VMEM) for _ in outs),
        scratch_shapes=list(scratch),
        compiler_params=pltpu.CompilerParams(vmem_limit_bytes=24 * 1024 * 1024),
        cost_estimate=pl.CostEstimate(
            flops=int(cost * 1.1e9), bytes_accessed=1 << 20, transcendentals=0
        ),
    )(*args)


MATRIX = (2, N, N)
PACKED = (3, N, 128)
VECTOR = (2, N, COLS)
ENDS = (6, N, 128)
RHS = (4, N, COLS)


def work(B):
    return [pltpu.VMEM((B, N, WIDE), jnp.float32)] * 2 + [pltpu.VMEM((BLOCK, 128), jnp.float32)]


def vdot(dot, a, v):
    high, low = split(jnp.concatenate(v, axis=1))
    turn = lambda s: jnp.concatenate([-s[:, COLS:], s[:, :COLS]], axis=1)
    both = three(dot, a[0], (high, low)) + three(dot, a[1], (turn(high), turn(low)))
    return both[:, :COLS], both[:, COLS:]


def real_vdot(a, v):
    both = three(nn, a, split(jnp.concatenate(v, axis=1)))
    return both[:, :COLS], both[:, COLS:]


def choose(flag, yes, no):
    pick = jnp.full(yes[0].shape, flag, jnp.int32) == 1
    return tuple(jnp.where(pick, y, n) for y, n in zip(yes, no))


def damping_body(info, shift, profile, coupling, low, occ, high, table, mine, yours):
    for out, k in ((mine, info[1]), (yours, 1 - info[1])):
        for slab in range(2):
            total = jnp.full((1, N), broadening, jnp.float32)
            for q in range(6):
                w = jnp.float32(0.0)
                for mode in range(shift.shape[0]):
                    c = coupling[mode]
                    w = w + jnp.where(q == k + 2 + shift[mode], c, 0.0)
                    w = w + jnp.where(q == k + 2 - shift[mode], c, 0.0)
                row = (low, occ, high)[q // 2][slab, q % 2 : q % 2 + 1, :]
                total = total + w * row
            out[slab, 0:1, :] = total
            out[slab, 1:2, :] = table[pl.ds(profile[slab], 1), :]


def first_body(info, onsite, hop, mine, theirs, xa, x, zn, left, right, near, ar, ai, m):
    row = lax.broadcasted_iota(jnp.int32, (N, N), 0)
    col = lax.broadcasted_iota(jnp.int32, (N, N), 1)
    eye = row == col
    energy = energy_low + energy_step * info[2].astype(jnp.float32)

    def block(i):
        flag = info[0] if i // 2 else 1 - info[0]
        at = i % 2
        (both,) = choose(flag, (mine[at],), (theirs[at],))
        return (
            jnp.where(eye, energy - both[1:2], 0.0) - onsite[...],
            jnp.where(eye, both[0:1], 0.0),
        )

    for e in range(2):
        re, im = block(2 * e)
        ar[e, :, 0:N] = re
        ai[e, :, 0:N] = im
    sweep(2, ar, ai, m)
    h = split(hop[...])
    ht = split(hop[...].T)
    got = []
    for e in range(2):
        one = (-ar[e, :, 0:N], -ai[e, :, 0:N])
        put(xa.at[e], one)
        xs = csplit(one)
        up = csplit(real_left(nn, h, xs))
        down = csplit(real_left(nn, ht, xs))
        got.append((up, down))
    (up0, down0), (up2, down2) = got
    middle = sub(sub(block(1), real_right(nn, down0, h)), real_right(nn, up2, ht))
    pack(left.at[pl.ds(0, 3)], neg(real_right(nn, up0, h)))
    pack(left.at[pl.ds(3, 3)], neg(real_right(nn, up0, ht)))
    pack(right.at[pl.ds(0, 3)], neg(real_right(nn, down2, ht)))
    pack(right.at[pl.ds(3, 3)], sub(block(3), real_right(nn, down2, h)))
    ar[0, :, 0:N] = middle[0]
    ai[0, :, 0:N] = middle[1]
    sweep(1, ar, ai, m)
    put(x, (-ar[0, :, 0:N], -ai[0, :, 0:N]))
    near_end(info[3], get(x), left, right, zn, lambda v: pack(near, v))


def first_rhs_body(info, xa, hop, kept, other, ia, left, right):
    h = split(hop[...])
    ht = split(hop[...].T)

    def r(i):
        flag = info[0] if i // 2 else 1 - info[0]
        at = i % 2
        return choose(flag, (kept[at, 0], kept[at, 1]), (other[at, 0], other[at, 1]))

    a = vdot(nn, csplit(get(xa.at[0])), r(0))
    c = vdot(nn, csplit(get(xa.at[1])), r(2))
    put(ia.at[0], a)
    put(ia.at[1], c)
    put(left.at[pl.ds(0, 2)], add(r(1), add(real_vdot(ht, a), real_vdot(h, c))))
    put(left.at[pl.ds(2, 2)], real_vdot(h, a))
    right[0] = jnp.zeros((N, COLS), jnp.float32)
    right[1] = jnp.zeros((N, COLS), jnp.float32)
    put(right.at[pl.ds(2, 2)], add(r(3), real_vdot(ht, c)))


def invert_body(own, other, x, ar, ai, m):
    now = add(unpack(own), unpack(other))
    ar[0, :, 0:N] = now[0]
    ai[0, :, 0:N] = now[1]
    sweep(1, ar, ai, m)
    put(x, (-ar[0, :, 0:N], -ai[0, :, 0:N]))


def coupling_of(ref):
    return unpack(ref.at[pl.ds(0, 3)])


def end_block(ref):
    return unpack(ref.at[pl.ds(3, 3)])


def near_end(flag, x, own, other, zn, store):
    t = csplit(choose(flag, coupling_of(other), coupling_of(own)))
    z = cdot(nn, t, csplit(x))
    put(zn, z)
    f = choose(flag, end_block(other), end_block(own))
    store(sub(f, cdot(nt, csplit(z), t)))


def near_body(level, info, x, own, other, zn, near):
    near_end(info[3 + level], get(x), own, other, zn, lambda v: pack(near, v))


def rhs_ends(ref):
    return (ref[0], ref[1]), (ref[2], ref[3])


def rest_body(level, info, x, zn, own, other, own_r, other_r, w, zf, out, out_r):
    flag = info[3 + level]
    xs = csplit(get(x))
    zns = csplit(get(zn))
    t_near = csplit(choose(flag, coupling_of(other), coupling_of(own)))
    t_far = csplit(choose(flag, coupling_of(own), coupling_of(other)))
    mine, mine_far = rhs_ends(own_r)
    theirs, theirs_far = rhs_ends(other_r)
    r = add(mine, theirs)
    z = cdot(nn, t_far, xs)
    put(w, vdot(nn, xs, r))
    put(out_r.at[pl.ds(0, 2)], sub(choose(flag, theirs_far, mine_far), vdot(nn, zns, r)))
    put(zf, z)
    z = csplit(z)
    pack(out.at[pl.ds(0, 3)], neg(cdot(nt, z, t_near)))
    f = choose(flag, end_block(own), end_block(other))
    pack(out.at[pl.ds(3, 3)], sub(f, cdot(nt, z, t_far)))
    put(out_r.at[pl.ds(2, 2)], sub(choose(flag, mine_far, theirs_far), vdot(nn, z, r)))


def solve_pair(low, xa, ia, hop, prev, middle, last, out):
    first = choose(low, prev, middle)
    second = choose(low, middle, last)
    t = add(real_vdot(split(hop[...].T), first), real_vdot(split(hop[...]), second))
    at = 1 - low
    x = xa[at, 0], xa[at, 1]
    put(out.at[0], add((ia[at, 0], ia[at, 1]), vdot(nn, csplit(x), t)))
    put(out.at[1], second)


def last_body(level, info, x, own, other, zn, end, ar, ai, m):
    def store(v):
        ar[0, :, 0:N] = v[0]
        ai[0, :, 0:N] = v[1]

    near_end(info[3 + level], get(x), own, other, zn, store)
    sweep(1, ar, ai, m)
    put(end, (-ar[0, :, 0:N], -ai[0, :, 0:N]))


def back_body(count, info, x, zn, end, own_r, other_r, *refs):
    levels = [refs[3 * i : 3 * i + 3] for i in range(count)]
    xa, ia, hop, prev_out, mid, last_out, out = refs[3 * count :]
    flag = info[3 + count]
    mine, mine_far = rhs_ends(own_r)
    theirs, theirs_far = rhs_ends(other_r)
    r = add(mine, theirs)
    zns = csplit(get(zn))
    w = vdot(nn, csplit(get(x)), r)
    rest = sub(choose(flag, theirs_far, mine_far), vdot(nn, zns, r))
    end = vdot(nn, csplit(get(end)), rest)
    one = sub(w, vdot(tn, zns, end))
    near, far = one, choose(flag, (jnp.zeros((N, COLS), jnp.float32),) * 2, end)
    for i in range(count - 1, -1, -1):
        w, z_near, z_far = levels[i]
        one = sub(
            sub(get(w), vdot(tn, csplit(get(z_near)), near)),
            vdot(tn, csplit(get(z_far)), far),
        )
        flag = info[3 + i]
        if i:
            near, far = one, choose(flag, far, near)
    prev = choose(flag, far, near)
    last = choose(flag, near, far)
    put(prev_out, prev)
    put(mid, one)
    put(last_out, last)
    solve_pair(info[0], xa, ia, hop, prev, one, last, out)


def own_body(info, xa, ia, mid, hop, prev, last, out):
    solve_pair(1 - info[0], xa, ia, hop, get(prev), get(mid), get(last), out)


def finish_body(info, mine, other, amplitude, density):
    for which, part in ((info[1], mine), (1 - info[1], other)):
        for slab in range(2):
            re, im = part[slab, 0], part[slab, 1]
            amplitude[slab, 0, which] = re
            amplitude[slab, 1, which] = im
            total = jnp.sum((re * re + im * im).T, axis=0, keepdims=True)
            density[slab, pl.ds(which, 1), :] = total


def per_device(
    source,
    onsite_block,
    hopping_block,
    potential_table,
    slab_profile,
    occupation,
    coupling,
    phonon_shift,
):
    slabs = lax.axis_size("slab")
    energy_count = occupation.shape[1]
    place = lax.axis_index("slab")
    odd = lax.rem(place, 2)
    side = (lax.rem(place, 4) // 2 + odd + 1) % 2

    def pair(array):
        return lax.ppermute(array, "slab", [(s, s ^ 1) for s in range(slabs)])

    def along(array, by):
        width = lax.axis_size("energy")
        pairs = [(e, e + by) for e in range(width) if 0 <= e + by < width]
        return lax.ppermute(array, "energy", pairs)

    def swapped(array, distance):
        spot = lambda g, chain: 2 * g + ((1 - chain) if g % 2 == 0 else chain)
        pairs = [
            (spot(g, chain), spot(g ^ distance, chain))
            for g in range(slabs // 2)
            for chain in range(2)
        ]
        return lax.ppermute(array, "slab", pairs)

    group = place // 2
    count = (slabs // 2 - 1).bit_length()
    bit = lambda k: (group >> k) & 1 if 0 <= k < count else 0
    facing = [(bit(k - 1) == bit(k)) * 1 for k in range(count + 1)]
    point = lax.axis_index("energy") * energy_count + side
    info = jnp.stack([jnp.asarray(v, jnp.int32) for v in (odd, side, point, *facing)])
    mine, yours = call(
        damping_body,
        1,
        [(2, 2, N)] * 2,
        (
            info,
            phonon_shift,
            slab_profile,
            coupling,
            along(occupation, 1),
            occupation,
            along(occupation, -1),
            potential_table,
        ),
        scalars=4,
    )
    theirs = pair(yours)
    kept = lax.dynamic_index_in_dim(source, side, 2, keepdims=False)
    given = pair(lax.dynamic_index_in_dim(source, 1 - side, 2, keepdims=False))

    xa, x, zn, own, other, near = call(
        first_body,
        30,
        [(2,) + MATRIX, MATRIX, MATRIX, ENDS, ENDS, PACKED],
        (info, onsite_block, hopping_block, mine, theirs),
        work(2),
        scalars=1,
    )
    ia, own_r, other_r = call(
        first_rhs_body,
        3,
        [(2,) + VECTOR, RHS, RHS],
        (info, xa, hopping_block, kept, given),
        scalars=1,
    )
    held = []
    for level in range(count):
        distance = 1 << level
        facing_block = swapped(near, distance)
        w, zf, ends, sides = call(
            functools.partial(rest_body, level),
            5,
            [VECTOR, MATRIX, ENDS, RHS],
            (info, x, zn, own, other, own_r, other_r),
            scalars=1,
        )
        held += [w, zn, zf]
        other = swapped(ends, distance)
        other_r = swapped(sides, distance)
        own, own_r = ends, sides
        (x,) = call(invert_body, 12, [MATRIX], (near, facing_block), work(1))
        if level < count - 1:
            zn, near = call(
                functools.partial(near_body, level + 1),
                3,
                [MATRIX, PACKED],
                (info, x, own, other),
                scalars=1,
            )
    zn, end = call(
        functools.partial(last_body, count),
        15,
        [MATRIX, MATRIX],
        (info, x, own, other),
        work(1),
        scalars=1,
    )
    prev, mid, last, sent = call(
        functools.partial(back_body, count),
        7,
        [VECTOR, VECTOR, VECTOR, (2,) + VECTOR],
        (info, x, zn, end, own_r, other_r, *held, xa, ia, hopping_block),
        scalars=1,
    )
    back = pair(sent)
    (mine,) = call(
        own_body,
        2,
        [(2,) + VECTOR],
        (info, xa, ia, mid, hopping_block, prev, last),
        scalars=1,
    )
    return call(
        finish_body, 2, [source.shape, occupation.shape], (info, mine, back), scalars=1
    )


def solution(mesh):
    placed = (
        P("slab", None, "energy", None, None),
        P(),
        P(),
        P(),
        P("slab"),
        P("slab", "energy", None),
        P(),
        P(),
    )
    return jax.shard_map(
        per_device,
        mesh=mesh,
        in_specs=placed,
        out_specs=(P("slab", None, "energy", None, None), P("slab", "energy", None)),
        check_vma=False,
    )
```

```python
import functools

import jax
import jax.numpy as jnp
from jax import lax
from jax.experimental import pallas as pl
from jax.experimental.pallas import tpu as pltpu
from jax.sharding import PartitionSpec as P

broadening = 0.05
energy_low = -1.2
energy_step = 0.15
N = 192
COLS = 128
WIDE = 256
BLOCK = 32


def split(x):
    hi = x.astype(jnp.bfloat16)
    lo = (x - hi.astype(jnp.float32)).astype(jnp.bfloat16)
    return hi, lo


def tn(a, b):
    return lax.dot_general(a, b, (((0,), (0,)), ((), ())), preferred_element_type=jnp.float32)


def spread(row):
    return jnp.broadcast_to(row, (8, 128))


def solve_eight(cr, ci, now, side):
    row = lax.broadcasted_iota(jnp.int32, (8, 128), 0)
    for p in range(8):
        dr, di = spread(cr[p][p : p + 1]), spread(ci[p][p : p + 1])
        inv = 1.0 / (dr * dr + di * di)
        er, ei = dr * inv, -di * inv
        here = row == p
        wr = jnp.where(here, 1.0 - er, cr[p] * er - ci[p] * ei)
        wi = jnp.where(here, -ei, cr[p] * ei + ci[p] * er)
        for j in range(p + 1, 8):
            fr, fi = spread(cr[j][p : p + 1]), spread(ci[j][p : p + 1])
            cr[j], ci[j] = cr[j] - (wr * fr - wi * fi), ci[j] - (wr * fi + wi * fr)
        n, t = spread(now[p : p + 1]), spread(side[p : p + 1])
        now, side = now - (wr * n + wi * t), side - (wr * t - wi * n)
    return now, side


def take(x, index):
    return lax.gather(
        x,
        index[:, :, None],
        lax.GatherDimensionNumbers(
            offset_dims=(),
            collapsed_slice_dims=(1,),
            start_index_map=(1,),
            operand_batching_dims=(0,),
            start_indices_batching_dims=(0,),
        ),
        slice_sizes=(1, 1),
        mode=lax.GatherScatterMode.PROMISE_IN_BOUNDS,
    )


def small_inverse(m):
    lane = lax.broadcasted_iota(jnp.int32, (8, 128), 1)
    row = lax.broadcasted_iota(jnp.int32, (8, 128), 0)
    start = (lane // 64) * 64
    real = lane - start < 32
    off = lane - (lane // 32) * 32

    def turned(x):
        return jnp.where(real, -pltpu.roll(x, 96, 1), pltpu.roll(x, 32, 1))

    def group(g, _):
        o = 8 * g
        own = m[0:8, :]
        parts = [m[8 * h : 8 * h + 8, :] for h in range(1, 4)]
        at = [start + (o + j) for j in range(8)]
        far = [a + 32 for a in at]
        cr = [take(own, a) for a in at]
        ci = [take(own, a) for a in far]
        wide_r = [[take(x, a) for a in at] for x in parts]
        wide_i = [[take(x, a) for a in far] for x in parts]
        inside = (off >= o) & (off < o + 8)
        eye = jnp.where(real & (off - o == row), 1.0, 0.0)
        now = jnp.where(inside, eye, own)
        out, turn = solve_eight(cr, ci, now, turned(now))
        for h in range(3):
            x = jnp.where(inside, 0.0, parts[h])
            for j in range(8):
                x = x - (
                    wide_r[h][j] * spread(out[j : j + 1]) + wide_i[h][j] * spread(turn[j : j + 1])
                )
            m[8 * h : 8 * h + 8, :] = x
        m[24:32, :] = out
        return 0

    lax.fori_loop(0, 4, group, 0)


def sweep(B, ar, ai, m):
    b = BLOCK
    for e in range(B):
        ar[e, :, N:] = jnp.zeros((N, WIDE - N), jnp.float32)
        ai[e, :, N:] = jnp.zeros((N, WIDE - N), jnp.float32)
    lane = lax.broadcasted_iota(jnp.int32, (b, WIDE), 1)
    row = lax.broadcasted_iota(jnp.int32, (b, WIDE), 0)
    l128 = lax.broadcasted_iota(jnp.int32, (b, 128), 1)
    r128 = lax.broadcasted_iota(jnp.int32, (b, 128), 0)
    quarter = l128 // 32

    def step(k, _):
        o = pl.multiple_of(k * b, b)
        rows = [(ar[e, pl.ds(o, b), :], ai[e, pl.ds(o, b), :]) for e in range(B)]
        q = jnp.where((lax.rem(quarter, 2) == 0) & (l128 - 32 * quarter == r128), 1.0, 0.0)
        for e in range(B):
            for part in range(2):
                turn = lax.rem(WIDE - o + 64 * e + 32 * part, WIDE)
                q = jnp.where(
                    quarter == 2 * e + part, pltpu.roll(rows[e][part], turn, 1)[:, 0:128], q
                )
        m[...] = q
        small_inverse(m)
        q = m[...]
        for e in range(B):
            rr, ri = rows[e]
            dr = q[:, 64 * e : 64 * e + 32]
            di = q[:, 64 * e + 32 : 64 * e + 64]
            inside = (lane >= o) & (lane < o + b)
            eye = lane - o == row
            r2 = jnp.where(inside, jnp.where(eye, -1.0, 0.0), rr)
            i2 = jnp.where(inside, 0.0, ri)
            drh, drl = split(dr)
            dih, dil = split(di)
            r2h, r2l = split(r2)
            i2h, i2l = split(i2)
            lhs = jnp.concatenate([drh, dih, drl, dil, drh, dih], 0)
            Rr = tn(lhs, jnp.concatenate([r2h, -i2h, r2h, -i2h, r2l, -i2l], 0))
            Ri = tn(lhs, jnp.concatenate([i2h, r2h, i2h, r2h, i2l, r2l], 0))
            Rrh, Rrl = split(Rr)
            Rih, Ril = split(Ri)
            rh, rl = split(rr)
            ih, il = split(ri)
            lhs = jnp.concatenate([rh, ih, rl, il, rh, ih], 0)[:, 0:N]
            Ur = tn(lhs, jnp.concatenate([Rrh, -Rih, Rrh, -Rih, Rrl, -Ril], 0))
            Ui = tn(lhs, jnp.concatenate([Rih, Rrh, Rih, Rrh, Ril, Rrl], 0))
            wide = lax.broadcasted_iota(jnp.int32, (N, WIDE), 1)
            strip = (wide >= o) & (wide < o + b)
            ar[e] = jnp.where(strip, 0.0, ar[e]) - Ur
            ai[e] = jnp.where(strip, 0.0, ai[e]) - Ui
            ar[e, pl.ds(o, b), :] = Rr
            ai[e, pl.ds(o, b), :] = Ri
        return 0

    lax.fori_loop(0, N // b, step, 0)


def nn(a, b):
    return jnp.dot(a, b, preferred_element_type=jnp.float32)


def nt(a, b):
    return lax.dot_general(a, b, (((1,), (1,)), ((), ())), preferred_element_type=jnp.float32)


def three(dot, a, b):
    return dot(a[0], b[0]) + (dot(a[0], b[1]) + dot(a[1], b[0]))


def csplit(x):
    return split(x[0]), split(x[1])


def cdot(dot, a, b):
    re = three(dot, a[0], b[0]) - three(dot, a[1], b[1])
    im = three(dot, a[0], b[1]) + three(dot, a[1], b[0])
    return re, im


def real_left(dot, a, b):
    return three(dot, a, b[0]), three(dot, a, b[1])


def real_right(dot, a, b):
    return three(dot, a[0], b), three(dot, a[1], b)


def put(ref, x):
    ref[0] = x[0]
    ref[1] = x[1]


def get(ref):
    return ref[0], ref[1]


def neg(x):
    return -x[0], -x[1]


def add(x, y):
    return x[0] + y[0], x[1] + y[1]


def sub(x, y):
    return x[0] - y[0], x[1] - y[1]


def pack(ref, x):
    ref[0] = x[0][:, 0:128]
    ref[1] = x[1][:, 0:128]
    ref[2] = jnp.concatenate([x[0][:, 128:N], x[1][:, 128:N]], axis=1)


def unpack(ref):
    rest = ref[2]
    return (
        jnp.concatenate([ref[0], rest[:, 0:64]], axis=1),
        jnp.concatenate([ref[1], rest[:, 64:128]], axis=1),
    )


def call(body, cost, outs, args, scratch=(), scalars=0):
    return pl.pallas_call(
        body,
        out_shape=tuple(jax.ShapeDtypeStruct(s, jnp.float32) for s in outs),
        in_specs=[pl.BlockSpec(memory_space=pltpu.SMEM)] * scalars
        + [pl.BlockSpec(memory_space=pltpu.VMEM)] * (len(args) - scalars),
        out_specs=tuple(pl.BlockSpec(memory_space=pltpu.VMEM) for _ in outs),
        scratch_shapes=list(scratch),
        compiler_params=pltpu.CompilerParams(vmem_limit_bytes=24 * 1024 * 1024),
        cost_estimate=pl.CostEstimate(
            flops=int(cost * 1.1e9), bytes_accessed=1 << 20, transcendentals=0
        ),
    )(*args)


MATRIX = (2, N, N)
PACKED = (3, N, 128)
VECTOR = (2, N, COLS)
ENDS = (6, N, 128)
RHS = (4, N, COLS)


def work(B):
    return [pltpu.VMEM((B, N, WIDE), jnp.float32)] * 2 + [pltpu.VMEM((BLOCK, 128), jnp.float32)]


def vdot(dot, a, v):
    high, low = split(jnp.concatenate(v, axis=1))
    turn = lambda s: jnp.concatenate([-s[:, COLS:], s[:, :COLS]], axis=1)
    both = three(dot, a[0], (high, low)) + three(dot, a[1], (turn(high), turn(low)))
    return both[:, :COLS], both[:, COLS:]


def real_vdot(a, v):
    both = three(nn, a, split(jnp.concatenate(v, axis=1)))
    return both[:, :COLS], both[:, COLS:]


def choose(flag, yes, no):
    pick = jnp.full(yes[0].shape, flag, jnp.int32) == 1
    return tuple(jnp.where(pick, y, n) for y, n in zip(yes, no))


def damping_body(info, shift, profile, coupling, low, occ, high, table, mine, yours):
    for out, k in ((mine, info[1]), (yours, 1 - info[1])):
        for slab in range(2):
            total = jnp.full((1, N), broadening, jnp.float32)
            for q in range(6):
                w = jnp.float32(0.0)
                for mode in range(shift.shape[0]):
                    c = coupling[mode]
                    w = w + jnp.where(q == k + 2 + shift[mode], c, 0.0)
                    w = w + jnp.where(q == k + 2 - shift[mode], c, 0.0)
                row = (low, occ, high)[q // 2][slab, q % 2 : q % 2 + 1, :]
                total = total + w * row
            out[slab, 0:1, :] = total
            out[slab, 1:2, :] = table[pl.ds(profile[slab], 1), :]


def first_body(info, onsite, hop, mine, theirs, xa, x, zn, left, right, near, ar, ai, m):
    row = lax.broadcasted_iota(jnp.int32, (N, N), 0)
    col = lax.broadcasted_iota(jnp.int32, (N, N), 1)
    eye = row == col
    energy = energy_low + energy_step * info[2].astype(jnp.float32)

    def block(i):
        flag = info[0] if i // 2 else 1 - info[0]
        at = i % 2
        (both,) = choose(flag, (mine[at],), (theirs[at],))
        return (
            jnp.where(eye, energy - both[1:2], 0.0) - onsite[...],
            jnp.where(eye, both[0:1], 0.0),
        )

    for e in range(2):
        re, im = block(2 * e)
        ar[e, :, 0:N] = re
        ai[e, :, 0:N] = im
    sweep(2, ar, ai, m)
    h = split(hop[...])
    ht = split(hop[...].T)
    got = []
    for e in range(2):
        one = (-ar[e, :, 0:N], -ai[e, :, 0:N])
        put(xa.at[e], one)
        xs = csplit(one)
        up = csplit(real_left(nn, h, xs))
        down = csplit(real_left(nn, ht, xs))
        got.append((up, down))
    (up0, down0), (up2, down2) = got
    middle = sub(sub(block(1), real_right(nn, down0, h)), real_right(nn, up2, ht))
    pack(left.at[pl.ds(0, 3)], neg(real_right(nn, up0, h)))
    pack(left.at[pl.ds(3, 3)], neg(real_right(nn, up0, ht)))
    pack(right.at[pl.ds(0, 3)], neg(real_right(nn, down2, ht)))
    pack(right.at[pl.ds(3, 3)], sub(block(3), real_right(nn, down2, h)))
    ar[0, :, 0:N] = middle[0]
    ai[0, :, 0:N] = middle[1]
    sweep(1, ar, ai, m)
    put(x, (-ar[0, :, 0:N], -ai[0, :, 0:N]))
    near_end(info[3], get(x), left, right, zn, lambda v: pack(near, v))


def first_rhs_body(info, xa, hop, kept, other, ia, left, right):
    h = split(hop[...])
    ht = split(hop[...].T)

    def r(i):
        flag = info[0] if i // 2 else 1 - info[0]
        at = i % 2
        return choose(flag, (kept[at, 0], kept[at, 1]), (other[at, 0], other[at, 1]))

    a = vdot(nn, csplit(get(xa.at[0])), r(0))
    c = vdot(nn, csplit(get(xa.at[1])), r(2))
    put(ia.at[0], a)
    put(ia.at[1], c)
    put(left.at[pl.ds(0, 2)], add(r(1), add(real_vdot(ht, a), real_vdot(h, c))))
    put(left.at[pl.ds(2, 2)], real_vdot(h, a))
    right[0] = jnp.zeros((N, COLS), jnp.float32)
    right[1] = jnp.zeros((N, COLS), jnp.float32)
    put(right.at[pl.ds(2, 2)], add(r(3), real_vdot(ht, c)))


def invert_body(own, other, x, ar, ai, m):
    now = add(unpack(own), unpack(other))
    ar[0, :, 0:N] = now[0]
    ai[0, :, 0:N] = now[1]
    sweep(1, ar, ai, m)
    put(x, (-ar[0, :, 0:N], -ai[0, :, 0:N]))


def coupling_of(ref):
    return unpack(ref.at[pl.ds(0, 3)])


def end_block(ref):
    return unpack(ref.at[pl.ds(3, 3)])


def near_end(flag, x, own, other, zn, store):
    t = csplit(choose(flag, coupling_of(other), coupling_of(own)))
    z = cdot(nn, t, csplit(x))
    put(zn, z)
    f = choose(flag, end_block(other), end_block(own))
    store(sub(f, cdot(nt, csplit(z), t)))


def near_body(level, info, x, own, other, zn, near):
    near_end(info[3 + level], get(x), own, other, zn, lambda v: pack(near, v))


def rhs_ends(ref):
    return (ref[0], ref[1]), (ref[2], ref[3])


def rest_body(level, info, x, zn, own, other, own_r, other_r, w, zf, out, out_r):
    flag = info[3 + level]
    xs = csplit(get(x))
    zns = csplit(get(zn))
    t_near = csplit(choose(flag, coupling_of(other), coupling_of(own)))
    t_far = csplit(choose(flag, coupling_of(own), coupling_of(other)))
    mine, mine_far = rhs_ends(own_r)
    theirs, theirs_far = rhs_ends(other_r)
    r = add(mine, theirs)
    z = cdot(nn, t_far, xs)
    put(w, vdot(nn, xs, r))
    put(out_r.at[pl.ds(0, 2)], sub(choose(flag, theirs_far, mine_far), vdot(nn, zns, r)))
    put(zf, z)
    z = csplit(z)
    pack(out.at[pl.ds(0, 3)], neg(cdot(nt, z, t_near)))
    f = choose(flag, end_block(own), end_block(other))
    pack(out.at[pl.ds(3, 3)], sub(f, cdot(nt, z, t_far)))
    put(out_r.at[pl.ds(2, 2)], sub(choose(flag, mine_far, theirs_far), vdot(nn, z, r)))


def solve_pair(low, xa, ia, hop, prev, middle, last, out):
    first = choose(low, prev, middle)
    second = choose(low, middle, last)
    t = add(real_vdot(split(hop[...].T), first), real_vdot(split(hop[...]), second))
    at = 1 - low
    x = xa[at, 0], xa[at, 1]
    put(out.at[0], add((ia[at, 0], ia[at, 1]), vdot(nn, csplit(x), t)))
    put(out.at[1], second)


def last_body(level, info, x, own, other, zn, end, ar, ai, m):
    def store(v):
        ar[0, :, 0:N] = v[0]
        ai[0, :, 0:N] = v[1]

    near_end(info[3 + level], get(x), own, other, zn, store)
    sweep(1, ar, ai, m)
    put(end, (-ar[0, :, 0:N], -ai[0, :, 0:N]))


def back_body(count, info, x, zn, end, own_r, other_r, *refs):
    levels = [refs[3 * i : 3 * i + 3] for i in range(count)]
    xa, ia, hop, prev_out, mid, last_out, out = refs[3 * count :]
    flag = info[3 + count]
    mine, mine_far = rhs_ends(own_r)
    theirs, theirs_far = rhs_ends(other_r)
    r = add(mine, theirs)
    zns = csplit(get(zn))
    w = vdot(nn, csplit(get(x)), r)
    rest = sub(choose(flag, theirs_far, mine_far), vdot(nn, zns, r))
    end = vdot(nn, csplit(get(end)), rest)
    one = sub(w, vdot(tn, zns, end))
    near, far = one, choose(flag, (jnp.zeros((N, COLS), jnp.float32),) * 2, end)
    for i in range(count - 1, -1, -1):
        w, z_near, z_far = levels[i]
        one = sub(
            sub(get(w), vdot(tn, csplit(get(z_near)), near)),
            vdot(tn, csplit(get(z_far)), far),
        )
        flag = info[3 + i]
        if i:
            near, far = one, choose(flag, far, near)
    prev = choose(flag, far, near)
    last = choose(flag, near, far)
    put(prev_out, prev)
    put(mid, one)
    put(last_out, last)
    solve_pair(info[0], xa, ia, hop, prev, one, last, out)


def own_body(info, xa, ia, mid, hop, prev, last, out):
    solve_pair(1 - info[0], xa, ia, hop, get(prev), get(mid), get(last), out)


def finish_body(info, mine, other, amplitude, density):
    for which, part in ((info[1], mine), (1 - info[1], other)):
        for slab in range(2):
            re, im = part[slab, 0], part[slab, 1]
            amplitude[slab, 0, which] = re
            amplitude[slab, 1, which] = im
            total = jnp.sum((re * re + im * im).T, axis=0, keepdims=True)
            density[slab, pl.ds(which, 1), :] = total


def per_device(
    source,
    onsite_block,
    hopping_block,
    potential_table,
    slab_profile,
    occupation,
    coupling,
    phonon_shift,
):
    slabs = lax.axis_size("slab")
    energy_count = occupation.shape[1]
    place = lax.axis_index("slab")
    odd = lax.rem(place, 2)
    side = (lax.rem(place, 4) // 2 + odd + 1) % 2

    def pair(array):
        return lax.ppermute(array, "slab", [(s, s ^ 1) for s in range(slabs)])

    def along(array, by):
        width = lax.axis_size("energy")
        pairs = [(e, e + by) for e in range(width) if 0 <= e + by < width]
        return lax.ppermute(array, "energy", pairs)

    def swapped(array, distance, one_way=False):
        spot = lambda g, chain: 2 * g + ((1 - chain) if g % 2 == 0 else chain)
        pairs = [
            (spot(g, chain), spot(g ^ distance, chain))
            for g in range(slabs // 2)
            for chain in range(2)
            if g & distance or not one_way
        ]
        return lax.ppermute(array, "slab", pairs)

    group = place // 2
    count = (slabs // 2 - 1).bit_length()
    bit = lambda k: (group >> k) & 1 if 0 <= k < count else 0
    facing = [(bit(k - 1) == bit(k)) * 1 for k in range(count + 1)]
    point = lax.axis_index("energy") * energy_count + side
    info = jnp.stack([jnp.asarray(v, jnp.int32) for v in (odd, side, point, *facing)])
    mine, yours = call(
        damping_body,
        1,
        [(2, 2, N)] * 2,
        (
            info,
            phonon_shift,
            slab_profile,
            coupling,
            along(occupation, 1),
            occupation,
            along(occupation, -1),
            potential_table,
        ),
        scalars=4,
    )
    theirs = pair(yours)
    kept = lax.dynamic_index_in_dim(source, side, 2, keepdims=False)
    given = pair(lax.dynamic_index_in_dim(source, 1 - side, 2, keepdims=False))

    xa, x, zn, own, other, near = call(
        first_body,
        30,
        [(2,) + MATRIX, MATRIX, MATRIX, ENDS, ENDS, PACKED],
        (info, onsite_block, hopping_block, mine, theirs),
        work(2),
        scalars=1,
    )
    ia, own_r, other_r = call(
        first_rhs_body,
        3,
        [(2,) + VECTOR, RHS, RHS],
        (info, xa, hopping_block, kept, given),
        scalars=1,
    )
    held = []
    for level in range(count):
        distance = 1 << level
        facing_block = swapped(near, distance)
        w, zf, ends, sides = call(
            functools.partial(rest_body, level),
            5,
            [VECTOR, MATRIX, ENDS, RHS],
            (info, x, zn, own, other, own_r, other_r),
            scalars=1,
        )
        held += [w, zn, zf]
        other = swapped(ends, distance, one_way=level == count - 1)
        other_r = swapped(sides, distance)
        own, own_r = ends, sides
        (x,) = call(invert_body, 12, [MATRIX], (near, facing_block), work(1))
        if level < count - 1:
            zn, near = call(
                functools.partial(near_body, level + 1),
                3,
                [MATRIX, PACKED],
                (info, x, own, other),
                scalars=1,
            )
    zn, end = call(
        functools.partial(last_body, count),
        15,
        [MATRIX, MATRIX],
        (info, x, own, other),
        work(1),
        scalars=1,
    )
    prev, mid, last, sent = call(
        functools.partial(back_body, count),
        7,
        [VECTOR, VECTOR, VECTOR, (2,) + VECTOR],
        (info, x, zn, end, own_r, other_r, *held, xa, ia, hopping_block),
        scalars=1,
    )
    back = pair(sent)
    (mine,) = call(
        own_body,
        2,
        [(2,) + VECTOR],
        (info, xa, ia, mid, hopping_block, prev, last),
        scalars=1,
    )
    return call(
        finish_body, 2, [source.shape, occupation.shape], (info, mine, back), scalars=1
    )


def solution(mesh):
    placed = (
        P("slab", None, "energy", None, None),
        P(),
        P(),
        P(),
        P("slab"),
        P("slab", "energy", None),
        P(),
        P(),
    )
    return jax.shard_map(
        per_device,
        mesh=mesh,
        in_specs=placed,
        out_specs=(P("slab", None, "energy", None, None), P("slab", "energy", None)),
        check_vma=False,
    )
```

```python
import functools

import jax
import jax.numpy as jnp
from jax import lax
from jax.experimental import pallas as pl
from jax.experimental.pallas import tpu as pltpu
from jax.sharding import PartitionSpec as P

broadening = 0.05
energy_low = -1.2
energy_step = 0.15
N = 192
COLS = 128
WIDE = 256
BLOCK = 32


def split(x):
    hi = x.astype(jnp.bfloat16)
    lo = (x - hi.astype(jnp.float32)).astype(jnp.bfloat16)
    return hi, lo


def tn(a, b):
    return lax.dot_general(a, b, (((0,), (0,)), ((), ())), preferred_element_type=jnp.float32)


def spread(row):
    return jnp.broadcast_to(row, (8, 128))


def solve_eight(cr, ci, now, side):
    row = lax.broadcasted_iota(jnp.int32, (8, 128), 0)
    for p in range(8):
        dr, di = spread(cr[p][p : p + 1]), spread(ci[p][p : p + 1])
        inv = 1.0 / (dr * dr + di * di)
        er, ei = dr * inv, -di * inv
        here = row == p
        wr = jnp.where(here, 1.0 - er, cr[p] * er - ci[p] * ei)
        wi = jnp.where(here, -ei, cr[p] * ei + ci[p] * er)
        for j in range(p + 1, 8):
            fr, fi = spread(cr[j][p : p + 1]), spread(ci[j][p : p + 1])
            cr[j], ci[j] = cr[j] - (wr * fr - wi * fi), ci[j] - (wr * fi + wi * fr)
        n, t = spread(now[p : p + 1]), spread(side[p : p + 1])
        now, side = now - (wr * n + wi * t), side - (wr * t - wi * n)
    return now, side


def take(x, index):
    return lax.gather(
        x,
        index[:, :, None],
        lax.GatherDimensionNumbers(
            offset_dims=(),
            collapsed_slice_dims=(1,),
            start_index_map=(1,),
            operand_batching_dims=(0,),
            start_indices_batching_dims=(0,),
        ),
        slice_sizes=(1, 1),
        mode=lax.GatherScatterMode.PROMISE_IN_BOUNDS,
    )


def small_inverse(m):
    lane = lax.broadcasted_iota(jnp.int32, (8, 128), 1)
    row = lax.broadcasted_iota(jnp.int32, (8, 128), 0)
    start = (lane // 64) * 64
    real = lane - start < 32
    off = lane - (lane // 32) * 32

    def turned(x):
        return jnp.where(real, -pltpu.roll(x, 96, 1), pltpu.roll(x, 32, 1))

    def group(g, _):
        o = 8 * g
        own = m[0:8, :]
        parts = [m[8 * h : 8 * h + 8, :] for h in range(1, 4)]
        at = [start + (o + j) for j in range(8)]
        far = [a + 32 for a in at]
        cr = [take(own, a) for a in at]
        ci = [take(own, a) for a in far]
        wide_r = [[take(x, a) for a in at] for x in parts]
        wide_i = [[take(x, a) for a in far] for x in parts]
        inside = (off >= o) & (off < o + 8)
        eye = jnp.where(real & (off - o == row), 1.0, 0.0)
        now = jnp.where(inside, eye, own)
        out, turn = solve_eight(cr, ci, now, turned(now))
        for h in range(3):
            x = jnp.where(inside, 0.0, parts[h])
            for j in range(8):
                x = x - (
                    wide_r[h][j] * spread(out[j : j + 1]) + wide_i[h][j] * spread(turn[j : j + 1])
                )
            m[8 * h : 8 * h + 8, :] = x
        m[24:32, :] = out
        return 0

    lax.fori_loop(0, 4, group, 0)


def sweep(B, ar, ai, m):
    b = BLOCK
    for e in range(B):
        ar[e, :, N:] = jnp.zeros((N, WIDE - N), jnp.float32)
        ai[e, :, N:] = jnp.zeros((N, WIDE - N), jnp.float32)
    lane = lax.broadcasted_iota(jnp.int32, (b, WIDE), 1)
    row = lax.broadcasted_iota(jnp.int32, (b, WIDE), 0)
    l128 = lax.broadcasted_iota(jnp.int32, (b, 128), 1)
    r128 = lax.broadcasted_iota(jnp.int32, (b, 128), 0)
    quarter = l128 // 32

    def step(k, _):
        o = pl.multiple_of(k * b, b)
        rows = [(ar[e, pl.ds(o, b), :], ai[e, pl.ds(o, b), :]) for e in range(B)]
        q = jnp.where((lax.rem(quarter, 2) == 0) & (l128 - 32 * quarter == r128), 1.0, 0.0)
        for e in range(B):
            for part in range(2):
                turn = lax.rem(WIDE - o + 64 * e + 32 * part, WIDE)
                q = jnp.where(
                    quarter == 2 * e + part, pltpu.roll(rows[e][part], turn, 1)[:, 0:128], q
                )
        m[...] = q
        small_inverse(m)
        q = m[...]
        for e in range(B):
            rr, ri = rows[e]
            dr = q[:, 64 * e : 64 * e + 32]
            di = q[:, 64 * e + 32 : 64 * e + 64]
            inside = (lane >= o) & (lane < o + b)
            eye = lane - o == row
            r2 = jnp.where(inside, jnp.where(eye, -1.0, 0.0), rr)
            i2 = jnp.where(inside, 0.0, ri)
            drh, drl = split(dr)
            dih, dil = split(di)
            r2h, r2l = split(r2)
            i2h, i2l = split(i2)
            lhs = jnp.concatenate([drh, dih, drl, dil, drh, dih], 0)
            Rr = tn(lhs, jnp.concatenate([r2h, -i2h, r2h, -i2h, r2l, -i2l], 0))
            Ri = tn(lhs, jnp.concatenate([i2h, r2h, i2h, r2h, i2l, r2l], 0))
            Rrh, Rrl = split(Rr)
            Rih, Ril = split(Ri)
            rh, rl = split(rr)
            ih, il = split(ri)
            lhs = jnp.concatenate([rh, ih, rl, il, rh, ih], 0)[:, 0:N]
            Ur = tn(lhs, jnp.concatenate([Rrh, -Rih, Rrh, -Rih, Rrl, -Ril], 0))
            Ui = tn(lhs, jnp.concatenate([Rih, Rrh, Rih, Rrh, Ril, Rrl], 0))
            wide = lax.broadcasted_iota(jnp.int32, (N, WIDE), 1)
            strip = (wide >= o) & (wide < o + b)
            ar[e] = jnp.where(strip, 0.0, ar[e]) - Ur
            ai[e] = jnp.where(strip, 0.0, ai[e]) - Ui
            ar[e, pl.ds(o, b), :] = Rr
            ai[e, pl.ds(o, b), :] = Ri
        return 0

    lax.fori_loop(0, N // b, step, 0)


def nn(a, b):
    return jnp.dot(a, b, preferred_element_type=jnp.float32)


def nt(a, b):
    return lax.dot_general(a, b, (((1,), (1,)), ((), ())), preferred_element_type=jnp.float32)


def three(dot, a, b):
    return dot(a[0], b[0]) + (dot(a[0], b[1]) + dot(a[1], b[0]))


def csplit(x):
    return split(x[0]), split(x[1])


def cdot(dot, a, b):
    re = three(dot, a[0], b[0]) - three(dot, a[1], b[1])
    im = three(dot, a[0], b[1]) + three(dot, a[1], b[0])
    return re, im


def real_left(dot, a, b):
    return three(dot, a, b[0]), three(dot, a, b[1])


def real_right(dot, a, b):
    return three(dot, a[0], b), three(dot, a[1], b)


def put(ref, x):
    ref[0] = x[0]
    ref[1] = x[1]


def get(ref):
    return ref[0], ref[1]


def neg(x):
    return -x[0], -x[1]


def add(x, y):
    return x[0] + y[0], x[1] + y[1]


def sub(x, y):
    return x[0] - y[0], x[1] - y[1]


def pack(ref, base, x):
    ref[base : base + 192, :] = x[0][:, 0:128]
    ref[base + 192 : base + 384, :] = x[1][:, 0:128]
    ref[base + 384 : base + 576, :] = jnp.concatenate([x[0][:, 128:N], x[1][:, 128:N]], axis=1)


def unpack(ref, base):
    rest = ref[base + 384 : base + 576, :]
    return (
        jnp.concatenate([ref[base : base + 192, :], rest[:, 0:64]], axis=1),
        jnp.concatenate([ref[base + 192 : base + 384, :], rest[:, 64:128]], axis=1),
    )


def pack_symmetric(ref, base, x):
    ref[base : base + 192, :] = x[0][:, 0:128]
    ref[base + 192 : base + 384, :] = x[1][:, 0:128]
    ref[base + 384 : base + 448, :] = jnp.concatenate(
        [x[0][128:N, 128:N], x[1][128:N, 128:N]], axis=1
    )


def unpack_symmetric(ref, base):
    corner = ref[base + 384 : base + 448, :]
    out = []
    for part in range(2):
        left = ref[base + 192 * part : base + 192 * part + 192, :]
        right = jnp.concatenate(
            [left[128:N].T, corner[:, 64 * part : 64 * part + 64]], axis=0
        )
        out.append(jnp.concatenate([left, right], axis=1))
    return tuple(out)


def call(body, cost, outs, args, scratch=(), scalars=0):
    return pl.pallas_call(
        body,
        out_shape=tuple(jax.ShapeDtypeStruct(s, jnp.float32) for s in outs),
        in_specs=[pl.BlockSpec(memory_space=pltpu.SMEM)] * scalars
        + [pl.BlockSpec(memory_space=pltpu.VMEM)] * (len(args) - scalars),
        out_specs=tuple(pl.BlockSpec(memory_space=pltpu.VMEM) for _ in outs),
        scratch_shapes=list(scratch),
        compiler_params=pltpu.CompilerParams(vmem_limit_bytes=24 * 1024 * 1024),
        cost_estimate=pl.CostEstimate(
            flops=int(cost * 1.1e9), bytes_accessed=1 << 20, transcendentals=0
        ),
    )(*args)


MATRIX = (2, N, N)
PACKED = (448, 128)
VECTOR = (2, N, COLS)
ENDS = (1024, 128)
RHS = (4, N, COLS)


def work(B):
    return [pltpu.VMEM((B, N, WIDE), jnp.float32)] * 2 + [pltpu.VMEM((BLOCK, 128), jnp.float32)]


def vdot(dot, a, v):
    high, low = split(jnp.concatenate(v, axis=1))
    turn = lambda s: jnp.concatenate([-s[:, COLS:], s[:, :COLS]], axis=1)
    both = three(dot, a[0], (high, low)) + three(dot, a[1], (turn(high), turn(low)))
    return both[:, :COLS], both[:, COLS:]


def real_vdot(a, v):
    both = three(nn, a, split(jnp.concatenate(v, axis=1)))
    return both[:, :COLS], both[:, COLS:]


def choose(flag, yes, no):
    pick = jnp.full(yes[0].shape, flag, jnp.int32) == 1
    return tuple(jnp.where(pick, y, n) for y, n in zip(yes, no))


def damping_body(info, shift, profile, coupling, low, occ, high, table, mine, yours):
    for out, k in ((mine, info[1]), (yours, 1 - info[1])):
        for slab in range(2):
            total = jnp.full((1, N), broadening, jnp.float32)
            for q in range(6):
                w = jnp.float32(0.0)
                for mode in range(shift.shape[0]):
                    c = coupling[mode]
                    w = w + jnp.where(q == k + 2 + shift[mode], c, 0.0)
                    w = w + jnp.where(q == k + 2 - shift[mode], c, 0.0)
                row = (low, occ, high)[q // 2][slab, q % 2 : q % 2 + 1, :]
                total = total + w * row
            out[slab, 0:1, :] = total
            out[slab, 1:2, :] = table[pl.ds(profile[slab], 1), :]


def first_body(info, onsite, hop, mine, theirs, xa, x, zn, left, right, near, ar, ai, m):
    row = lax.broadcasted_iota(jnp.int32, (N, N), 0)
    col = lax.broadcasted_iota(jnp.int32, (N, N), 1)
    eye = row == col
    energy = energy_low + energy_step * info[2].astype(jnp.float32)

    def block(i):
        flag = info[0] if i // 2 else 1 - info[0]
        at = i % 2
        (both,) = choose(flag, (mine[at],), (theirs[at],))
        return (
            jnp.where(eye, energy - both[1:2], 0.0) - onsite[...],
            jnp.where(eye, both[0:1], 0.0),
        )

    for e in range(2):
        re, im = block(2 * e)
        ar[e, :, 0:N] = re
        ai[e, :, 0:N] = im
    sweep(2, ar, ai, m)
    h = split(hop[...])
    ht = split(hop[...].T)
    got = []
    for e in range(2):
        one = (-ar[e, :, 0:N], -ai[e, :, 0:N])
        put(xa.at[e], one)
        xs = csplit(one)
        up = csplit(real_left(nn, h, xs))
        down = csplit(real_left(nn, ht, xs))
        got.append((up, down))
    (up0, down0), (up2, down2) = got
    middle = sub(sub(block(1), real_right(nn, down0, h)), real_right(nn, up2, ht))
    pack(left, 0, neg(real_right(nn, up0, h)))
    pack_symmetric(left, 576, neg(real_right(nn, up0, ht)))
    pack(right, 0, neg(real_right(nn, down2, ht)))
    pack_symmetric(right, 576, sub(block(3), real_right(nn, down2, h)))
    ar[0, :, 0:N] = middle[0]
    ai[0, :, 0:N] = middle[1]
    sweep(1, ar, ai, m)
    put(x, (-ar[0, :, 0:N], -ai[0, :, 0:N]))
    near_end(info[3], get(x), left, right, zn, lambda v: pack_symmetric(near, 0, v))


def first_rhs_body(info, xa, hop, kept, other, ia, left, right):
    h = split(hop[...])
    ht = split(hop[...].T)

    def r(i):
        flag = info[0] if i // 2 else 1 - info[0]
        at = i % 2
        return choose(flag, (kept[at, 0], kept[at, 1]), (other[at, 0], other[at, 1]))

    a = vdot(nn, csplit(get(xa.at[0])), r(0))
    c = vdot(nn, csplit(get(xa.at[1])), r(2))
    put(ia.at[0], a)
    put(ia.at[1], c)
    put(left.at[pl.ds(0, 2)], add(r(1), add(real_vdot(ht, a), real_vdot(h, c))))
    put(left.at[pl.ds(2, 2)], real_vdot(h, a))
    right[0] = jnp.zeros((N, COLS), jnp.float32)
    right[1] = jnp.zeros((N, COLS), jnp.float32)
    put(right.at[pl.ds(2, 2)], add(r(3), real_vdot(ht, c)))


def invert_body(own, other, x, ar, ai, m):
    now = add(unpack_symmetric(own, 0), unpack_symmetric(other, 0))
    ar[0, :, 0:N] = now[0]
    ai[0, :, 0:N] = now[1]
    sweep(1, ar, ai, m)
    put(x, (-ar[0, :, 0:N], -ai[0, :, 0:N]))


def coupling_of(ref):
    return unpack(ref, 0)


def end_block(ref):
    return unpack_symmetric(ref, 576)


def near_end(flag, x, own, other, zn, store):
    t = csplit(choose(flag, coupling_of(other), coupling_of(own)))
    z = cdot(nn, t, csplit(x))
    put(zn, z)
    f = choose(flag, end_block(other), end_block(own))
    store(sub(f, cdot(nt, csplit(z), t)))


def near_body(level, info, x, own, other, zn, near):
    near_end(info[3 + level], get(x), own, other, zn, lambda v: pack_symmetric(near, 0, v))


def rhs_ends(ref):
    return (ref[0], ref[1]), (ref[2], ref[3])


def rest_body(level, info, x, zn, own, other, own_r, other_r, w, zf, out, out_r):
    flag = info[3 + level]
    xs = csplit(get(x))
    zns = csplit(get(zn))
    t_near = csplit(choose(flag, coupling_of(other), coupling_of(own)))
    t_far = csplit(choose(flag, coupling_of(own), coupling_of(other)))
    mine, mine_far = rhs_ends(own_r)
    theirs, theirs_far = rhs_ends(other_r)
    r = add(mine, theirs)
    z = cdot(nn, t_far, xs)
    put(w, vdot(nn, xs, r))
    put(out_r.at[pl.ds(0, 2)], sub(choose(flag, theirs_far, mine_far), vdot(nn, zns, r)))
    put(zf, z)
    z = csplit(z)
    pack(out, 0, neg(cdot(nt, z, t_near)))
    f = choose(flag, end_block(own), end_block(other))
    pack_symmetric(out, 576, sub(f, cdot(nt, z, t_far)))
    put(out_r.at[pl.ds(2, 2)], sub(choose(flag, mine_far, theirs_far), vdot(nn, z, r)))


def solve_pair(low, xa, ia, hop, prev, middle, last, out):
    first = choose(low, prev, middle)
    second = choose(low, middle, last)
    t = add(real_vdot(split(hop[...].T), first), real_vdot(split(hop[...]), second))
    at = 1 - low
    x = xa[at, 0], xa[at, 1]
    put(out.at[0], add((ia[at, 0], ia[at, 1]), vdot(nn, csplit(x), t)))
    put(out.at[1], second)


def last_body(level, info, x, own, other, zn, end, ar, ai, m):
    def store(v):
        ar[0, :, 0:N] = v[0]
        ai[0, :, 0:N] = v[1]

    near_end(info[3 + level], get(x), own, other, zn, store)
    sweep(1, ar, ai, m)
    put(end, (-ar[0, :, 0:N], -ai[0, :, 0:N]))


def back_body(count, info, x, zn, end, own_r, other_r, *refs):
    levels = [refs[3 * i : 3 * i + 3] for i in range(count)]
    xa, ia, hop, prev_out, mid, last_out, out = refs[3 * count :]
    flag = info[3 + count]
    mine, mine_far = rhs_ends(own_r)
    theirs, theirs_far = rhs_ends(other_r)
    r = add(mine, theirs)
    zns = csplit(get(zn))
    w = vdot(nn, csplit(get(x)), r)
    rest = sub(choose(flag, theirs_far, mine_far), vdot(nn, zns, r))
    end = vdot(nn, csplit(get(end)), rest)
    one = sub(w, vdot(tn, zns, end))
    near, far = one, choose(flag, (jnp.zeros((N, COLS), jnp.float32),) * 2, end)
    for i in range(count - 1, -1, -1):
        w, z_near, z_far = levels[i]
        one = sub(
            sub(get(w), vdot(tn, csplit(get(z_near)), near)),
            vdot(tn, csplit(get(z_far)), far),
        )
        flag = info[3 + i]
        if i:
            near, far = one, choose(flag, far, near)
    prev = choose(flag, far, near)
    last = choose(flag, near, far)
    put(prev_out, prev)
    put(mid, one)
    put(last_out, last)
    solve_pair(info[0], xa, ia, hop, prev, one, last, out)


def own_body(info, xa, ia, mid, hop, prev, last, out):
    solve_pair(1 - info[0], xa, ia, hop, get(prev), get(mid), get(last), out)


def finish_body(info, mine, other, amplitude, density):
    for which, part in ((info[1], mine), (1 - info[1], other)):
        for slab in range(2):
            re, im = part[slab, 0], part[slab, 1]
            amplitude[slab, 0, which] = re
            amplitude[slab, 1, which] = im
            total = jnp.sum((re * re + im * im).T, axis=0, keepdims=True)
            density[slab, pl.ds(which, 1), :] = total


def per_device(
    source,
    onsite_block,
    hopping_block,
    potential_table,
    slab_profile,
    occupation,
    coupling,
    phonon_shift,
):
    slabs = lax.axis_size("slab")
    energy_count = occupation.shape[1]
    place = lax.axis_index("slab")
    odd = lax.rem(place, 2)
    side = (lax.rem(place, 4) // 2 + odd + 1) % 2

    def pair(array):
        return lax.ppermute(array, "slab", [(s, s ^ 1) for s in range(slabs)])

    def along(array, by):
        width = lax.axis_size("energy")
        pairs = [(e, e + by) for e in range(width) if 0 <= e + by < width]
        return lax.ppermute(array, "energy", pairs)

    def swapped(array, distance, one_way=False):
        spot = lambda g, chain: 2 * g + ((1 - chain) if g % 2 == 0 else chain)
        pairs = [
            (spot(g, chain), spot(g ^ distance, chain))
            for g in range(slabs // 2)
            for chain in range(2)
            if g & distance or not one_way
        ]
        return lax.ppermute(array, "slab", pairs)

    group = place // 2
    count = (slabs // 2 - 1).bit_length()
    bit = lambda k: (group >> k) & 1 if 0 <= k < count else 0
    facing = [(bit(k - 1) == bit(k)) * 1 for k in range(count + 1)]
    point = lax.axis_index("energy") * energy_count + side
    info = jnp.stack([jnp.asarray(v, jnp.int32) for v in (odd, side, point, *facing)])
    mine, yours = call(
        damping_body,
        1,
        [(2, 2, N)] * 2,
        (
            info,
            phonon_shift,
            slab_profile,
            coupling,
            along(occupation, 1),
            occupation,
            along(occupation, -1),
            potential_table,
        ),
        scalars=4,
    )
    theirs = pair(yours)
    kept = lax.dynamic_index_in_dim(source, side, 2, keepdims=False)
    given = pair(lax.dynamic_index_in_dim(source, 1 - side, 2, keepdims=False))

    xa, x, zn, own, other, near = call(
        first_body,
        30,
        [(2,) + MATRIX, MATRIX, MATRIX, ENDS, ENDS, PACKED],
        (info, onsite_block, hopping_block, mine, theirs),
        work(2),
        scalars=1,
    )
    ia, own_r, other_r = call(
        first_rhs_body,
        3,
        [(2,) + VECTOR, RHS, RHS],
        (info, xa, hopping_block, kept, given),
        scalars=1,
    )
    held = []
    for level in range(count):
        distance = 1 << level
        facing_block = swapped(near, distance)
        w, zf, ends, sides = call(
            functools.partial(rest_body, level),
            5,
            [VECTOR, MATRIX, ENDS, RHS],
            (info, x, zn, own, other, own_r, other_r),
            scalars=1,
        )
        held += [w, zn, zf]
        other = swapped(ends, distance, one_way=level == count - 1)
        other_r = swapped(sides, distance)
        own, own_r = ends, sides
        (x,) = call(invert_body, 12, [MATRIX], (near, facing_block), work(1))
        if level < count - 1:
            zn, near = call(
                functools.partial(near_body, level + 1),
                3,
                [MATRIX, PACKED],
                (info, x, own, other),
                scalars=1,
            )
    zn, end = call(
        functools.partial(last_body, count),
        15,
        [MATRIX, MATRIX],
        (info, x, own, other),
        work(1),
        scalars=1,
    )
    prev, mid, last, sent = call(
        functools.partial(back_body, count),
        7,
        [VECTOR, VECTOR, VECTOR, (2,) + VECTOR],
        (info, x, zn, end, own_r, other_r, *held, xa, ia, hopping_block),
        scalars=1,
    )
    back = pair(sent)
    (mine,) = call(
        own_body,
        2,
        [(2,) + VECTOR],
        (info, xa, ia, mid, hopping_block, prev, last),
        scalars=1,
    )
    return call(
        finish_body, 2, [source.shape, occupation.shape], (info, mine, back), scalars=1
    )


def solution(mesh):
    placed = (
        P("slab", None, "energy", None, None),
        P(),
        P(),
        P(),
        P("slab"),
        P("slab", "energy", None),
        P(),
        P(),
    )
    return jax.shard_map(
        per_device,
        mesh=mesh,
        in_specs=placed,
        out_specs=(P("slab", None, "energy", None, None), P("slab", "energy", None)),
        check_vma=False,
    )
```
